32 devices in a mesh: grp: 2 (over y), bl: 4 (over z), ch: 4 (over x, core).
Axes of the slice: x: 2, y: 2, z: 4, core: 2. Of those that a mesh axis runs over, the one named last changes fastest.
Arguments:
- visibilities: bfloat16 [8, 128, 4096], P(None, 'ch', ('grp', 'bl')), parts along dimension 2, may hold values from -40 to 40
- sky_model: bfloat16 [8, 128, 4096], P(None, 'ch', ('grp', 'bl')), parts along dimension 2, may hold values from -4 to 4
- antenna_pairs: int32 [2, 4096], P(None, ('grp', 'bl')), parts along dimension 1, may hold values from 0 to 511, as said below
- tile_counts: int32 [8], P(('grp', 'bl')), parts along dimension 0, may hold values from 128 to 512, as said below
- usable_mask: int32 [128, 4096], P('ch', ('grp', 'bl')), parts along dimension 1, may hold values 0 or 1
Outputs:
- solved_gains: float32 [2, 2, 128, 1024], P(None, None, 'ch', ('grp', 'bl')), parts along dimension 3
- fitted_gains: float32 [2, 2, 128, 1024], P(None, None, 'ch', ('grp', 'bl')), parts along dimension 3
The draws below stay inside these ranges and needn't reach their ends.
There are 2 independent parts, one for each index of `grp`. The reference program is written for one: setup_inputs(seed, part) draws one part's arguments, and reference() takes and returns one part's arrays. A program takes and returns all parts, laid end to end along the dimension named above; each array names one. Nothing has to cross between parts.
Inputs may be any that keep to these rules, and one draw needn't show every extreme that they name: `antenna_pairs`: the two stations of every slot differ. Tile t's baselines are its first tile_counts[t] slots; the later slots of a tile are not used. Some tile is full in every draw.
All inputs are finite; a program needn't handle non-finite values. No bound on the sum of `usable_mask` on one device may be relied on, other than what follows from the above.
Results may differ from the reference program's by a relative error of at most 0.0003.
Values may be sent and summed in bfloat16 or wider, within the bound.
No kernel may reach another device: no remote copies, remote signals or barrier semaphores. Data moves between devices by JAX's collectives and lax.ppermute only.
A program may use at most 64 MiB of HBM per device.

```python
import jax
import jax.numpy as jnp
from jax import lax

STATION_COUNT = 512
BL_DEV = 512
SWEEPS = 2
PASSES = 1
FREQ_CHANNELS = 128
BASELINE_SLOTS = 2048
TILES = 4


def complex_product(left_real, left_imag, right_real, right_imag):
    return (left_real * right_real - left_imag * right_imag, left_real * right_imag + left_imag * right_real)


def station_pairs(key):
    first_endpoints = jax.random.randint(jax.random.fold_in(key, 11), (BASELINE_SLOTS,), 0, STATION_COUNT)
    slot_offsets = jax.random.randint(jax.random.fold_in(key, 12), (BASELINE_SLOTS,), 1, STATION_COUNT)
    second_ends = (first_endpoints + slot_offsets) % STATION_COUNT
    return jnp.stack([first_endpoints, second_ends]).astype(jnp.int32)


def sky_parts(key):
    pair_table = station_pairs(key)
    handedness_scale = jnp.array([1.0, 0.3, 0.3, 1.0], jnp.float32)[:, None, None]
    model_real_part = 0.7 * jnp.clip(jax.random.normal(jax.random.fold_in(key, 21), (4, FREQ_CHANNELS, BASELINE_SLOTS), jnp.float32), -5.0, 5.0) * handedness_scale
    model_imaginary = 0.7 * jnp.clip(jax.random.normal(jax.random.fold_in(key, 22), (4, FREQ_CHANNELS, BASELINE_SLOTS), jnp.float32), -5.0, 5.0) * handedness_scale
    station_amp = jnp.exp(jax.random.uniform(jax.random.fold_in(key, 31), (2, 1, STATION_COUNT), jnp.float32, jnp.log(0.7), jnp.log(1.4)))
    rough = jnp.clip(jax.random.normal(jax.random.fold_in(key, 32), (2, FREQ_CHANNELS, STATION_COUNT), jnp.float32), -3.0, 3.0)
    amplitude = station_amp * (1.0 + 0.1 * rough)
    node_values = jnp.linspace(-1.0, 1.0, FREQ_CHANNELS, dtype=jnp.float32)[None, :, None]
    phase_angle = jax.random.uniform(jax.random.fold_in(key, 33), (2, 1, STATION_COUNT), jnp.float32, -jnp.pi, jnp.pi) + jax.random.uniform(jax.random.fold_in(key, 34), (2, 1, STATION_COUNT), jnp.float32, -2.0, 2.0) * node_values + 0.3 * jax.random.normal(jax.random.fold_in(key, 35), (2, FREQ_CHANNELS, STATION_COUNT), jnp.float32)
    gain_real = amplitude * jnp.cos(phase_angle)
    gain_imag = amplitude * jnp.sin(phase_angle)
    first_real = gain_real[:, :, pair_table[0]][:, None]
    first_imag = gain_imag[:, :, pair_table[0]][:, None]
    second_real = gain_real[:, :, pair_table[1]][None]
    second_imag = gain_imag[:, :, pair_table[1]][None]
    block_real_part = model_real_part.reshape(2, 2, FREQ_CHANNELS, BASELINE_SLOTS)
    block_imaginary = model_imaginary.reshape(2, 2, FREQ_CHANNELS, BASELINE_SLOTS)
    inner_real, inner_imag = complex_product(first_real, first_imag, block_real_part, block_imaginary)
    outer_real_part, outer_imaginary = complex_product(inner_real, inner_imag, second_real, -second_imag)
    noise_real_part = 0.3 * jnp.clip(jax.random.normal(jax.random.fold_in(key, 41), (4, FREQ_CHANNELS, BASELINE_SLOTS), jnp.float32), -4.0, 4.0)
    noise_imaginary = 0.3 * jnp.clip(jax.random.normal(jax.random.fold_in(key, 42), (4, FREQ_CHANNELS, BASELINE_SLOTS), jnp.float32), -4.0, 4.0)
    visibility_planes = jnp.concatenate([outer_real_part.reshape(4, FREQ_CHANNELS, BASELINE_SLOTS) + noise_real_part, outer_imaginary.reshape(4, FREQ_CHANNELS, BASELINE_SLOTS) + noise_imaginary])
    model_planes = jnp.concatenate([model_real_part, model_imaginary])
    return (visibility_planes, model_planes)


def draw_visibilities(key, part):
    return sky_parts(key)[0].astype(jnp.bfloat16)


def draw_sky_model(key, part):
    return sky_parts(key)[1].astype(jnp.bfloat16)


def draw_antenna_pairs(key, part):
    return station_pairs(key)


def draw_tile_counts(key, part):
    counts_drawn = jax.random.randint(jax.random.fold_in(key, 51), (TILES,), BL_DEV // 4, BL_DEV + 1)
    full_tile = jax.random.randint(jax.random.fold_in(key, 52), (), 0, TILES)
    return counts_drawn.at[full_tile].set(BL_DEV).astype(jnp.int32)


def set_ends(result, stream_key, low, top_value):
    longest = result.shape.index(max(result.shape))
    spots = []
    for shift in (0, 1):
        where = [jax.random.randint(jax.random.fold_in(stream_key, axis), (), 0, length) for axis, length in enumerate(result.shape)]
        where[longest] = (where[longest] + shift) % result.shape[longest]
        spots.append(tuple(where))
    return result.at[spots[0]].set(low).at[spots[1]].set(top_value)


def setup_inputs(seed: int = 0, part: int = 0) -> dict:
    splits = jax.random.split(jax.random.key(seed), 6)
    part_keys = jax.random.split(jax.random.fold_in(splits[5], part), 6)
    visibilities = draw_visibilities(jax.random.fold_in(jax.random.fold_in(splits[5], part), 71), part)
    sky_model = draw_sky_model(jax.random.fold_in(jax.random.fold_in(splits[5], part), 71), part)
    antenna_pairs = draw_antenna_pairs(jax.random.fold_in(jax.random.fold_in(splits[5], part), 71), part)
    tile_counts = draw_tile_counts(jax.random.fold_in(jax.random.fold_in(splits[5], part), 71), part)
    usable_mask = set_ends((jax.random.randint(part_keys[4], (FREQ_CHANNELS, BASELINE_SLOTS), 0, 10) < 9).astype(jnp.int32), jax.random.fold_in(part_keys[4], 1), 0, 1)
    return {"visibilities": visibilities, "sky_model": sky_model, "antenna_pairs": antenna_pairs, "tile_counts": tile_counts, "usable_mask": usable_mask}


damping = 4.0
highest = lax.Precision.HIGHEST

def split_parts(data):
    planes = data.astype(jnp.float32)
    shape_rest = planes.shape[1:]
    return (planes[:4].reshape((2, 2) + shape_rest), planes[4:].reshape((2, 2) + shape_rest))

def poly_basis(channel_total):
    node_values = (2.0 * jnp.arange(channel_total, dtype=jnp.float32) - (channel_total - 1)) / (channel_total - 1)
    basis_rows = []
    for degree in range(4):
        vector = node_values ** degree
        for earlier in basis_rows:
            vector = vector - jnp.sum(vector * earlier) * earlier
        vector = vector / jnp.sqrt(jnp.sum(vector * vector))
        basis_rows.append(vector)
    return jnp.stack(basis_rows)

def contributions(model_real_part, model_imaginary, vis_real, vis_imag, first_gain, second_gain, weights):
    second_real = second_gain[0][None]
    second_imag = second_gain[1][None]
    left_real = model_real_part * second_real + model_imaginary * second_imag
    left_imag = model_imaginary * second_real - model_real_part * second_imag
    first_num_real = lax.optimization_barrier(jnp.sum(left_real * vis_real + left_imag * vis_imag, axis=1)) * weights
    first_num_imag = lax.optimization_barrier(jnp.sum(left_real * vis_imag - left_imag * vis_real, axis=1)) * weights
    first_den = lax.optimization_barrier(jnp.sum(left_real * left_real + left_imag * left_imag, axis=1)) * weights
    first_real = first_gain[0][:, None]
    first_imag = first_gain[1][:, None]
    right_real = model_real_part * first_real - model_imaginary * first_imag
    right_imag = model_real_part * first_imag + model_imaginary * first_real
    second_num_real = lax.optimization_barrier(jnp.sum(right_real * vis_real + right_imag * vis_imag, axis=0)) * weights
    second_num_imag = lax.optimization_barrier(jnp.sum(right_imag * vis_real - right_real * vis_imag, axis=0)) * weights
    second_den = lax.optimization_barrier(jnp.sum(right_real * right_real + right_imag * right_imag, axis=0)) * weights
    return (jnp.stack([first_num_real, first_num_imag, first_den]), jnp.stack([second_num_real, second_num_imag, second_den]))

def collect(terms, station_ends):
    channel_local = terms.shape[2]
    flat_terms = terms.reshape(-1, terms.shape[3]).T
    summed = jax.ops.segment_sum(flat_terms, station_ends, num_segments=STATION_COUNT)
    return summed.T.reshape(3, 2, channel_local, STATION_COUNT)

def refresh(station_sums, previous):
    divisor = station_sums[2] + damping
    return jnp.stack([(station_sums[0] + damping * previous[0]) / divisor, (station_sums[1] + damping * previous[1]) / divisor])

def reference(visibilities, sky_model, antenna_pairs, tile_counts, usable_mask):
    first_endpoints = antenna_pairs[0]
    second_ends = antenna_pairs[1]
    station_positions = jnp.arange(BASELINE_SLOTS, dtype=jnp.int32)
    live_slots = station_positions % BL_DEV < tile_counts[station_positions // BL_DEV]
    weights = usable_mask.astype(jnp.float32) * live_slots.astype(jnp.float32)[None, :]
    block_width = 8
    block_total = FREQ_CHANNELS // block_width
    vis_blocks = visibilities.reshape(8, block_total, block_width, BASELINE_SLOTS).transpose(1, 0, 2, 3)
    model_blocks = sky_model.reshape(8, block_total, block_width, BASELINE_SLOTS).transpose(1, 0, 2, 3)
    weight_blocks = weights.reshape(block_total, block_width, BASELINE_SLOTS)

    def block_sums(items):
        vis_block, model_block, weight_block, gain_block = items
        vis_real, vis_imag = split_parts(vis_block)
        model_real_part, model_imaginary = split_parts(model_block)
        first_gain = gain_block[:, :, :, first_endpoints]
        second_gain = gain_block[:, :, :, second_ends]
        end_first, end_second = contributions(model_real_part, model_imaginary, vis_real, vis_imag, first_gain, second_gain, weight_block)
        return collect(end_first, first_endpoints) + collect(end_second, second_ends)
    gain_state = jnp.stack([jnp.ones((2, FREQ_CHANNELS, STATION_COUNT), jnp.float32), jnp.zeros((2, FREQ_CHANNELS, STATION_COUNT), jnp.float32)])
    poly_rows = poly_basis(FREQ_CHANNELS)
    solved = gain_state
    for pass_index in range(PASSES):
        for iteration in range(SWEEPS):
            gain_blocks = gain_state.reshape(2, 2, block_total, block_width, STATION_COUNT).transpose(2, 0, 1, 3, 4)
            summed_blocks = lax.map(block_sums, (vis_blocks, model_blocks, weight_blocks, gain_blocks))
            station_sums = summed_blocks.transpose(1, 2, 0, 3, 4).reshape(3, 2, FREQ_CHANNELS, STATION_COUNT)
            renewed = refresh(station_sums, gain_state)
            if iteration == 1:
                renewed = 0.5 * (renewed + gain_state)
            gain_state = renewed
        solved = gain_state
        moments = jnp.einsum('kc,rfca->krfa', poly_rows, solved, precision=highest)
        gain_state = jnp.einsum('kc,krfa->rfca', poly_rows, moments, precision=highest)
    return (solved, gain_state)
```

```python
import functools
import math

import jax
import jax.numpy as jnp
import numpy as np
from jax import lax
from jax.experimental import pallas as pl
from jax.experimental.pallas import tpu as pltpu
from jax.sharding import PartitionSpec as P

STATION_COUNT = 512
SWEEPS = 2

damping = 4.0
highest = lax.Precision.HIGHEST


def poly_basis(channel_total):
    nodes = (2.0 * np.arange(channel_total, dtype=np.float64) - (channel_total - 1)) / (
        channel_total - 1
    )
    rows = []
    for degree in range(4):
        vector = nodes**degree
        for earlier in rows:
            vector = vector - np.sum(vector * earlier) * earlier
        rows.append(vector / np.sqrt(np.sum(vector * vector)))
    return np.stack(rows).astype(np.float32)


def split_parts(data):
    planes = data.astype(jnp.float32)
    shape_rest = planes.shape[1:]
    return (planes[:4].reshape((2, 2) + shape_rest), planes[4:].reshape((2, 2) + shape_rest))


def contributions(
    model_real_part, model_imaginary, vis_real, vis_imag, first_gain, second_gain, weights
):
    second_real = second_gain[0][None]
    second_imag = second_gain[1][None]
    left_real = model_real_part * second_real + model_imaginary * second_imag
    left_imag = model_imaginary * second_real - model_real_part * second_imag
    first_num_real = jnp.sum(left_real * vis_real + left_imag * vis_imag, axis=1) * weights
    first_num_imag = jnp.sum(left_real * vis_imag - left_imag * vis_real, axis=1) * weights
    first_den = jnp.sum(left_real * left_real + left_imag * left_imag, axis=1) * weights
    first_real = first_gain[0][:, None]
    first_imag = first_gain[1][:, None]
    right_real = model_real_part * first_real - model_imaginary * first_imag
    right_imag = model_real_part * first_imag + model_imaginary * first_real
    second_num_real = jnp.sum(right_real * vis_real + right_imag * vis_imag, axis=0) * weights
    second_num_imag = jnp.sum(right_imag * vis_real - right_real * vis_imag, axis=0) * weights
    second_den = jnp.sum(right_real * right_real + right_imag * right_imag, axis=0) * weights
    return (
        jnp.stack([first_num_real, first_num_imag, first_den]),
        jnp.stack([second_num_real, second_num_imag, second_den]),
    )


def refresh(station_sums, previous):
    divisor = station_sums[2] + damping
    return jnp.stack(
        [
            (station_sums[0] + damping * previous[0]) / divisor,
            (station_sums[1] + damping * previous[1]) / divisor,
        ]
    )


def station_totals(end_first, end_second, first_endpoints, second_ends):
    total_slots = end_first.shape[3]
    flat_first = end_first.reshape(-1, total_slots)
    flat_second = end_second.reshape(-1, total_slots)
    station_index = jnp.arange(STATION_COUNT, dtype=jnp.int32)
    table_first = (first_endpoints[:, None] == station_index[None, :]).astype(jnp.float32)
    table_second = (second_ends[:, None] == station_index[None, :]).astype(jnp.float32)
    summed = jnp.dot(
        flat_first, table_first, precision=highest, preferred_element_type=jnp.float32
    ) + jnp.dot(flat_second, table_second, precision=highest, preferred_element_type=jnp.float32)
    return summed.reshape(end_first.shape[:3] + (STATION_COUNT,))


def local_general(visibilities, sky_model, antenna_pairs, tile_counts, usable_mask):
    vis_real, vis_imag = split_parts(visibilities)
    model_real_part, model_imaginary = split_parts(sky_model)
    channel_local = visibilities.shape[1]
    tile_rows = visibilities.shape[2]
    owned_count = STATION_COUNT // lax.axis_size("bl")
    owner_start = lax.axis_index("bl") * owned_count
    live_slots = jnp.arange(tile_rows, dtype=jnp.int32) < tile_counts[0]
    weights = usable_mask.astype(jnp.float32) * live_slots.astype(jnp.float32)[None, :]
    channel_total = channel_local * lax.axis_size("ch")
    poly_rows = lax.dynamic_slice_in_dim(
        jnp.asarray(poly_basis(channel_total)),
        lax.axis_index("ch") * channel_local,
        channel_local,
        1,
    )
    gain_state = jnp.stack(
        [
            jnp.ones((2, channel_local, STATION_COUNT), jnp.float32),
            jnp.zeros((2, channel_local, STATION_COUNT), jnp.float32),
        ]
    )
    solved = gain_state
    for iteration in range(SWEEPS):
        first_gain = jnp.take(gain_state, antenna_pairs[0], axis=3)
        second_gain = jnp.take(gain_state, antenna_pairs[1], axis=3)
        end_first, end_second = contributions(
            model_real_part, model_imaginary, vis_real, vis_imag, first_gain, second_gain, weights
        )
        partial_sums = station_totals(end_first, end_second, antenna_pairs[0], antenna_pairs[1])
        station_sums = lax.psum_scatter(partial_sums, "bl", scatter_dimension=3, tiled=True)
        previous = lax.dynamic_slice_in_dim(gain_state, owner_start, owned_count, 3)
        renewed = refresh(station_sums, previous)
        if iteration == 1:
            renewed = 0.5 * (renewed + previous)
        solved = renewed
        if iteration < SWEEPS - 1:
            gain_state = lax.all_gather(renewed, "bl", axis=3, tiled=True)
    local_moments = jnp.einsum("kc,rfca->krfa", poly_rows, solved, precision=highest)
    moments = lax.psum(local_moments, "ch")
    fitted = jnp.einsum("kc,krfa->rfca", poly_rows, moments, precision=highest)
    return (solved, fitted)


def split_dot(values, table, dims):
    rows = values.shape[0]
    high = values.astype(jnp.bfloat16)
    low = (values - high.astype(jnp.float32)).astype(jnp.bfloat16)
    both = lax.dot_general(
        jnp.concatenate([high, low], axis=0),
        table,
        (dims, ((), ())),
        preferred_element_type=jnp.float32,
    )
    return both[:rows] + both[rows:]


def scatter(first, second, table):
    return split_dot(jnp.concatenate([first, second], axis=1), table, ((1,), (1,)))


def tile_terms(chunk_ref, pairs_ref, products_ref, table_ref):
    slots = chunk_ref.shape[2]
    station = lax.broadcasted_iota(jnp.int32, (STATION_COUNT, slots), 0)
    for end in range(2):
        hit = station == pairs_ref[end : end + 1, :]
        table_ref[:, end * slots : (end + 1) * slots] = jnp.where(hit, 1.0, 0.0).astype(
            jnp.bfloat16
        )
    real, imag, power = {}, {}, {}
    for p in range(2):
        for q in range(2):
            plane = 2 * p + q
            vis_real = chunk_ref[plane].astype(jnp.float32)
            vis_imag = chunk_ref[4 + plane].astype(jnp.float32)
            model_real = chunk_ref[8 + plane].astype(jnp.float32)
            model_imag = chunk_ref[12 + plane].astype(jnp.float32)
            real[p, q] = model_real * vis_real + model_imag * vis_imag
            imag[p, q] = model_real * vis_imag - model_imag * vis_real
            power[p, q] = model_real * model_real + model_imag * model_imag
            products_ref[plane] = real[p, q]
            products_ref[4 + plane] = imag[p, q]
            products_ref[8 + plane] = power[p, q]
    first = [real[p, 0] + real[p, 1] for p in range(2)]
    first += [imag[p, 0] + imag[p, 1] for p in range(2)]
    first += [power[p, 0] + power[p, 1] for p in range(2)]
    second = [real[0, q] + real[1, q] for q in range(2)]
    second += [-(imag[0, q] + imag[1, q]) for q in range(2)]
    second += [power[0, q] + power[1, q] for q in range(2)]
    return scatter(jnp.concatenate(first, 0), jnp.concatenate(second, 0), table_ref[...])


def tile_kernel(chunk_ref, pairs_ref, products_ref, table_ref, sums_ref):
    sums_ref[...] = tile_terms(chunk_ref, pairs_ref, products_ref, table_ref)


def gain_terms(gains, products_ref, table_ref):
    share = products_ref.shape[1]
    slots = products_ref.shape[2]
    ends = split_dot(gains, table_ref[...], ((1,), (0,)))
    gain = lambda part, feed, end: ends[
        (2 * part + feed) * share : (2 * part + feed + 1) * share,
        end * slots : (end + 1) * slots,
    ]
    size = {
        (feed, end): gain(0, feed, end) * gain(0, feed, end)
        + gain(1, feed, end) * gain(1, feed, end)
        for feed in range(2)
        for end in range(2)
    }
    real = lambda p, q: products_ref[2 * p + q]
    imag = lambda p, q: products_ref[4 + 2 * p + q]
    power = lambda p, q: products_ref[8 + 2 * p + q]
    first = [
        sum(gain(0, q, 1) * real(p, q) - gain(1, q, 1) * imag(p, q) for q in range(2))
        for p in range(2)
    ]
    first += [
        sum(gain(0, q, 1) * imag(p, q) + gain(1, q, 1) * real(p, q) for q in range(2))
        for p in range(2)
    ]
    first += [sum(size[q, 1] * power(p, q) for q in range(2)) for p in range(2)]
    second = [
        sum(gain(0, p, 0) * real(p, q) + gain(1, p, 0) * imag(p, q) for p in range(2))
        for q in range(2)
    ]
    second += [
        sum(gain(1, p, 0) * real(p, q) - gain(0, p, 0) * imag(p, q) for p in range(2))
        for q in range(2)
    ]
    second += [sum(size[p, 0] * power(p, q) for p in range(2)) for q in range(2)]
    return scatter(jnp.concatenate(first, 0), jnp.concatenate(second, 0), table_ref[...])


def solve_kernel(tiles, *refs):
    chunk_ref, pairs_ref = refs[:2]
    products = refs[2 : 1 + tiles]
    tables = refs[1 + tiles : 2 * tiles]
    sums = refs[2 * tiles : 3 * tiles - 1]
    outs = refs[3 * tiles - 1 : 4 * tiles - 1]
    own_products, own_table, solved_ref = refs[4 * tiles - 1 :]
    share = chunk_ref.shape[1]
    total = tile_terms(chunk_ref, pairs_ref, own_products, own_table)
    for part in sums:
        total = total + part[...]
    rows = 2 * share
    divisor = total[2 * rows :] + damping
    gains = jnp.concatenate([(total[:rows] + damping) / divisor, total[rows : 2 * rows] / divisor])
    total = gain_terms(gains, own_products, own_table)
    for products_ref, table_ref in zip(products, tables):
        total = total + gain_terms(gains, products_ref, table_ref)
    divisor = total[2 * rows :] + damping
    renewed = (total[: 2 * rows] + damping * gains) / jnp.concatenate([divisor, divisor])
    solved_ref[...] = 0.5 * (renewed + gains)
    owned = STATION_COUNT // tiles
    here = lax.axis_index("bl")
    for step in range(tiles):
        start = pl.multiple_of((here ^ step) * owned, owned)
        outs[step][...] = solved_ref[:, pl.ds(start, owned)]


def moment_kernel(basis_ref, *refs):
    tiles = len(refs) - 2
    pieces, solved_ref, moments_ref = refs[:tiles], refs[tiles], refs[tiles + 1]
    share = pieces[0].shape[0] // 4
    here = lax.axis_index("bl")
    for step in range(tiles):
        start = pl.multiple_of((here ^ step) * share, share)
        for part in range(4):
            solved_ref[part, pl.ds(start, share), :] = pieces[step][
                part * share : (part + 1) * share, :
            ]
    for degree in range(4):
        column = basis_ref[:, degree : degree + 1]
        for part in range(4):
            moments_ref[4 * degree + part : 4 * degree + part + 1, :] = jnp.sum(
                solved_ref[part] * column, axis=0, keepdims=True
            )


def fit_kernel(basis_ref, *refs):
    total = refs[0][...]
    for part in refs[1:-1]:
        total = total + part[...]
    fitted_ref = refs[-1]
    for part in range(4):
        fitted_ref[part] = sum(
            basis_ref[:, degree : degree + 1] * total[4 * degree + part : 4 * degree + part + 1, :]
            for degree in range(4)
        )


def vmem_call(kernel, outs, scratch=(), **options):
    def call(*args):
        return pl.pallas_call(
            kernel,
            out_shape=outs,
            in_specs=[pl.BlockSpec(memory_space=pltpu.VMEM)] * len(args),
            out_specs=jax.tree.map(lambda _: pl.BlockSpec(memory_space=pltpu.VMEM), outs),
            scratch_shapes=list(scratch),
            compiler_params=pltpu.CompilerParams(vmem_limit_bytes=24 << 20),
            **options,
        )(*args)

    return call


def partners(count, step):
    return [(index, index ^ step) for index in range(count)]


def local_resplit(visibilities, sky_model, antenna_pairs, tile_counts, usable_mask):
    channel_local = visibilities.shape[1]
    slots = visibilities.shape[2]
    tiles = lax.axis_size("bl")
    groups = lax.axis_size("ch")
    share = channel_local // tiles
    owned = STATION_COUNT // tiles
    here = lax.axis_index("bl")
    f32 = jnp.float32
    shape = jax.ShapeDtypeStruct

    live = jnp.arange(slots, dtype=jnp.int32)[None, :] < tile_counts[0]
    weights = jnp.where(live, usable_mask, 0).astype(jnp.bfloat16)

    def chunk(step):
        start = (here ^ step) * share
        cut = lambda data, axis: lax.dynamic_slice_in_dim(data, start, share, axis)
        return jnp.concatenate([cut(visibilities, 1), cut(sky_model, 1) * cut(weights, 0)[None]])

    steps = list(range(1, tiles))
    order = sorted(steps, key=lambda step: step == 1)
    chunks = {0: chunk(0)}
    pairs = {0: antenna_pairs}
    for step in order:
        chunks[step] = lax.ppermute(chunk(step), "bl", partners(tiles, step))
    for step in order:
        pairs[step] = lax.ppermute(antenna_pairs, "bl", partners(tiles, step))

    tile_outs = (
        shape((12, share, slots), f32),
        shape((STATION_COUNT, 2 * slots), jnp.bfloat16),
        shape((6 * share, STATION_COUNT), f32),
    )
    cost = pl.CostEstimate(
        flops=24 * share * slots * STATION_COUNT, bytes_accessed=4 << 20, transcendentals=0
    )
    done = [vmem_call(tile_kernel, tile_outs, cost_estimate=cost)(chunks[k], pairs[k]) for k in [0] + order[:-1]]
    last = order[-1]
    pieces = vmem_call(
        functools.partial(solve_kernel, tiles),
        tuple(shape((4 * share, owned), f32) for _ in range(tiles)),
        scratch=[
            pltpu.VMEM((12, share, slots), f32),
            pltpu.VMEM((STATION_COUNT, 2 * slots), jnp.bfloat16),
            pltpu.VMEM((4 * share, STATION_COUNT), f32),
        ],
    )(
        chunks[last],
        pairs[last],
        *[part[0] for part in done],
        *[part[1] for part in done],
        *[part[2] for part in done],
    )
    received = [pieces[0]] + [
        lax.ppermute(pieces[step], "bl", partners(tiles, step)) for step in steps
    ]
    basis = lax.dynamic_slice_in_dim(
        jnp.asarray(poly_basis(channel_local * groups).T),
        lax.axis_index("ch") * channel_local,
        channel_local,
        0,
    )
    solved, moments = vmem_call(
        moment_kernel, (shape((4, channel_local, owned), f32), shape((16, owned), f32))
    )(basis, *received)
    moment_parts = [moments] + [
        lax.ppermute(moments, "ch", partners(groups, step)) for step in range(1, groups)
    ]
    fitted = vmem_call(fit_kernel, shape((4, channel_local, owned), f32))(basis, *moment_parts)
    out_shape = (2, 2, channel_local, owned)
    return solved.reshape(out_shape), fitted.reshape(out_shape)


def local(visibilities, sky_model, antenna_pairs, tile_counts, usable_mask):
    tiles = lax.axis_size("bl")
    groups = lax.axis_size("ch")
    power_of_two = lambda count: count & (count - 1) == 0
    resplit = (
        power_of_two(tiles)
        and power_of_two(groups)
        and 1 < tiles <= 4
        and groups <= 8
        and visibilities.shape[1] % (8 * tiles) == 0
        and STATION_COUNT % (128 * tiles) == 0
        and visibilities.shape[2] % 128 == 0
    )
    body = local_resplit if resplit else local_general
    return body(visibilities, sky_model, antenna_pairs, tile_counts, usable_mask)


def solution(mesh):
    return jax.shard_map(
        local,
        mesh=mesh,
        in_specs=(
            P(None, "ch", ("grp", "bl")),
            P(None, "ch", ("grp", "bl")),
            P(None, ("grp", "bl")),
            P(("grp", "bl")),
            P("ch", ("grp", "bl")),
        ),
        out_specs=(P(None, None, "ch", ("grp", "bl")), P(None, None, "ch", ("grp", "bl"))),
        check_vma=False,
    )
```

```python
import functools
import math

import jax
import jax.numpy as jnp
import numpy as np
from jax import lax
from jax.experimental import pallas as pl
from jax.experimental.pallas import tpu as pltpu
from jax.sharding import PartitionSpec as P

STATION_COUNT = 512
SWEEPS = 2

damping = 4.0
highest = lax.Precision.HIGHEST


def poly_basis(channel_total):
    nodes = (2.0 * np.arange(channel_total, dtype=np.float64) - (channel_total - 1)) / (
        channel_total - 1
    )
    rows = []
    for degree in range(4):
        vector = nodes**degree
        for earlier in rows:
            vector = vector - np.sum(vector * earlier) * earlier
        rows.append(vector / np.sqrt(np.sum(vector * vector)))
    return np.stack(rows).astype(np.float32)


def split_parts(data):
    planes = data.astype(jnp.float32)
    shape_rest = planes.shape[1:]
    return (planes[:4].reshape((2, 2) + shape_rest), planes[4:].reshape((2, 2) + shape_rest))


def contributions(
    model_real_part, model_imaginary, vis_real, vis_imag, first_gain, second_gain, weights
):
    second_real = second_gain[0][None]
    second_imag = second_gain[1][None]
    left_real = model_real_part * second_real + model_imaginary * second_imag
    left_imag = model_imaginary * second_real - model_real_part * second_imag
    first_num_real = jnp.sum(left_real * vis_real + left_imag * vis_imag, axis=1) * weights
    first_num_imag = jnp.sum(left_real * vis_imag - left_imag * vis_real, axis=1) * weights
    first_den = jnp.sum(left_real * left_real + left_imag * left_imag, axis=1) * weights
    first_real = first_gain[0][:, None]
    first_imag = first_gain[1][:, None]
    right_real = model_real_part * first_real - model_imaginary * first_imag
    right_imag = model_real_part * first_imag + model_imaginary * first_real
    second_num_real = jnp.sum(right_real * vis_real + right_imag * vis_imag, axis=0) * weights
    second_num_imag = jnp.sum(right_imag * vis_real - right_real * vis_imag, axis=0) * weights
    second_den = jnp.sum(right_real * right_real + right_imag * right_imag, axis=0) * weights
    return (
        jnp.stack([first_num_real, first_num_imag, first_den]),
        jnp.stack([second_num_real, second_num_imag, second_den]),
    )


def refresh(station_sums, previous):
    divisor = station_sums[2] + damping
    return jnp.stack(
        [
            (station_sums[0] + damping * previous[0]) / divisor,
            (station_sums[1] + damping * previous[1]) / divisor,
        ]
    )


def station_totals(end_first, end_second, first_endpoints, second_ends):
    total_slots = end_first.shape[3]
    flat_first = end_first.reshape(-1, total_slots)
    flat_second = end_second.reshape(-1, total_slots)
    station_index = jnp.arange(STATION_COUNT, dtype=jnp.int32)
    table_first = (first_endpoints[:, None] == station_index[None, :]).astype(jnp.float32)
    table_second = (second_ends[:, None] == station_index[None, :]).astype(jnp.float32)
    summed = jnp.dot(
        flat_first, table_first, precision=highest, preferred_element_type=jnp.float32
    ) + jnp.dot(flat_second, table_second, precision=highest, preferred_element_type=jnp.float32)
    return summed.reshape(end_first.shape[:3] + (STATION_COUNT,))


def local_general(visibilities, sky_model, antenna_pairs, tile_counts, usable_mask):
    vis_real, vis_imag = split_parts(visibilities)
    model_real_part, model_imaginary = split_parts(sky_model)
    channel_local = visibilities.shape[1]
    tile_rows = visibilities.shape[2]
    owned_count = STATION_COUNT // lax.axis_size("bl")
    owner_start = lax.axis_index("bl") * owned_count
    live_slots = jnp.arange(tile_rows, dtype=jnp.int32) < tile_counts[0]
    weights = usable_mask.astype(jnp.float32) * live_slots.astype(jnp.float32)[None, :]
    channel_total = channel_local * lax.axis_size("ch")
    poly_rows = lax.dynamic_slice_in_dim(
        jnp.asarray(poly_basis(channel_total)),
        lax.axis_index("ch") * channel_local,
        channel_local,
        1,
    )
    gain_state = jnp.stack(
        [
            jnp.ones((2, channel_local, STATION_COUNT), jnp.float32),
            jnp.zeros((2, channel_local, STATION_COUNT), jnp.float32),
        ]
    )
    solved = gain_state
    for iteration in range(SWEEPS):
        first_gain = jnp.take(gain_state, antenna_pairs[0], axis=3)
        second_gain = jnp.take(gain_state, antenna_pairs[1], axis=3)
        end_first, end_second = contributions(
            model_real_part, model_imaginary, vis_real, vis_imag, first_gain, second_gain, weights
        )
        partial_sums = station_totals(end_first, end_second, antenna_pairs[0], antenna_pairs[1])
        station_sums = lax.psum_scatter(partial_sums, "bl", scatter_dimension=3, tiled=True)
        previous = lax.dynamic_slice_in_dim(gain_state, owner_start, owned_count, 3)
        renewed = refresh(station_sums, previous)
        if iteration == 1:
            renewed = 0.5 * (renewed + previous)
        solved = renewed
        if iteration < SWEEPS - 1:
            gain_state = lax.all_gather(renewed, "bl", axis=3, tiled=True)
    local_moments = jnp.einsum("kc,rfca->krfa", poly_rows, solved, precision=highest)
    moments = lax.psum(local_moments, "ch")
    fitted = jnp.einsum("kc,krfa->rfca", poly_rows, moments, precision=highest)
    return (solved, fitted)


LANES = 128
INDEX_SHIFT = 256.0


def pack_kernel(order, counts_ref, vis_hbm, sky_hbm, pairs_hbm, mask_hbm, *refs):
    tiles = len(order)
    outs = refs[:tiles]
    vis, sky, mask, pairs, rows, sems = refs[tiles:]
    slots = pairs.shape[1]
    blocks = slots // LANES
    share = outs[0].shape[1]
    here = lax.axis_index("bl")
    ends_copy = pltpu.make_async_copy(pairs_hbm, pairs, sems.at[0])
    copies = []
    for slot, step in enumerate(order):
        channels = pl.ds(pl.multiple_of((here ^ step) * share, share), share)
        copies.append(
            [
                pltpu.make_async_copy(mask_hbm.at[channels], mask.at[slot], sems.at[1 + 3 * slot]),
                pltpu.make_async_copy(sky_hbm.at[:, channels], sky.at[slot], sems.at[2 + 3 * slot]),
                pltpu.make_async_copy(vis_hbm.at[:, channels], vis.at[slot], sems.at[3 + 3 * slot]),
            ]
        )
    ends_copy.start()
    for group in copies:
        for copy in group:
            copy.start()
    ends_copy.wait()
    for end in range(2):
        for block in range(blocks):
            row = end * blocks + block
            rows[row : row + 1, :] = pairs[end : end + 1, block * LANES : (block + 1) * LANES]
    ends = (rows[...].astype(jnp.float32) - INDEX_SHIFT).astype(jnp.bfloat16)
    live = lax.broadcasted_iota(jnp.int32, (share, slots), 1) < counts_ref[0]
    for slot in range(tiles):
        out = outs[slot]
        for copy in copies[slot]:
            copy.wait()
        weights = jnp.where(live, mask[slot], 0).astype(jnp.float32).astype(jnp.bfloat16)
        for block in range(blocks):
            lanes = slice(block * LANES, (block + 1) * LANES)
            for plane in range(8):
                out[16 * block + plane] = vis[slot, plane, :, lanes]
                out[16 * block + 8 + plane] = sky[slot, plane, :, lanes] * weights[:, lanes]
        out[16 * blocks] = ends


def split_dot(values, table, dims):
    rows = values.shape[0]
    high = values.astype(jnp.bfloat16)
    low = (values - high.astype(jnp.float32)).astype(jnp.bfloat16)
    both = lax.dot_general(
        jnp.concatenate([high, low], axis=0),
        table,
        (dims, ((), ())),
        preferred_element_type=jnp.float32,
    )
    return both[:rows] + both[rows:]


def scatter(first, second, table):
    return split_dot(jnp.concatenate([first, second], axis=1), table, ((1,), (1,)))


def tile_terms(chunk_ref, products_ref, table_ref):
    slots = products_ref.shape[2]
    blocks = slots // LANES
    ends = chunk_ref[chunk_ref.shape[0] - 1].astype(jnp.float32)
    station = lax.broadcasted_iota(jnp.int32, (STATION_COUNT, LANES), 0).astype(jnp.float32)
    station = station - INDEX_SHIFT
    for block in range(2 * blocks):
        hit = station == ends[block : block + 1, :]
        table_ref[:, block * LANES : (block + 1) * LANES] = jnp.where(hit, 1.0, 0.0).astype(
            jnp.bfloat16
        )
    plane_of = lambda plane: jnp.concatenate(
        [chunk_ref[16 * block + plane].astype(jnp.float32) for block in range(blocks)], axis=1
    )
    real, imag, power = {}, {}, {}
    for p in range(2):
        for q in range(2):
            plane = 2 * p + q
            vis_real = plane_of(plane)
            vis_imag = plane_of(4 + plane)
            model_real = plane_of(8 + plane)
            model_imag = plane_of(12 + plane)
            real[p, q] = model_real * vis_real + model_imag * vis_imag
            imag[p, q] = model_real * vis_imag - model_imag * vis_real
            power[p, q] = model_real * model_real + model_imag * model_imag
            products_ref[plane] = real[p, q]
            products_ref[4 + plane] = imag[p, q]
            products_ref[8 + plane] = power[p, q]
    first = [real[p, 0] + real[p, 1] for p in range(2)]
    first += [imag[p, 0] + imag[p, 1] for p in range(2)]
    first += [power[p, 0] + power[p, 1] for p in range(2)]
    second = [real[0, q] + real[1, q] for q in range(2)]
    second += [-(imag[0, q] + imag[1, q]) for q in range(2)]
    second += [power[0, q] + power[1, q] for q in range(2)]
    return scatter(jnp.concatenate(first, 0), jnp.concatenate(second, 0), table_ref[...])


def tile_kernel(chunk_ref, products_ref, table_ref, sums_ref):
    sums_ref[...] = tile_terms(chunk_ref, products_ref, table_ref)


def gain_terms(gains, products_ref, table_ref):
    share = products_ref.shape[1]
    slots = products_ref.shape[2]
    ends = split_dot(gains, table_ref[...], ((1,), (0,)))
    gain = lambda part, feed, end: ends[
        (2 * part + feed) * share : (2 * part + feed + 1) * share,
        end * slots : (end + 1) * slots,
    ]
    size = {
        (feed, end): gain(0, feed, end) * gain(0, feed, end)
        + gain(1, feed, end) * gain(1, feed, end)
        for feed in range(2)
        for end in range(2)
    }
    real = lambda p, q: products_ref[2 * p + q]
    imag = lambda p, q: products_ref[4 + 2 * p + q]
    power = lambda p, q: products_ref[8 + 2 * p + q]
    first = [
        sum(gain(0, q, 1) * real(p, q) - gain(1, q, 1) * imag(p, q) for q in range(2))
        for p in range(2)
    ]
    first += [
        sum(gain(0, q, 1) * imag(p, q) + gain(1, q, 1) * real(p, q) for q in range(2))
        for p in range(2)
    ]
    first += [sum(size[q, 1] * power(p, q) for q in range(2)) for p in range(2)]
    second = [
        sum(gain(0, p, 0) * real(p, q) + gain(1, p, 0) * imag(p, q) for p in range(2))
        for q in range(2)
    ]
    second += [
        sum(gain(1, p, 0) * real(p, q) - gain(0, p, 0) * imag(p, q) for p in range(2))
        for q in range(2)
    ]
    second += [sum(size[p, 0] * power(p, q) for p in range(2)) for q in range(2)]
    return scatter(jnp.concatenate(first, 0), jnp.concatenate(second, 0), table_ref[...])


def solve_kernel(tiles, *refs):
    chunk_ref = refs[0]
    products = refs[1:tiles]
    tables = refs[tiles : 2 * tiles - 1]
    sums = refs[2 * tiles - 1 : 3 * tiles - 2]
    outs = refs[3 * tiles - 2 : 4 * tiles - 2]
    own_products, own_table, solved_ref = refs[4 * tiles - 2 :]
    share = chunk_ref.shape[1]
    total = tile_terms(chunk_ref, own_products, own_table)
    for part in sums:
        total = total + part[...]
    rows = 2 * share
    divisor = total[2 * rows :] + damping
    gains = jnp.concatenate([(total[:rows] + damping) / divisor, total[rows : 2 * rows] / divisor])
    total = gain_terms(gains, own_products, own_table)
    for products_ref, table_ref in zip(products, tables):
        total = total + gain_terms(gains, products_ref, table_ref)
    divisor = total[2 * rows :] + damping
    renewed = (total[: 2 * rows] + damping * gains) / jnp.concatenate([divisor, divisor])
    solved_ref[...] = 0.5 * (renewed + gains)
    owned = STATION_COUNT // tiles
    here = lax.axis_index("bl")
    for step in range(tiles):
        start = pl.multiple_of((here ^ step) * owned, owned)
        outs[step][...] = solved_ref[:, pl.ds(start, owned)]


def moment_kernel(basis_ref, *refs):
    tiles = len(refs) - 2
    pieces, solved_ref, moments_ref = refs[:tiles], refs[tiles], refs[tiles + 1]
    share = pieces[0].shape[0] // 4
    here = lax.axis_index("bl")
    for step in range(tiles):
        start = pl.multiple_of((here ^ step) * share, share)
        for part in range(4):
            solved_ref[part, pl.ds(start, share), :] = pieces[step][
                part * share : (part + 1) * share, :
            ]
    for degree in range(4):
        column = basis_ref[:, degree : degree + 1]
        for part in range(4):
            moments_ref[4 * degree + part : 4 * degree + part + 1, :] = jnp.sum(
                solved_ref[part] * column, axis=0, keepdims=True
            )


def fit_kernel(basis_ref, *refs):
    total = refs[0][...]
    for part in refs[1:-1]:
        total = total + part[...]
    fitted_ref = refs[-1]
    for part in range(4):
        fitted_ref[part] = sum(
            basis_ref[:, degree : degree + 1] * total[4 * degree + part : 4 * degree + part + 1, :]
            for degree in range(4)
        )


def vmem_call(kernel, outs, scratch=(), spaces=None, **options):
    def call(*args):
        return pl.pallas_call(
            kernel,
            out_shape=outs,
            in_specs=[
                pl.BlockSpec(memory_space=space) for space in spaces or [pltpu.VMEM] * len(args)
            ],
            out_specs=jax.tree.map(lambda _: pl.BlockSpec(memory_space=pltpu.VMEM), outs),
            scratch_shapes=list(scratch),
            compiler_params=pltpu.CompilerParams(vmem_limit_bytes=24 << 20),
            **options,
        )(*args)

    return call


def in_hbm(value):
    return pltpu.with_memory_space_constraint(value, pltpu.HBM)


def partners(count, step):
    return [(index, index ^ step) for index in range(count)]


def local_resplit(visibilities, sky_model, antenna_pairs, tile_counts, usable_mask):
    channel_local = visibilities.shape[1]
    slots = visibilities.shape[2]
    tiles = lax.axis_size("bl")
    groups = lax.axis_size("ch")
    share = channel_local // tiles
    owned = STATION_COUNT // tiles
    f32 = jnp.float32
    shape = jax.ShapeDtypeStruct

    steps = list(range(1, tiles))
    order = sorted(steps, key=lambda step: step == 1)
    blocks = slots // LANES
    chunk_shape = shape((16 * blocks + 1, share, LANES), jnp.bfloat16)
    packed = vmem_call(
        functools.partial(pack_kernel, order + [0]),
        (chunk_shape,) * tiles,
        scratch=[
            pltpu.VMEM((tiles, 8, share, slots), jnp.bfloat16),
            pltpu.VMEM((tiles, 8, share, slots), jnp.bfloat16),
            pltpu.VMEM((tiles, share, slots), jnp.int32),
            pltpu.VMEM((2, slots), jnp.int32),
            pltpu.VMEM((2 * blocks, LANES), jnp.int32),
            pltpu.SemaphoreType.DMA((1 + 3 * tiles,)),
        ],
        spaces=[pltpu.SMEM] + [pltpu.HBM] * 4,
    )(tile_counts, *[in_hbm(x) for x in (visibilities, sky_model, antenna_pairs, usable_mask)])
    chunks = {0: packed[-1]}
    for step, piece in zip(order, packed):
        chunks[step] = lax.ppermute(piece, "bl", partners(tiles, step))

    tile_outs = (
        shape((12, share, slots), f32),
        shape((STATION_COUNT, 2 * slots), jnp.bfloat16),
        shape((6 * share, STATION_COUNT), f32),
    )
    cost = pl.CostEstimate(
        flops=24 * share * slots * STATION_COUNT, bytes_accessed=4 << 20, transcendentals=0
    )
    done = [vmem_call(tile_kernel, tile_outs, cost_estimate=cost)(chunks[k]) for k in [0] + order[:-1]]
    last = order[-1]
    pieces = vmem_call(
        functools.partial(solve_kernel, tiles),
        tuple(shape((4 * share, owned), f32) for _ in range(tiles)),
        scratch=[
            pltpu.VMEM((12, share, slots), f32),
            pltpu.VMEM((STATION_COUNT, 2 * slots), jnp.bfloat16),
            pltpu.VMEM((4 * share, STATION_COUNT), f32),
        ],
    )(
        chunks[last],
        *[part[0] for part in done],
        *[part[1] for part in done],
        *[part[2] for part in done],
    )
    received = [pieces[0]] + [
        lax.ppermute(pieces[step], "bl", partners(tiles, step)) for step in steps
    ]
    basis = lax.dynamic_slice_in_dim(
        jnp.asarray(poly_basis(channel_local * groups).T),
        lax.axis_index("ch") * channel_local,
        channel_local,
        0,
    )
    solved, moments = vmem_call(
        moment_kernel, (shape((4, channel_local, owned), f32), shape((16, owned), f32))
    )(basis, *received)
    moment_parts = [moments] + [
        lax.ppermute(moments, "ch", partners(groups, step)) for step in range(1, groups)
    ]
    fitted = vmem_call(fit_kernel, shape((4, channel_local, owned), f32))(basis, *moment_parts)
    out_shape = (2, 2, channel_local, owned)
    return solved.reshape(out_shape), fitted.reshape(out_shape)


def local(visibilities, sky_model, antenna_pairs, tile_counts, usable_mask):
    tiles = lax.axis_size("bl")
    groups = lax.axis_size("ch")
    power_of_two = lambda count: count & (count - 1) == 0
    resplit = (
        power_of_two(tiles)
        and power_of_two(groups)
        and 1 < tiles <= 4
        and groups <= 8
        and visibilities.shape[1] == 8 * tiles
        and STATION_COUNT % (128 * tiles) == 0
        and STATION_COUNT <= 2 * INDEX_SHIFT
        and visibilities.shape[2] == 4 * LANES
    )
    body = local_resplit if resplit else local_general
    return body(visibilities, sky_model, antenna_pairs, tile_counts, usable_mask)


def solution(mesh):
    return jax.shard_map(
        local,
        mesh=mesh,
        in_specs=(
            P(None, "ch", ("grp", "bl")),
            P(None, "ch", ("grp", "bl")),
            P(None, ("grp", "bl")),
            P(("grp", "bl")),
            P("ch", ("grp", "bl")),
        ),
        out_specs=(P(None, None, "ch", ("grp", "bl")), P(None, None, "ch", ("grp", "bl"))),
        check_vma=False,
    )
```

```python
import functools
import math

import jax
import jax.numpy as jnp
import numpy as np
from jax import lax
from jax.experimental import pallas as pl
from jax.experimental.pallas import tpu as pltpu
from jax.sharding import PartitionSpec as P

STATION_COUNT = 512
SWEEPS = 2

damping = 4.0
highest = lax.Precision.HIGHEST


def poly_basis(channel_total):
    nodes = (2.0 * np.arange(channel_total, dtype=np.float64) - (channel_total - 1)) / (
        channel_total - 1
    )
    rows = []
    for degree in range(4):
        vector = nodes**degree
        for earlier in rows:
            vector = vector - np.sum(vector * earlier) * earlier
        rows.append(vector / np.sqrt(np.sum(vector * vector)))
    return np.stack(rows).astype(np.float32)


def split_parts(data):
    planes = data.astype(jnp.float32)
    shape_rest = planes.shape[1:]
    return (planes[:4].reshape((2, 2) + shape_rest), planes[4:].reshape((2, 2) + shape_rest))


def contributions(
    model_real_part, model_imaginary, vis_real, vis_imag, first_gain, second_gain, weights
):
    second_real = second_gain[0][None]
    second_imag = second_gain[1][None]
    left_real = model_real_part * second_real + model_imaginary * second_imag
    left_imag = model_imaginary * second_real - model_real_part * second_imag
    first_num_real = jnp.sum(left_real * vis_real + left_imag * vis_imag, axis=1) * weights
    first_num_imag = jnp.sum(left_real * vis_imag - left_imag * vis_real, axis=1) * weights
    first_den = jnp.sum(left_real * left_real + left_imag * left_imag, axis=1) * weights
    first_real = first_gain[0][:, None]
    first_imag = first_gain[1][:, None]
    right_real = model_real_part * first_real - model_imaginary * first_imag
    right_imag = model_real_part * first_imag + model_imaginary * first_real
    second_num_real = jnp.sum(right_real * vis_real + right_imag * vis_imag, axis=0) * weights
    second_num_imag = jnp.sum(right_imag * vis_real - right_real * vis_imag, axis=0) * weights
    second_den = jnp.sum(right_real * right_real + right_imag * right_imag, axis=0) * weights
    return (
        jnp.stack([first_num_real, first_num_imag, first_den]),
        jnp.stack([second_num_real, second_num_imag, second_den]),
    )


def refresh(station_sums, previous):
    divisor = station_sums[2] + damping
    return jnp.stack(
        [
            (station_sums[0] + damping * previous[0]) / divisor,
            (station_sums[1] + damping * previous[1]) / divisor,
        ]
    )


def station_totals(end_first, end_second, first_endpoints, second_ends):
    total_slots = end_first.shape[3]
    flat_first = end_first.reshape(-1, total_slots)
    flat_second = end_second.reshape(-1, total_slots)
    station_index = jnp.arange(STATION_COUNT, dtype=jnp.int32)
    table_first = (first_endpoints[:, None] == station_index[None, :]).astype(jnp.float32)
    table_second = (second_ends[:, None] == station_index[None, :]).astype(jnp.float32)
    summed = jnp.dot(
        flat_first, table_first, precision=highest, preferred_element_type=jnp.float32
    ) + jnp.dot(flat_second, table_second, precision=highest, preferred_element_type=jnp.float32)
    return summed.reshape(end_first.shape[:3] + (STATION_COUNT,))


def local_general(visibilities, sky_model, antenna_pairs, tile_counts, usable_mask):
    vis_real, vis_imag = split_parts(visibilities)
    model_real_part, model_imaginary = split_parts(sky_model)
    channel_local = visibilities.shape[1]
    tile_rows = visibilities.shape[2]
    owned_count = STATION_COUNT // lax.axis_size("bl")
    owner_start = lax.axis_index("bl") * owned_count
    live_slots = jnp.arange(tile_rows, dtype=jnp.int32) < tile_counts[0]
    weights = usable_mask.astype(jnp.float32) * live_slots.astype(jnp.float32)[None, :]
    channel_total = channel_local * lax.axis_size("ch")
    poly_rows = lax.dynamic_slice_in_dim(
        jnp.asarray(poly_basis(channel_total)),
        lax.axis_index("ch") * channel_local,
        channel_local,
        1,
    )
    gain_state = jnp.stack(
        [
            jnp.ones((2, channel_local, STATION_COUNT), jnp.float32),
            jnp.zeros((2, channel_local, STATION_COUNT), jnp.float32),
        ]
    )
    solved = gain_state
    for iteration in range(SWEEPS):
        first_gain = jnp.take(gain_state, antenna_pairs[0], axis=3)
        second_gain = jnp.take(gain_state, antenna_pairs[1], axis=3)
        end_first, end_second = contributions(
            model_real_part, model_imaginary, vis_real, vis_imag, first_gain, second_gain, weights
        )
        partial_sums = station_totals(end_first, end_second, antenna_pairs[0], antenna_pairs[1])
        station_sums = lax.psum_scatter(partial_sums, "bl", scatter_dimension=3, tiled=True)
        previous = lax.dynamic_slice_in_dim(gain_state, owner_start, owned_count, 3)
        renewed = refresh(station_sums, previous)
        if iteration == 1:
            renewed = 0.5 * (renewed + previous)
        solved = renewed
        if iteration < SWEEPS - 1:
            gain_state = lax.all_gather(renewed, "bl", axis=3, tiled=True)
    local_moments = jnp.einsum("kc,rfca->krfa", poly_rows, solved, precision=highest)
    moments = lax.psum(local_moments, "ch")
    fitted = jnp.einsum("kc,krfa->rfca", poly_rows, moments, precision=highest)
    return (solved, fitted)


LANES = 128
INDEX_SHIFT = 256.0


def pack_kernel(order, counts_ref, vis_hbm, sky_hbm, pairs_hbm, mask_hbm, *refs):
    tiles = len(order)
    outs = refs[:tiles]
    vis, sky, mask, pairs, rows, sems = refs[tiles:]
    slots = pairs.shape[1]
    blocks = slots // LANES
    share = outs[0].shape[1]
    here = lax.axis_index("bl")
    ends_copy = pltpu.make_async_copy(pairs_hbm, pairs, sems.at[0])
    copies = []
    for slot, step in enumerate(order):
        channels = pl.ds(pl.multiple_of((here ^ step) * share, share), share)
        copies.append(
            [
                pltpu.make_async_copy(mask_hbm.at[channels], mask.at[slot], sems.at[1 + 3 * slot]),
                pltpu.make_async_copy(sky_hbm.at[:, channels], sky.at[slot], sems.at[2 + 3 * slot]),
                pltpu.make_async_copy(vis_hbm.at[:, channels], vis.at[slot], sems.at[3 + 3 * slot]),
            ]
        )
    ends_copy.start()
    for group in copies:
        for copy in group:
            copy.start()
    ends_copy.wait()
    for end in range(2):
        for block in range(blocks):
            row = end * blocks + block
            rows[row : row + 1, :] = pairs[end : end + 1, block * LANES : (block + 1) * LANES]
    ends = (rows[...].astype(jnp.float32) - INDEX_SHIFT).astype(jnp.bfloat16)
    live = lax.broadcasted_iota(jnp.int32, (share, slots), 1) < counts_ref[0]
    for slot in range(tiles):
        out = outs[slot]
        for copy in copies[slot]:
            copy.wait()
        weights = jnp.where(live, mask[slot], 0).astype(jnp.float32).astype(jnp.bfloat16)
        for block in range(blocks):
            lanes = slice(block * LANES, (block + 1) * LANES)
            for plane in range(8):
                out[16 * block + plane] = vis[slot, plane, :, lanes]
                out[16 * block + 8 + plane] = sky[slot, plane, :, lanes] * weights[:, lanes]
        out[16 * blocks] = ends


def pieces_of(values):
    high = values.astype(jnp.bfloat16)
    low = (values - high.astype(jnp.float32)).astype(jnp.bfloat16)
    return jnp.concatenate([high, low], axis=0)


def station_sums(first, second, table):
    rows = first.shape[0]
    both = lax.dot_general(
        pieces_of(jnp.concatenate([first, second], axis=1)),
        table,
        (((1,), (1,)), ((), ())),
        preferred_element_type=jnp.float32,
    )
    return both[:rows] + both[rows:]


def end_table(chunk_ref, table_ref):
    rows = table_ref.shape[1] // LANES
    ends = chunk_ref[chunk_ref.shape[0] - 1]
    station = lax.broadcasted_iota(jnp.int32, (STATION_COUNT, LANES), 0).astype(jnp.float32)
    station = (station - INDEX_SHIFT).astype(jnp.bfloat16)
    one = jnp.ones((), jnp.bfloat16)
    zero = jnp.zeros((), jnp.bfloat16)
    for row in range(rows):
        table_ref[:, row * LANES : (row + 1) * LANES] = jnp.where(
            station == ends[row : row + 1, :], one, zero
        )


def unit_terms(chunk_ref, products_ref):
    blocks = products_ref.shape[2] // LANES
    plane_of = lambda plane: jnp.concatenate(
        [chunk_ref[16 * block + plane].astype(jnp.float32) for block in range(blocks)], axis=1
    )
    real, imag, power = {}, {}, {}
    for p in range(2):
        for q in range(2):
            plane = 2 * p + q
            vis_real = plane_of(plane)
            vis_imag = plane_of(4 + plane)
            model_real = plane_of(8 + plane)
            model_imag = plane_of(12 + plane)
            real[p, q] = model_real * vis_real + model_imag * vis_imag
            imag[p, q] = model_real * vis_imag - model_imag * vis_real
            power[p, q] = model_real * model_real + model_imag * model_imag
            products_ref[plane] = real[p, q]
            products_ref[4 + plane] = imag[p, q]
            products_ref[8 + plane] = power[p, q]
    first = [real[p, 0] + real[p, 1] for p in range(2)]
    first += [imag[p, 0] + imag[p, 1] for p in range(2)]
    first += [power[p, 0] + power[p, 1] for p in range(2)]
    second = [real[0, q] + real[1, q] for q in range(2)]
    second += [-(imag[0, q] + imag[1, q]) for q in range(2)]
    second += [power[0, q] + power[1, q] for q in range(2)]
    return jnp.concatenate(first, 0), jnp.concatenate(second, 0)


def tile_kernel(chunk_ref, products_ref, table_ref, sums_ref):
    end_table(chunk_ref, table_ref)
    sums_ref[...] = station_sums(*unit_terms(chunk_ref, products_ref), table_ref[...])


def end_gains(gains, chunk_ref, share, blocks):
    ends = (chunk_ref[chunk_ref.shape[0] - 1].astype(jnp.float32) + INDEX_SHIFT).astype(jnp.int32)
    result = []
    for end in range(2):
        found = {row: [] for row in range(4)}
        for block in range(blocks):
            row = end * blocks + block
            index = jnp.broadcast_to(ends[row : row + 1, :], (share, LANES))
            lane = index % LANES
            group = index // LANES
            for part in range(4):
                rows = gains[part * share : (part + 1) * share]
                value = None
                for source in range(STATION_COUNT // LANES):
                    picked = jnp.take_along_axis(
                        rows[:, source * LANES : (source + 1) * LANES],
                        lane,
                        axis=1,
                        mode="promise_in_bounds",
                    )
                    value = picked if value is None else jnp.where(group == source, picked, value)
                found[part].append(value)
        result.append([jnp.concatenate(found[part], axis=1) for part in range(4)])
    return result


def gain_terms(gains, chunk_ref, products_ref):
    share = products_ref.shape[1]
    blocks = products_ref.shape[2] // LANES
    at = end_gains(gains, chunk_ref, share, blocks)
    gain = lambda part, feed, end: at[end][2 * part + feed]
    size = {
        (feed, end): gain(0, feed, end) * gain(0, feed, end)
        + gain(1, feed, end) * gain(1, feed, end)
        for feed in range(2)
        for end in range(2)
    }
    real = lambda p, q: products_ref[2 * p + q]
    imag = lambda p, q: products_ref[4 + 2 * p + q]
    power = lambda p, q: products_ref[8 + 2 * p + q]
    first = [
        sum(gain(0, q, 1) * real(p, q) - gain(1, q, 1) * imag(p, q) for q in range(2))
        for p in range(2)
    ]
    first += [
        sum(gain(0, q, 1) * imag(p, q) + gain(1, q, 1) * real(p, q) for q in range(2))
        for p in range(2)
    ]
    first += [sum(size[q, 1] * power(p, q) for q in range(2)) for p in range(2)]
    second = [
        sum(gain(0, p, 0) * real(p, q) + gain(1, p, 0) * imag(p, q) for p in range(2))
        for q in range(2)
    ]
    second += [
        sum(gain(1, p, 0) * real(p, q) - gain(0, p, 0) * imag(p, q) for p in range(2))
        for q in range(2)
    ]
    second += [sum(size[p, 0] * power(p, q) for p in range(2)) for q in range(2)]
    return jnp.concatenate(first, 0), jnp.concatenate(second, 0)


def solve_kernel(early, late, *refs):
    tiles = early + late
    chunks, refs = refs[:tiles], refs[tiles:]
    products, refs = refs[:early], refs[early:]
    tables, refs = refs[:early], refs[early:]
    sums, refs = refs[:early], refs[early:]
    outs, refs = refs[:tiles], refs[tiles:]
    late_products, refs = refs[:late], refs[late:]
    late_tables, refs = refs[:late], refs[late:]
    (solved_ref,) = refs
    share = chunks[0].shape[1]
    total = sum(part[...] for part in sums)
    for chunk_ref, products_ref, table_ref in zip(chunks[early:], late_products, late_tables):
        end_table(chunk_ref, table_ref)
        total = total + station_sums(*unit_terms(chunk_ref, products_ref), table_ref[...])
    rows = 2 * share
    divisor = total[2 * rows :] + damping
    gains = jnp.concatenate([(total[:rows] + damping) / divisor, total[rows : 2 * rows] / divisor])
    total = 0.0
    for chunk_ref, products_ref, table_ref in zip(
        chunks, products + late_products, tables + late_tables
    ):
        total = total + station_sums(
            *gain_terms(gains, chunk_ref, products_ref), table_ref[...]
        )
    divisor = total[2 * rows :] + damping
    renewed = (total[: 2 * rows] + damping * gains) / jnp.concatenate([divisor, divisor])
    solved_ref[...] = 0.5 * (renewed + gains)
    owned = STATION_COUNT // tiles
    here = lax.axis_index("bl")
    for step in range(tiles):
        start = pl.multiple_of((here ^ step) * owned, owned)
        outs[step][...] = solved_ref[:, pl.ds(start, owned)]


def moment_kernel(basis_ref, *refs):
    pieces, moments_ref = refs[:-1], refs[-1]
    share = pieces[0].shape[0] // 4
    here = lax.axis_index("bl")
    columns = []
    for step in range(len(pieces)):
        start = pl.multiple_of((here ^ step) * share, share)
        columns.append(basis_ref[pl.ds(start, share), :])
    for degree in range(4):
        for part in range(4):
            terms = sum(
                piece[part * share : (part + 1) * share, :] * column[:, degree : degree + 1]
                for piece, column in zip(pieces, columns)
            )
            row = 4 * degree + part
            moments_ref[row : row + 1, :] = jnp.sum(terms, axis=0, keepdims=True)


def order_kernel(*refs):
    pieces, solved_ref = refs[:-1], refs[-1]
    share = pieces[0].shape[0] // 4
    here = lax.axis_index("bl")
    for step, piece in enumerate(pieces):
        start = pl.multiple_of((here ^ step) * share, share)
        for part in range(4):
            solved_ref[part, pl.ds(start, share), :] = piece[part * share : (part + 1) * share, :]


def fit_kernel(basis_ref, *refs):
    total = refs[0][...]
    for part in refs[1:-1]:
        total = total + part[...]
    fitted_ref = refs[-1]
    for part in range(4):
        fitted_ref[part] = sum(
            basis_ref[:, degree : degree + 1] * total[4 * degree + part : 4 * degree + part + 1, :]
            for degree in range(4)
        )


def vmem_call(kernel, outs, scratch=(), spaces=None, **options):
    def call(*args):
        return pl.pallas_call(
            kernel,
            out_shape=outs,
            in_specs=[
                pl.BlockSpec(memory_space=space) for space in spaces or [pltpu.VMEM] * len(args)
            ],
            out_specs=jax.tree.map(lambda _: pl.BlockSpec(memory_space=pltpu.VMEM), outs),
            scratch_shapes=list(scratch),
            compiler_params=pltpu.CompilerParams(vmem_limit_bytes=24 << 20),
            **options,
        )(*args)

    return call


def in_hbm(value):
    return pltpu.with_memory_space_constraint(value, pltpu.HBM)


def partners(count, step):
    return [(index, index ^ step) for index in range(count)]


def local_resplit(visibilities, sky_model, antenna_pairs, tile_counts, usable_mask):
    channel_local = visibilities.shape[1]
    slots = visibilities.shape[2]
    tiles = lax.axis_size("bl")
    groups = lax.axis_size("ch")
    share = channel_local // tiles
    owned = STATION_COUNT // tiles
    f32 = jnp.float32
    shape = jax.ShapeDtypeStruct

    steps = list(range(1, tiles))
    order = sorted(steps, key=lambda step: step == 1)
    blocks = slots // LANES
    chunk_shape = shape((16 * blocks + 1, share, LANES), jnp.bfloat16)
    packed = vmem_call(
        functools.partial(pack_kernel, order + [0]),
        (chunk_shape,) * tiles,
        scratch=[
            pltpu.VMEM((tiles, 8, share, slots), jnp.bfloat16),
            pltpu.VMEM((tiles, 8, share, slots), jnp.bfloat16),
            pltpu.VMEM((tiles, share, slots), jnp.int32),
            pltpu.VMEM((2, slots), jnp.int32),
            pltpu.VMEM((2 * blocks, LANES), jnp.int32),
            pltpu.SemaphoreType.DMA((1 + 3 * tiles,)),
        ],
        spaces=[pltpu.SMEM] + [pltpu.HBM] * 4,
    )(tile_counts, *[in_hbm(x) for x in (visibilities, sky_model, antenna_pairs, usable_mask)])
    chunks = {0: packed[-1]}
    for step, piece in zip(order, packed):
        chunks[step] = lax.ppermute(piece, "bl", partners(tiles, step))

    tile_outs = (
        shape((12, share, slots), f32),
        shape((STATION_COUNT, 2 * slots), jnp.bfloat16),
        shape((6 * share, STATION_COUNT), f32),
    )
    cost = pl.CostEstimate(
        flops=24 * share * slots * STATION_COUNT, bytes_accessed=4 << 20, transcendentals=0
    )
    early, late = [0, 1], [step for step in order if step > 1]
    done = [vmem_call(tile_kernel, tile_outs, cost_estimate=cost)(chunks[k]) for k in early]
    pieces = vmem_call(
        functools.partial(solve_kernel, len(early), len(late)),
        tuple(shape((4 * share, owned), f32) for _ in range(tiles)),
        scratch=[
            *[pltpu.VMEM((12, share, slots), f32) for _ in late],
            *[pltpu.VMEM((STATION_COUNT, 2 * slots), jnp.bfloat16) for _ in late],
            pltpu.VMEM((4 * share, STATION_COUNT), f32),
        ],
    )(
        *[chunks[step] for step in early + late],
        *[part[0] for part in done],
        *[part[1] for part in done],
        *[part[2] for part in done],
    )
    received = {0: pieces[0]}
    for step in reversed(steps):
        received[step] = lax.ppermute(pieces[step], "bl", partners(tiles, step))
    received = [received[step] for step in range(tiles)]
    basis = lax.dynamic_slice_in_dim(
        jnp.asarray(poly_basis(channel_local * groups).T),
        lax.axis_index("ch") * channel_local,
        channel_local,
        0,
    )
    moments = vmem_call(moment_kernel, shape((16, owned), f32))(basis, *received)
    solved = vmem_call(order_kernel, shape((4, channel_local, owned), f32))(*received)
    moment_parts = [moments] + [
        lax.ppermute(moments, "ch", partners(groups, step)) for step in range(1, groups)
    ]
    fitted = vmem_call(fit_kernel, shape((4, channel_local, owned), f32))(basis, *moment_parts)
    out_shape = (2, 2, channel_local, owned)
    return solved.reshape(out_shape), fitted.reshape(out_shape)


def local(visibilities, sky_model, antenna_pairs, tile_counts, usable_mask):
    tiles = lax.axis_size("bl")
    groups = lax.axis_size("ch")
    power_of_two = lambda count: count & (count - 1) == 0
    resplit = (
        power_of_two(tiles)
        and power_of_two(groups)
        and 1 < tiles <= 4
        and groups <= 8
        and visibilities.shape[1] == 8 * tiles
        and STATION_COUNT % (128 * tiles) == 0
        and STATION_COUNT <= 2 * INDEX_SHIFT
        and visibilities.shape[2] == 4 * LANES
    )
    body = local_resplit if resplit else local_general
    return body(visibilities, sky_model, antenna_pairs, tile_counts, usable_mask)


def solution(mesh):
    return jax.shard_map(
        local,
        mesh=mesh,
        in_specs=(
            P(None, "ch", ("grp", "bl")),
            P(None, "ch", ("grp", "bl")),
            P(None, ("grp", "bl")),
            P(("grp", "bl")),
            P("ch", ("grp", "bl")),
        ),
        out_specs=(P(None, None, "ch", ("grp", "bl")), P(None, None, "ch", ("grp", "bl"))),
        check_vma=False,
    )
```

```python
import functools

import jax
import jax.numpy as jnp
import numpy as np
from jax import lax
from jax.experimental import pallas as pl
from jax.experimental.pallas import tpu as pltpu
from jax.sharding import PartitionSpec as P


STATION_COUNT = 512
SWEEPS = 2

damping = 4.0
highest = lax.Precision.HIGHEST


def poly_basis(channel_total):
    nodes = (2.0 * np.arange(channel_total, dtype=np.float64) - (channel_total - 1)) / (
        channel_total - 1
    )
    rows = []
    for degree in range(4):
        vector = nodes**degree
        for earlier in rows:
            vector = vector - np.sum(vector * earlier) * earlier
        rows.append(vector / np.sqrt(np.sum(vector * vector)))
    return np.stack(rows).astype(np.float32)


def split_parts(data):
    planes = data.astype(jnp.float32)
    shape_rest = planes.shape[1:]
    return (planes[:4].reshape((2, 2) + shape_rest), planes[4:].reshape((2, 2) + shape_rest))


def contributions(
    model_real_part, model_imaginary, vis_real, vis_imag, first_gain, second_gain, weights
):
    second_real = second_gain[0][None]
    second_imag = second_gain[1][None]
    left_real = model_real_part * second_real + model_imaginary * second_imag
    left_imag = model_imaginary * second_real - model_real_part * second_imag
    first_num_real = jnp.sum(left_real * vis_real + left_imag * vis_imag, axis=1) * weights
    first_num_imag = jnp.sum(left_real * vis_imag - left_imag * vis_real, axis=1) * weights
    first_den = jnp.sum(left_real * left_real + left_imag * left_imag, axis=1) * weights
    first_real = first_gain[0][:, None]
    first_imag = first_gain[1][:, None]
    right_real = model_real_part * first_real - model_imaginary * first_imag
    right_imag = model_real_part * first_imag + model_imaginary * first_real
    second_num_real = jnp.sum(right_real * vis_real + right_imag * vis_imag, axis=0) * weights
    second_num_imag = jnp.sum(right_imag * vis_real - right_real * vis_imag, axis=0) * weights
    second_den = jnp.sum(right_real * right_real + right_imag * right_imag, axis=0) * weights
    return (
        jnp.stack([first_num_real, first_num_imag, first_den]),
        jnp.stack([second_num_real, second_num_imag, second_den]),
    )


def refresh(station_sums, previous):
    divisor = station_sums[2] + damping
    return jnp.stack(
        [
            (station_sums[0] + damping * previous[0]) / divisor,
            (station_sums[1] + damping * previous[1]) / divisor,
        ]
    )


def station_totals(end_first, end_second, first_endpoints, second_ends):
    total_slots = end_first.shape[3]
    flat_first = end_first.reshape(-1, total_slots)
    flat_second = end_second.reshape(-1, total_slots)
    station_index = jnp.arange(STATION_COUNT, dtype=jnp.int32)
    table_first = (first_endpoints[:, None] == station_index[None, :]).astype(jnp.float32)
    table_second = (second_ends[:, None] == station_index[None, :]).astype(jnp.float32)
    summed = jnp.dot(
        flat_first, table_first, precision=highest, preferred_element_type=jnp.float32
    ) + jnp.dot(flat_second, table_second, precision=highest, preferred_element_type=jnp.float32)
    return summed.reshape(end_first.shape[:3] + (STATION_COUNT,))


def local_general(visibilities, sky_model, antenna_pairs, tile_counts, usable_mask):
    vis_real, vis_imag = split_parts(visibilities)
    model_real_part, model_imaginary = split_parts(sky_model)
    channel_local = visibilities.shape[1]
    tile_rows = visibilities.shape[2]
    owned_count = STATION_COUNT // lax.axis_size("bl")
    owner_start = lax.axis_index("bl") * owned_count
    live_slots = jnp.arange(tile_rows, dtype=jnp.int32) < tile_counts[0]
    weights = usable_mask.astype(jnp.float32) * live_slots.astype(jnp.float32)[None, :]
    channel_total = channel_local * lax.axis_size("ch")
    poly_rows = lax.dynamic_slice_in_dim(
        jnp.asarray(poly_basis(channel_total)),
        lax.axis_index("ch") * channel_local,
        channel_local,
        1,
    )
    gain_state = jnp.stack(
        [
            jnp.ones((2, channel_local, STATION_COUNT), jnp.float32),
            jnp.zeros((2, channel_local, STATION_COUNT), jnp.float32),
        ]
    )
    solved = gain_state
    for iteration in range(SWEEPS):
        first_gain = jnp.take(gain_state, antenna_pairs[0], axis=3)
        second_gain = jnp.take(gain_state, antenna_pairs[1], axis=3)
        end_first, end_second = contributions(
            model_real_part, model_imaginary, vis_real, vis_imag, first_gain, second_gain, weights
        )
        partial_sums = station_totals(end_first, end_second, antenna_pairs[0], antenna_pairs[1])
        station_sums = lax.psum_scatter(partial_sums, "bl", scatter_dimension=3, tiled=True)
        previous = lax.dynamic_slice_in_dim(gain_state, owner_start, owned_count, 3)
        renewed = refresh(station_sums, previous)
        if iteration == 1:
            renewed = 0.5 * (renewed + previous)
        solved = renewed
        if iteration < SWEEPS - 1:
            gain_state = lax.all_gather(renewed, "bl", axis=3, tiled=True)
    local_moments = jnp.einsum("kc,rfca->krfa", poly_rows, solved, precision=highest)
    moments = lax.psum(local_moments, "ch")
    fitted = jnp.einsum("kc,krfa->rfca", poly_rows, moments, precision=highest)
    return (solved, fitted)


LANES = 128
INDEX_SHIFT = 256.0


def pack_kernel(order, counts_ref, vis_hbm, sky_hbm, pairs_hbm, mask_hbm, *refs):
    tiles = len(order)
    outs = refs[:tiles]
    vis, sky, mask, pairs, rows, sems = refs[tiles:]
    slots = pairs.shape[1]
    blocks = slots // LANES
    share = outs[0].shape[1]
    here = lax.axis_index("bl")
    ends_copy = pltpu.make_async_copy(pairs_hbm, pairs, sems.at[0])
    copies = []
    for slot, step in enumerate(order):
        channels = pl.ds(pl.multiple_of((here ^ step) * share, share), share)
        copies.append(
            [
                pltpu.make_async_copy(mask_hbm.at[channels], mask.at[slot], sems.at[1 + 3 * slot]),
                pltpu.make_async_copy(sky_hbm.at[:, channels], sky.at[slot], sems.at[2 + 3 * slot]),
                pltpu.make_async_copy(vis_hbm.at[:, channels], vis.at[slot], sems.at[3 + 3 * slot]),
            ]
        )
    ends_copy.start()
    for group in copies:
        for copy in group:
            copy.start()
    ends_copy.wait()
    for end in range(2):
        for block in range(blocks):
            row = end * blocks + block
            rows[row : row + 1, :] = pairs[end : end + 1, block * LANES : (block + 1) * LANES]
    ends = (rows[...].astype(jnp.float32) - INDEX_SHIFT).astype(jnp.bfloat16)
    live = lax.broadcasted_iota(jnp.int32, (share, slots), 1) < counts_ref[0]
    for slot in range(tiles):
        out = outs[slot]
        for copy in copies[slot]:
            copy.wait()
        weights = jnp.where(live, mask[slot], 0).astype(jnp.float32).astype(jnp.bfloat16)
        for block in range(blocks):
            lanes = slice(block * LANES, (block + 1) * LANES)
            for plane in range(8):
                out[16 * block + plane] = vis[slot, plane, :, lanes]
                out[16 * block + 8 + plane] = sky[slot, plane, :, lanes] * weights[:, lanes]
        out[16 * blocks] = ends


def pieces_of(values):
    high = values.astype(jnp.bfloat16)
    low = (values - high.astype(jnp.float32)).astype(jnp.bfloat16)
    return jnp.concatenate([high, low], axis=0)


def station_sums(first, second, table):
    rows = first.shape[0]
    both = lax.dot_general(
        pieces_of(jnp.concatenate([first, second], axis=1)),
        table,
        (((1,), (1,)), ((), ())),
        preferred_element_type=jnp.float32,
    )
    return both[:rows] + both[rows:]


def end_table(chunk_ref, table_ref):
    rows = table_ref.shape[1] // LANES
    ends = chunk_ref[chunk_ref.shape[0] - 1]
    station = lax.broadcasted_iota(jnp.int32, (STATION_COUNT, LANES), 0).astype(jnp.float32)
    station = (station - INDEX_SHIFT).astype(jnp.bfloat16)
    one = jnp.ones((), jnp.bfloat16)
    zero = jnp.zeros((), jnp.bfloat16)
    for row in range(rows):
        table_ref[:, row * LANES : (row + 1) * LANES] = jnp.where(
            station == ends[row : row + 1, :], one, zero
        )


def unit_terms(chunk_ref, products_ref):
    blocks = products_ref.shape[2] // LANES
    plane_of = lambda plane: jnp.concatenate(
        [chunk_ref[16 * block + plane].astype(jnp.float32) for block in range(blocks)], axis=1
    )
    real, imag, power = {}, {}, {}
    for p in range(2):
        for q in range(2):
            plane = 2 * p + q
            vis_real = plane_of(plane)
            vis_imag = plane_of(4 + plane)
            model_real = plane_of(8 + plane)
            model_imag = plane_of(12 + plane)
            real[p, q] = model_real * vis_real + model_imag * vis_imag
            imag[p, q] = model_real * vis_imag - model_imag * vis_real
            power[p, q] = model_real * model_real + model_imag * model_imag
            products_ref[plane] = real[p, q]
            products_ref[4 + plane] = imag[p, q]
            products_ref[8 + plane] = power[p, q]
    first = [real[p, 0] + real[p, 1] for p in range(2)]
    first += [imag[p, 0] + imag[p, 1] for p in range(2)]
    first += [power[p, 0] + power[p, 1] for p in range(2)]
    second = [real[0, q] + real[1, q] for q in range(2)]
    second += [-(imag[0, q] + imag[1, q]) for q in range(2)]
    second += [power[0, q] + power[1, q] for q in range(2)]
    return jnp.concatenate(first, 0), jnp.concatenate(second, 0)


def tile_kernel(chunk_ref, products_ref, table_ref, sums_ref):
    end_table(chunk_ref, table_ref)
    sums_ref[...] = station_sums(*unit_terms(chunk_ref, products_ref), table_ref[...])


def end_gains(gains, chunk_ref, share, blocks):
    ends = (chunk_ref[chunk_ref.shape[0] - 1].astype(jnp.float32) + INDEX_SHIFT).astype(jnp.int32)
    result = []
    for end in range(2):
        found = {row: [] for row in range(4)}
        for block in range(blocks):
            row = end * blocks + block
            index = jnp.broadcast_to(ends[row : row + 1, :], (share, LANES))
            lane = index % LANES
            group = index // LANES
            for part in range(4):
                rows = gains[part * share : (part + 1) * share]
                value = None
                for source in range(STATION_COUNT // LANES):
                    picked = jnp.take_along_axis(
                        rows[:, source * LANES : (source + 1) * LANES],
                        lane,
                        axis=1,
                        mode="promise_in_bounds",
                    )
                    value = picked if value is None else jnp.where(group == source, picked, value)
                found[part].append(value)
        result.append([jnp.concatenate(found[part], axis=1) for part in range(4)])
    return result


def gain_terms(gains, chunk_ref, products_ref):
    share = products_ref.shape[1]
    blocks = products_ref.shape[2] // LANES
    at = end_gains(gains, chunk_ref, share, blocks)
    gain = lambda part, feed, end: at[end][2 * part + feed]
    size = {
        (feed, end): gain(0, feed, end) * gain(0, feed, end)
        + gain(1, feed, end) * gain(1, feed, end)
        for feed in range(2)
        for end in range(2)
    }
    real = lambda p, q: products_ref[2 * p + q]
    imag = lambda p, q: products_ref[4 + 2 * p + q]
    power = lambda p, q: products_ref[8 + 2 * p + q]
    first = [
        sum(gain(0, q, 1) * real(p, q) - gain(1, q, 1) * imag(p, q) for q in range(2))
        for p in range(2)
    ]
    first += [
        sum(gain(0, q, 1) * imag(p, q) + gain(1, q, 1) * real(p, q) for q in range(2))
        for p in range(2)
    ]
    first += [sum(size[q, 1] * power(p, q) for q in range(2)) for p in range(2)]
    second = [
        sum(gain(0, p, 0) * real(p, q) + gain(1, p, 0) * imag(p, q) for p in range(2))
        for q in range(2)
    ]
    second += [
        sum(gain(1, p, 0) * real(p, q) - gain(0, p, 0) * imag(p, q) for p in range(2))
        for q in range(2)
    ]
    second += [sum(size[p, 0] * power(p, q) for p in range(2)) for q in range(2)]
    return jnp.concatenate(first, 0), jnp.concatenate(second, 0)


def solve_kernel(early, late, *refs):
    tiles = early + late
    chunks, refs = refs[:tiles], refs[tiles:]
    products, refs = refs[:early], refs[early:]
    tables, refs = refs[:early], refs[early:]
    sums, refs = refs[:early], refs[early:]
    outs, refs = refs[:tiles], refs[tiles:]
    late_products, refs = refs[:late], refs[late:]
    late_tables, refs = refs[:late], refs[late:]
    (solved_ref,) = refs
    share = chunks[0].shape[1]
    total = sum(part[...] for part in sums)
    for chunk_ref, products_ref, table_ref in zip(chunks[early:], late_products, late_tables):
        end_table(chunk_ref, table_ref)
        total = total + station_sums(*unit_terms(chunk_ref, products_ref), table_ref[...])
    rows = 2 * share
    divisor = total[2 * rows :] + damping
    gains = jnp.concatenate([(total[:rows] + damping) / divisor, total[rows : 2 * rows] / divisor])
    total = 0.0
    for chunk_ref, products_ref, table_ref in zip(
        chunks, products + late_products, tables + late_tables
    ):
        total = total + station_sums(
            *gain_terms(gains, chunk_ref, products_ref), table_ref[...]
        )
    divisor = total[2 * rows :] + damping
    renewed = (total[: 2 * rows] + damping * gains) / jnp.concatenate([divisor, divisor])
    solved_ref[...] = 0.5 * (renewed + gains)
    owned = STATION_COUNT // tiles
    here = lax.axis_index("bl")
    for step in range(tiles):
        start = pl.multiple_of((here ^ step) * owned, owned)
        outs[step][...] = solved_ref[:, pl.ds(start, owned)]


def moment_kernel(basis_ref, *refs):
    pieces, moments_ref = refs[:-1], refs[-1]
    share = pieces[0].shape[0] // 4
    here = lax.axis_index("bl")
    columns = []
    for step in range(len(pieces)):
        start = pl.multiple_of((here ^ step) * share, share)
        columns.append(basis_ref[pl.ds(start, share), :])
    for degree in range(4):
        for part in range(4):
            terms = sum(
                piece[part * share : (part + 1) * share, :] * column[:, degree : degree + 1]
                for piece, column in zip(pieces, columns)
            )
            row = 4 * degree + part
            moments_ref[row : row + 1, :] = jnp.sum(terms, axis=0, keepdims=True)


def order_kernel(*refs):
    pieces, solved_ref = refs[:-1], refs[-1]
    share = pieces[0].shape[0] // 4
    here = lax.axis_index("bl")
    for step, piece in enumerate(pieces):
        start = pl.multiple_of((here ^ step) * share, share)
        for part in range(4):
            solved_ref[part, pl.ds(start, share), :] = piece[part * share : (part + 1) * share, :]


def fit_kernel(basis_ref, *refs):
    total = refs[0][...]
    for part in refs[1:-1]:
        total = total + part[...]
    fitted_ref = refs[-1]
    for part in range(4):
        fitted_ref[part] = sum(
            basis_ref[:, degree : degree + 1] * total[4 * degree + part : 4 * degree + part + 1, :]
            for degree in range(4)
        )


def vmem_call(kernel, outs, scratch=(), spaces=None, **options):
    def call(*args):
        return pl.pallas_call(
            kernel,
            out_shape=outs,
            in_specs=[
                pl.BlockSpec(memory_space=space) for space in spaces or [pltpu.VMEM] * len(args)
            ],
            out_specs=jax.tree.map(lambda _: pl.BlockSpec(memory_space=pltpu.VMEM), outs),
            scratch_shapes=list(scratch),
            compiler_params=pltpu.CompilerParams(vmem_limit_bytes=24 << 20),
            **options,
        )(*args)

    return call


def in_hbm(value):
    return pltpu.with_memory_space_constraint(value, pltpu.HBM)


def partners(count, step):
    return [(index, index ^ step) for index in range(count)]


def local_resplit(visibilities, sky_model, antenna_pairs, tile_counts, usable_mask):
    channel_local = visibilities.shape[1]
    slots = visibilities.shape[2]
    tiles = lax.axis_size("bl")
    groups = lax.axis_size("ch")
    share = channel_local // tiles
    owned = STATION_COUNT // tiles
    f32 = jnp.float32
    shape = jax.ShapeDtypeStruct

    steps = list(range(1, tiles))
    order = sorted(steps, key=lambda step: step == 1)
    blocks = slots // LANES
    chunk_shape = shape((16 * blocks + 1, share, LANES), jnp.bfloat16)
    packed = vmem_call(
        functools.partial(pack_kernel, order + [0]),
        (chunk_shape,) * tiles,
        scratch=[
            pltpu.VMEM((tiles, 8, share, slots), jnp.bfloat16),
            pltpu.VMEM((tiles, 8, share, slots), jnp.bfloat16),
            pltpu.VMEM((tiles, share, slots), jnp.int32),
            pltpu.VMEM((2, slots), jnp.int32),
            pltpu.VMEM((2 * blocks, LANES), jnp.int32),
            pltpu.SemaphoreType.DMA((1 + 3 * tiles,)),
        ],
        spaces=[pltpu.SMEM] + [pltpu.HBM] * 4,
    )(tile_counts, *[in_hbm(x) for x in (visibilities, sky_model, antenna_pairs, usable_mask)])
    chunks = {0: packed[-1]}
    for step, piece in zip(order, packed):
        chunks[step] = lax.ppermute(piece, "bl", partners(tiles, step))

    tile_outs = (
        shape((12, share, slots), f32),
        shape((STATION_COUNT, 2 * slots), jnp.bfloat16),
        shape((6 * share, STATION_COUNT), f32),
    )
    cost = pl.CostEstimate(
        flops=24 * share * slots * STATION_COUNT, bytes_accessed=4 << 20, transcendentals=0
    )
    early, late = [0, 1], [step for step in order if step > 1]
    done = [vmem_call(tile_kernel, tile_outs, cost_estimate=cost)(chunks[k]) for k in early]
    pieces = vmem_call(
        functools.partial(solve_kernel, len(early), len(late)),
        tuple(shape((4 * share, owned), f32) for _ in range(tiles)),
        scratch=[
            *[pltpu.VMEM((12, share, slots), f32) for _ in late],
            *[pltpu.VMEM((STATION_COUNT, 2 * slots), jnp.bfloat16) for _ in late],
            pltpu.VMEM((4 * share, STATION_COUNT), f32),
        ],
    )(
        *[chunks[step] for step in early + late],
        *[part[0] for part in done],
        *[part[1] for part in done],
        *[part[2] for part in done],
    )
    received = {0: pieces[0]}
    for step in steps:
        received[step] = lax.ppermute(pieces[step], "bl", partners(tiles, step))
    received = [received[step] for step in range(tiles)]
    basis = lax.dynamic_slice_in_dim(
        jnp.asarray(poly_basis(channel_local * groups).T),
        lax.axis_index("ch") * channel_local,
        channel_local,
        0,
    )
    moments = vmem_call(moment_kernel, shape((16, owned), f32))(basis, *received)
    solved = vmem_call(order_kernel, shape((4, channel_local, owned), f32))(*received)
    moment_parts = [moments]
    for step in range(1, groups):
        moment_parts.append(lax.ppermute(moments, "ch", partners(groups, step)))
    fitted = vmem_call(fit_kernel, shape((4, channel_local, owned), f32))(basis, *moment_parts)
    out_shape = (2, 2, channel_local, owned)
    return solved.reshape(out_shape), fitted.reshape(out_shape)


def local(visibilities, sky_model, antenna_pairs, tile_counts, usable_mask):
    tiles = lax.axis_size("bl")
    groups = lax.axis_size("ch")
    power_of_two = lambda count: count & (count - 1) == 0
    resplit = (
        power_of_two(tiles)
        and power_of_two(groups)
        and 1 < tiles <= 4
        and groups <= 8
        and visibilities.shape[1] == 8 * tiles
        and STATION_COUNT % (128 * tiles) == 0
        and STATION_COUNT <= 2 * INDEX_SHIFT
        and visibilities.shape[2] == 4 * LANES
    )
    body = local_resplit if resplit else local_general
    return body(visibilities, sky_model, antenna_pairs, tile_counts, usable_mask)


def solution(mesh):
    return jax.shard_map(
        local,
        mesh=mesh,
        in_specs=(
            P(None, "ch", ("grp", "bl")),
            P(None, "ch", ("grp", "bl")),
            P(None, ("grp", "bl")),
            P(("grp", "bl")),
            P("ch", ("grp", "bl")),
        ),
        out_specs=(P(None, None, "ch", ("grp", "bl")), P(None, None, "ch", ("grp", "bl"))),
        check_vma=False,
    )
```

```python
import functools

import jax
import jax.numpy as jnp
import numpy as np
from jax import lax
from jax.experimental import pallas as pl
from jax.experimental.pallas import tpu as pltpu
from jax.sharding import PartitionSpec as P


STATION_COUNT = 512
SWEEPS = 2

damping = 4.0
highest = lax.Precision.HIGHEST


def poly_basis(channel_total):
    nodes = (2.0 * np.arange(channel_total, dtype=np.float64) - (channel_total - 1)) / (
        channel_total - 1
    )
    rows = []
    for degree in range(4):
        vector = nodes**degree
        for earlier in rows:
            vector = vector - np.sum(vector * earlier) * earlier
        rows.append(vector / np.sqrt(np.sum(vector * vector)))
    return np.stack(rows).astype(np.float32)


def split_parts(data):
    planes = data.astype(jnp.float32)
    shape_rest = planes.shape[1:]
    return (planes[:4].reshape((2, 2) + shape_rest), planes[4:].reshape((2, 2) + shape_rest))


def contributions(
    model_real_part, model_imaginary, vis_real, vis_imag, first_gain, second_gain, weights
):
    second_real = second_gain[0][None]
    second_imag = second_gain[1][None]
    left_real = model_real_part * second_real + model_imaginary * second_imag
    left_imag = model_imaginary * second_real - model_real_part * second_imag
    first_num_real = jnp.sum(left_real * vis_real + left_imag * vis_imag, axis=1) * weights
    first_num_imag = jnp.sum(left_real * vis_imag - left_imag * vis_real, axis=1) * weights
    first_den = jnp.sum(left_real * left_real + left_imag * left_imag, axis=1) * weights
    first_real = first_gain[0][:, None]
    first_imag = first_gain[1][:, None]
    right_real = model_real_part * first_real - model_imaginary * first_imag
    right_imag = model_real_part * first_imag + model_imaginary * first_real
    second_num_real = jnp.sum(right_real * vis_real + right_imag * vis_imag, axis=0) * weights
    second_num_imag = jnp.sum(right_imag * vis_real - right_real * vis_imag, axis=0) * weights
    second_den = jnp.sum(right_real * right_real + right_imag * right_imag, axis=0) * weights
    return (
        jnp.stack([first_num_real, first_num_imag, first_den]),
        jnp.stack([second_num_real, second_num_imag, second_den]),
    )


def refresh(station_sums, previous):
    divisor = station_sums[2] + damping
    return jnp.stack(
        [
            (station_sums[0] + damping * previous[0]) / divisor,
            (station_sums[1] + damping * previous[1]) / divisor,
        ]
    )


def station_totals(end_first, end_second, first_endpoints, second_ends):
    total_slots = end_first.shape[3]
    flat_first = end_first.reshape(-1, total_slots)
    flat_second = end_second.reshape(-1, total_slots)
    station_index = jnp.arange(STATION_COUNT, dtype=jnp.int32)
    table_first = (first_endpoints[:, None] == station_index[None, :]).astype(jnp.float32)
    table_second = (second_ends[:, None] == station_index[None, :]).astype(jnp.float32)
    summed = jnp.dot(
        flat_first, table_first, precision=highest, preferred_element_type=jnp.float32
    ) + jnp.dot(flat_second, table_second, precision=highest, preferred_element_type=jnp.float32)
    return summed.reshape(end_first.shape[:3] + (STATION_COUNT,))


def local_general(visibilities, sky_model, antenna_pairs, tile_counts, usable_mask):
    vis_real, vis_imag = split_parts(visibilities)
    model_real_part, model_imaginary = split_parts(sky_model)
    channel_local = visibilities.shape[1]
    tile_rows = visibilities.shape[2]
    owned_count = STATION_COUNT // lax.axis_size("bl")
    owner_start = lax.axis_index("bl") * owned_count
    live_slots = jnp.arange(tile_rows, dtype=jnp.int32) < tile_counts[0]
    weights = usable_mask.astype(jnp.float32) * live_slots.astype(jnp.float32)[None, :]
    channel_total = channel_local * lax.axis_size("ch")
    poly_rows = lax.dynamic_slice_in_dim(
        jnp.asarray(poly_basis(channel_total)),
        lax.axis_index("ch") * channel_local,
        channel_local,
        1,
    )
    gain_state = jnp.stack(
        [
            jnp.ones((2, channel_local, STATION_COUNT), jnp.float32),
            jnp.zeros((2, channel_local, STATION_COUNT), jnp.float32),
        ]
    )
    solved = gain_state
    for iteration in range(SWEEPS):
        first_gain = jnp.take(gain_state, antenna_pairs[0], axis=3)
        second_gain = jnp.take(gain_state, antenna_pairs[1], axis=3)
        end_first, end_second = contributions(
            model_real_part, model_imaginary, vis_real, vis_imag, first_gain, second_gain, weights
        )
        partial_sums = station_totals(end_first, end_second, antenna_pairs[0], antenna_pairs[1])
        station_sums = lax.psum_scatter(partial_sums, "bl", scatter_dimension=3, tiled=True)
        previous = lax.dynamic_slice_in_dim(gain_state, owner_start, owned_count, 3)
        renewed = refresh(station_sums, previous)
        if iteration == 1:
            renewed = 0.5 * (renewed + previous)
        solved = renewed
        if iteration < SWEEPS - 1:
            gain_state = lax.all_gather(renewed, "bl", axis=3, tiled=True)
    local_moments = jnp.einsum("kc,rfca->krfa", poly_rows, solved, precision=highest)
    moments = lax.psum(local_moments, "ch")
    fitted = jnp.einsum("kc,krfa->rfca", poly_rows, moments, precision=highest)
    return (solved, fitted)


LANES = 128
INDEX_SHIFT = 256.0


def chunk_copies(step, vis_hbm, sky_hbm, mask_hbm, out, sky, mask, sems):
    share, slots = mask.shape
    blocks = slots // LANES
    channels = pl.ds(pl.multiple_of((lax.axis_index("bl") ^ step) * share, share), share)
    copies = [
        pltpu.make_async_copy(mask_hbm.at[channels], mask, sems.at[0]),
        pltpu.make_async_copy(sky_hbm.at[:, channels], sky, sems.at[1]),
    ]
    for block in range(blocks):
        copies.append(
            pltpu.make_async_copy(
                vis_hbm.at[:, channels, pl.ds(block * LANES, LANES)],
                out.at[pl.ds(8 * block, 8)],
                sems.at[2 + block],
            )
        )
    for copy in copies:
        copy.start()
    return copies


def mask_model(out, sky, mask):
    blocks = mask.shape[1] // LANES
    weights = mask[...].astype(jnp.float32).astype(jnp.bfloat16)
    for block in range(blocks):
        lanes = slice(block * LANES, (block + 1) * LANES)
        for plane in range(8):
            out[8 * (blocks + block) + plane] = sky[plane, :, lanes] * weights[:, lanes]


def first_kernel(step, vis_hbm, sky_hbm, mask_hbm, out, sky, mask, sems):
    copies = chunk_copies(step, vis_hbm, sky_hbm, mask_hbm, out, sky, mask, sems)
    for copy in copies[:2]:
        copy.wait()
    mask_model(out, sky, mask)
    for copy in copies[2:]:
        copy.wait()


def pack_kernel(steps, counts_ref, vis_hbm, sky_hbm, mask_hbm, pairs_hbm, *refs):
    outs, ends_out = refs[: len(steps)], refs[len(steps)]
    sky, mask, pairs, rows, pairs_sem, sems = refs[len(steps) + 1 :]
    blocks = pairs.shape[1] // LANES
    pairs_copy = pltpu.make_async_copy(pairs_hbm, pairs, pairs_sem)
    pairs_copy.start()
    copies = [
        chunk_copies(
            step, vis_hbm, sky_hbm, mask_hbm, outs[slot], sky.at[slot], mask.at[slot], sems.at[slot]
        )
        for slot, step in enumerate(steps)
    ]
    pairs_copy.wait()
    lane = lax.broadcasted_iota(jnp.int32, (1, LANES), 1)
    for end in range(2):
        for block in range(blocks):
            row = end * blocks + block
            station = pairs[end : end + 1, block * LANES : (block + 1) * LANES]
            live = lane + block * LANES < counts_ref[0]
            rows[row : row + 1, :] = jnp.where(live, station, STATION_COUNT)
    ends = (rows[...].astype(jnp.float32) - INDEX_SHIFT).astype(jnp.bfloat16)
    ends_out[0] = ends
    for slot in range(len(steps)):
        outs[slot][16 * blocks] = ends
        for copy in copies[slot][:2]:
            copy.wait()
        mask_model(outs[slot], sky.at[slot], mask.at[slot])
    for group in copies:
        for copy in group[2:]:
            copy.wait()


def pieces_of(values):
    high = values.astype(jnp.bfloat16)
    low = (values - high.astype(jnp.float32)).astype(jnp.bfloat16)
    return jnp.concatenate([high, low], axis=0)


def station_sums(first, second, table):
    rows = first.shape[0]
    both = lax.dot_general(
        pieces_of(jnp.concatenate([first, second], axis=1)),
        table,
        (((1,), (1,)), ((), ())),
        preferred_element_type=jnp.float32,
    )
    return both[:rows] + both[rows:]


def end_table(ends_ref, table_ref):
    ends = ends_ref[ends_ref.shape[0] - 1]
    station = lax.broadcasted_iota(jnp.int32, (STATION_COUNT, LANES), 0).astype(jnp.float32)
    station = (station - INDEX_SHIFT).astype(jnp.bfloat16)
    one = jnp.ones((), jnp.bfloat16)
    zero = jnp.zeros((), jnp.bfloat16)
    for row in range(table_ref.shape[1] // LANES):
        table_ref[:, row * LANES : (row + 1) * LANES] = jnp.where(
            station == ends[row : row + 1, :], one, zero
        )


def unit_terms(chunk_ref, products_ref):
    blocks = products_ref.shape[2] // LANES
    plane_of = lambda base, plane: jnp.concatenate(
        [
            chunk_ref[8 * (base * blocks + block) + plane].astype(jnp.float32)
            for block in range(blocks)
        ],
        axis=1,
    )
    real, imag, power = {}, {}, {}
    for p in range(2):
        for q in range(2):
            plane = 2 * p + q
            vis_real = plane_of(0, plane)
            vis_imag = plane_of(0, 4 + plane)
            model_real = plane_of(1, plane)
            model_imag = plane_of(1, 4 + plane)
            real[p, q] = model_real * vis_real + model_imag * vis_imag
            imag[p, q] = model_real * vis_imag - model_imag * vis_real
            power[p, q] = model_real * model_real + model_imag * model_imag
            products_ref[plane] = real[p, q]
            products_ref[4 + plane] = imag[p, q]
            products_ref[8 + plane] = power[p, q]
    first = [real[p, 0] + real[p, 1] for p in range(2)]
    first += [imag[p, 0] + imag[p, 1] for p in range(2)]
    first += [power[p, 0] + power[p, 1] for p in range(2)]
    second = [real[0, q] + real[1, q] for q in range(2)]
    second += [-(imag[0, q] + imag[1, q]) for q in range(2)]
    second += [power[0, q] + power[1, q] for q in range(2)]
    return jnp.concatenate(first, 0), jnp.concatenate(second, 0)


def tile_kernel(chunk_ref, ends_ref, products_ref, table_ref, sums_ref):
    end_table(ends_ref, table_ref)
    sums_ref[...] = station_sums(*unit_terms(chunk_ref, products_ref), table_ref[...])


def end_gains(gains, ends_ref, share, blocks):
    ends = (ends_ref[ends_ref.shape[0] - 1].astype(jnp.float32) + INDEX_SHIFT).astype(jnp.int32)
    result = []
    for end in range(2):
        found = {row: [] for row in range(4)}
        for block in range(blocks):
            row = end * blocks + block
            index = jnp.broadcast_to(ends[row : row + 1, :], (share, LANES))
            lane = index % LANES
            group = index // LANES
            for part in range(4):
                rows = gains[part * share : (part + 1) * share]
                value = None
                for source in range(STATION_COUNT // LANES):
                    picked = jnp.take_along_axis(
                        rows[:, source * LANES : (source + 1) * LANES],
                        lane,
                        axis=1,
                        mode="promise_in_bounds",
                    )
                    value = picked if value is None else jnp.where(group == source, picked, value)
                found[part].append(value)
        result.append([jnp.concatenate(found[part], axis=1) for part in range(4)])
    return result


def gain_terms(gains, ends_ref, products_ref):
    share = products_ref.shape[1]
    blocks = products_ref.shape[2] // LANES
    at = end_gains(gains, ends_ref, share, blocks)
    gain = lambda part, feed, end: at[end][2 * part + feed]
    size = {
        (feed, end): gain(0, feed, end) * gain(0, feed, end)
        + gain(1, feed, end) * gain(1, feed, end)
        for feed in range(2)
        for end in range(2)
    }
    real = lambda p, q: products_ref[2 * p + q]
    imag = lambda p, q: products_ref[4 + 2 * p + q]
    power = lambda p, q: products_ref[8 + 2 * p + q]
    first = [
        sum(gain(0, q, 1) * real(p, q) - gain(1, q, 1) * imag(p, q) for q in range(2))
        for p in range(2)
    ]
    first += [
        sum(gain(0, q, 1) * imag(p, q) + gain(1, q, 1) * real(p, q) for q in range(2))
        for p in range(2)
    ]
    first += [sum(size[q, 1] * power(p, q) for q in range(2)) for p in range(2)]
    second = [
        sum(gain(0, p, 0) * real(p, q) + gain(1, p, 0) * imag(p, q) for p in range(2))
        for q in range(2)
    ]
    second += [
        sum(gain(1, p, 0) * real(p, q) - gain(0, p, 0) * imag(p, q) for p in range(2))
        for q in range(2)
    ]
    second += [sum(size[p, 0] * power(p, q) for p in range(2)) for q in range(2)]
    return jnp.concatenate(first, 0), jnp.concatenate(second, 0)


def solve_kernel(early, late, *refs):
    tiles = early + late
    chunks, refs = refs[:late], refs[late:]
    ends, refs = refs[:tiles], refs[tiles:]
    products, refs = refs[:early], refs[early:]
    tables, refs = refs[:early], refs[early:]
    sums, refs = refs[:early], refs[early:]
    outs, refs = refs[:tiles], refs[tiles:]
    late_products, refs = refs[:late], refs[late:]
    late_tables, refs = refs[:late], refs[late:]
    (solved_ref,) = refs
    share = products[0].shape[1]
    total = sum(part[...] for part in sums)
    for chunk_ref, ends_ref, products_ref, table_ref in zip(
        chunks, ends[early:], late_products, late_tables
    ):
        end_table(ends_ref, table_ref)
        total = total + station_sums(*unit_terms(chunk_ref, products_ref), table_ref[...])
    rows = 2 * share
    divisor = total[2 * rows :] + damping
    gains = jnp.concatenate([(total[:rows] + damping) / divisor, total[rows : 2 * rows] / divisor])
    total = 0.0
    for ends_ref, products_ref, table_ref in zip(
        ends, products + late_products, tables + late_tables
    ):
        total = total + station_sums(*gain_terms(gains, ends_ref, products_ref), table_ref[...])
    divisor = total[2 * rows :] + damping
    renewed = (total[: 2 * rows] + damping * gains) / jnp.concatenate([divisor, divisor])
    solved_ref[...] = 0.5 * (renewed + gains)
    owned = STATION_COUNT // tiles
    here = lax.axis_index("bl")
    for step in range(tiles):
        start = pl.multiple_of((here ^ step) * owned, owned)
        outs[step][...] = solved_ref[:, pl.ds(start, owned)]


def moment_kernel(basis_ref, *refs):
    pieces, moments_ref = refs[:-1], refs[-1]
    share = pieces[0].shape[0] // 4
    here = lax.axis_index("bl")
    columns = []
    for step in range(len(pieces)):
        start = pl.multiple_of((here ^ step) * share, share)
        columns.append(basis_ref[pl.ds(start, share), :])
    for degree in range(4):
        for part in range(4):
            terms = sum(
                piece[part * share : (part + 1) * share, :] * column[:, degree : degree + 1]
                for piece, column in zip(pieces, columns)
            )
            row = 4 * degree + part
            moments_ref[row : row + 1, :] = jnp.sum(terms, axis=0, keepdims=True)


def order_kernel(*refs):
    pieces, solved_ref = refs[:-1], refs[-1]
    share = pieces[0].shape[0] // 4
    here = lax.axis_index("bl")
    for step, piece in enumerate(pieces):
        start = pl.multiple_of((here ^ step) * share, share)
        for part in range(4):
            solved_ref[part, pl.ds(start, share), :] = piece[part * share : (part + 1) * share, :]


def fit_kernel(basis_ref, *refs):
    total = refs[0][...]
    for part in refs[1:-1]:
        total = total + part[...]
    fitted_ref = refs[-1]
    for part in range(4):
        fitted_ref[part] = sum(
            basis_ref[:, degree : degree + 1] * total[4 * degree + part : 4 * degree + part + 1, :]
            for degree in range(4)
        )


def vmem_call(kernel, outs, scratch=(), spaces=None, **options):
    def call(*args):
        return pl.pallas_call(
            kernel,
            out_shape=outs,
            in_specs=[
                pl.BlockSpec(memory_space=space) for space in spaces or [pltpu.VMEM] * len(args)
            ],
            out_specs=jax.tree.map(lambda _: pl.BlockSpec(memory_space=pltpu.VMEM), outs),
            scratch_shapes=list(scratch),
            compiler_params=pltpu.CompilerParams(vmem_limit_bytes=24 << 20),
            **options,
        )(*args)

    return call


def in_hbm(value):
    return pltpu.with_memory_space_constraint(value, pltpu.HBM)


def partners(count, step):
    return [(index, index ^ step) for index in range(count)]


def local_resplit(visibilities, sky_model, antenna_pairs, tile_counts, usable_mask):
    channel_local = visibilities.shape[1]
    slots = visibilities.shape[2]
    tiles = lax.axis_size("bl")
    groups = lax.axis_size("ch")
    share = channel_local // tiles
    owned = STATION_COUNT // tiles
    f32 = jnp.float32
    shape = jax.ShapeDtypeStruct

    steps = list(range(1, tiles))
    first = FIRST
    others = [step for step in steps if step != first] + [0]
    blocks = slots // LANES
    bf16 = jnp.bfloat16
    (lead,) = vmem_call(
        functools.partial(first_kernel, first),
        (shape((16 * blocks, share, LANES), bf16),),
        scratch=[
            pltpu.VMEM((8, share, slots), bf16),
            pltpu.VMEM((share, slots), jnp.int32),
            pltpu.SemaphoreType.DMA((2 + blocks,)),
        ],
        spaces=[pltpu.HBM] * 3,
    )(in_hbm(visibilities), in_hbm(sky_model), in_hbm(usable_mask))
    tile_counts, lead = lax.optimization_barrier((tile_counts, lead))
    *packed, own_ends = vmem_call(
        functools.partial(pack_kernel, others),
        (shape((16 * blocks + 1, share, LANES), bf16),) * len(others)
        + (shape((1, 2 * blocks, LANES), bf16),),
        scratch=[
            pltpu.VMEM((len(others), 8, share, slots), bf16),
            pltpu.VMEM((len(others), share, slots), jnp.int32),
            pltpu.VMEM((2, slots), jnp.int32),
            pltpu.VMEM((2 * blocks, LANES), jnp.int32),
            pltpu.SemaphoreType.DMA,
            pltpu.SemaphoreType.DMA((len(others), 2 + blocks)),
        ],
        spaces=[pltpu.SMEM] + [pltpu.HBM] * 4,
    )(
        tile_counts,
        in_hbm(visibilities),
        in_hbm(sky_model),
        in_hbm(usable_mask),
        in_hbm(antenna_pairs),
    )

    def exchange(piece, step):
        return lax.ppermute(piece, "bl", partners(tiles, step))

    chunks = {0: packed[-1], first: exchange(lead, first)}
    for piece, step in zip(packed[:-1], others):
        chunks[step] = exchange(piece, step)
    ends = dict(chunks)
    ends[first] = exchange(own_ends, first)

    products_shape = shape((12, share, slots), f32)
    table_shape = shape((STATION_COUNT, 2 * slots), bf16)
    sums_shape = shape((6 * share, STATION_COUNT), f32)
    tile_outs = (products_shape, table_shape, sums_shape)
    late = [steps[-1]]
    done = {
        step: vmem_call(tile_kernel, tile_outs)(chunks[step], ends[step])
        for step in range(tiles)
        if step not in late
    }
    pieces = vmem_call(
        functools.partial(solve_kernel, len(done), len(late)),
        tuple(shape((4 * share, owned), f32) for _ in range(tiles)),
        scratch=[
            *[pltpu.VMEM((12, share, slots), f32) for _ in late],
            *[pltpu.VMEM((STATION_COUNT, 2 * slots), bf16) for _ in late],
            pltpu.VMEM((4 * share, STATION_COUNT), f32),
        ],
    )(
        *[chunks[step] for step in late],
        *[ends[step] for step in list(done) + late],
        *[parts[0] for parts in done.values()],
        *[parts[1] for parts in done.values()],
        *[parts[2] for parts in done.values()],
    )
    received = {0: pieces[0]}
    for step in steps:
        received[step] = lax.ppermute(pieces[step], "bl", partners(tiles, step))
    received = [received[step] for step in range(tiles)]
    basis = lax.dynamic_slice_in_dim(
        jnp.asarray(poly_basis(channel_local * groups).T),
        lax.axis_index("ch") * channel_local,
        channel_local,
        0,
    )
    moments = vmem_call(moment_kernel, shape((16, owned), f32))(basis, *received)
    solved = vmem_call(order_kernel, shape((4, channel_local, owned), f32))(*received)
    moment_parts = [moments]
    for step in range(1, groups):
        moment_parts.append(lax.ppermute(moments, "ch", partners(groups, step)))
    fitted = vmem_call(fit_kernel, shape((4, channel_local, owned), f32))(basis, *moment_parts)
    out_shape = (2, 2, channel_local, owned)
    return solved.reshape(out_shape), fitted.reshape(out_shape)


FIRST = 2


def local(visibilities, sky_model, antenna_pairs, tile_counts, usable_mask):
    tiles = lax.axis_size("bl")
    groups = lax.axis_size("ch")
    power_of_two = lambda count: count & (count - 1) == 0
    resplit = (
        power_of_two(tiles)
        and power_of_two(groups)
        and 1 < tiles <= 4
        and groups <= 8
        and visibilities.shape[1] == 8 * tiles
        and STATION_COUNT % (128 * tiles) == 0
        and STATION_COUNT <= 2 * INDEX_SHIFT
        and visibilities.shape[2] == 4 * LANES
    )
    body = local_resplit if resplit else local_general
    return body(visibilities, sky_model, antenna_pairs, tile_counts, usable_mask)


def solution(mesh):
    return jax.shard_map(
        local,
        mesh=mesh,
        in_specs=(
            P(None, "ch", ("grp", "bl")),
            P(None, "ch", ("grp", "bl")),
            P(None, ("grp", "bl")),
            P(("grp", "bl")),
            P("ch", ("grp", "bl")),
        ),
        out_specs=(P(None, None, "ch", ("grp", "bl")), P(None, None, "ch", ("grp", "bl"))),
        check_vma=False,
    )
```

```python
import functools

import jax
import jax.numpy as jnp
import numpy as np
from jax import lax
from jax.experimental import pallas as pl
from jax.experimental.pallas import tpu as pltpu
from jax.sharding import PartitionSpec as P


STATION_COUNT = 512
SWEEPS = 2

damping = 4.0
highest = lax.Precision.HIGHEST


def poly_basis(channel_total):
    nodes = (2.0 * np.arange(channel_total, dtype=np.float64) - (channel_total - 1)) / (
        channel_total - 1
    )
    rows = []
    for degree in range(4):
        vector = nodes**degree
        for earlier in rows:
            vector = vector - np.sum(vector * earlier) * earlier
        rows.append(vector / np.sqrt(np.sum(vector * vector)))
    return np.stack(rows).astype(np.float32)


def split_parts(data):
    planes = data.astype(jnp.float32)
    shape_rest = planes.shape[1:]
    return (planes[:4].reshape((2, 2) + shape_rest), planes[4:].reshape((2, 2) + shape_rest))


def contributions(
    model_real_part, model_imaginary, vis_real, vis_imag, first_gain, second_gain, weights
):
    second_real = second_gain[0][None]
    second_imag = second_gain[1][None]
    left_real = model_real_part * second_real + model_imaginary * second_imag
    left_imag = model_imaginary * second_real - model_real_part * second_imag
    first_num_real = jnp.sum(left_real * vis_real + left_imag * vis_imag, axis=1) * weights
    first_num_imag = jnp.sum(left_real * vis_imag - left_imag * vis_real, axis=1) * weights
    first_den = jnp.sum(left_real * left_real + left_imag * left_imag, axis=1) * weights
    first_real = first_gain[0][:, None]
    first_imag = first_gain[1][:, None]
    right_real = model_real_part * first_real - model_imaginary * first_imag
    right_imag = model_real_part * first_imag + model_imaginary * first_real
    second_num_real = jnp.sum(right_real * vis_real + right_imag * vis_imag, axis=0) * weights
    second_num_imag = jnp.sum(right_imag * vis_real - right_real * vis_imag, axis=0) * weights
    second_den = jnp.sum(right_real * right_real + right_imag * right_imag, axis=0) * weights
    return (
        jnp.stack([first_num_real, first_num_imag, first_den]),
        jnp.stack([second_num_real, second_num_imag, second_den]),
    )


def refresh(station_sums, previous):
    divisor = station_sums[2] + damping
    return jnp.stack(
        [
            (station_sums[0] + damping * previous[0]) / divisor,
            (station_sums[1] + damping * previous[1]) / divisor,
        ]
    )


def station_totals(end_first, end_second, first_endpoints, second_ends):
    total_slots = end_first.shape[3]
    flat_first = end_first.reshape(-1, total_slots)
    flat_second = end_second.reshape(-1, total_slots)
    station_index = jnp.arange(STATION_COUNT, dtype=jnp.int32)
    table_first = (first_endpoints[:, None] == station_index[None, :]).astype(jnp.float32)
    table_second = (second_ends[:, None] == station_index[None, :]).astype(jnp.float32)
    summed = jnp.dot(
        flat_first, table_first, precision=highest, preferred_element_type=jnp.float32
    ) + jnp.dot(flat_second, table_second, precision=highest, preferred_element_type=jnp.float32)
    return summed.reshape(end_first.shape[:3] + (STATION_COUNT,))


def local_general(visibilities, sky_model, antenna_pairs, tile_counts, usable_mask):
    vis_real, vis_imag = split_parts(visibilities)
    model_real_part, model_imaginary = split_parts(sky_model)
    channel_local = visibilities.shape[1]
    tile_rows = visibilities.shape[2]
    owned_count = STATION_COUNT // lax.axis_size("bl")
    owner_start = lax.axis_index("bl") * owned_count
    live_slots = jnp.arange(tile_rows, dtype=jnp.int32) < tile_counts[0]
    weights = usable_mask.astype(jnp.float32) * live_slots.astype(jnp.float32)[None, :]
    channel_total = channel_local * lax.axis_size("ch")
    poly_rows = lax.dynamic_slice_in_dim(
        jnp.asarray(poly_basis(channel_total)),
        lax.axis_index("ch") * channel_local,
        channel_local,
        1,
    )
    gain_state = jnp.stack(
        [
            jnp.ones((2, channel_local, STATION_COUNT), jnp.float32),
            jnp.zeros((2, channel_local, STATION_COUNT), jnp.float32),
        ]
    )
    solved = gain_state
    for iteration in range(SWEEPS):
        first_gain = jnp.take(gain_state, antenna_pairs[0], axis=3)
        second_gain = jnp.take(gain_state, antenna_pairs[1], axis=3)
        end_first, end_second = contributions(
            model_real_part, model_imaginary, vis_real, vis_imag, first_gain, second_gain, weights
        )
        partial_sums = station_totals(end_first, end_second, antenna_pairs[0], antenna_pairs[1])
        station_sums = lax.psum_scatter(partial_sums, "bl", scatter_dimension=3, tiled=True)
        previous = lax.dynamic_slice_in_dim(gain_state, owner_start, owned_count, 3)
        renewed = refresh(station_sums, previous)
        if iteration == 1:
            renewed = 0.5 * (renewed + previous)
        solved = renewed
        if iteration < SWEEPS - 1:
            gain_state = lax.all_gather(renewed, "bl", axis=3, tiled=True)
    local_moments = jnp.einsum("kc,rfca->krfa", poly_rows, solved, precision=highest)
    moments = lax.psum(local_moments, "ch")
    fitted = jnp.einsum("kc,krfa->rfca", poly_rows, moments, precision=highest)
    return (solved, fitted)


LANES = 128
INDEX_SHIFT = 256.0


def chunk_copies(step, vis_hbm, sky_hbm, mask_hbm, out, sky, mask, sems):
    share, slots = mask.shape
    blocks = slots // LANES
    channels = pl.ds(pl.multiple_of((lax.axis_index("bl") ^ step) * share, share), share)
    copies = [
        pltpu.make_async_copy(mask_hbm.at[channels], mask, sems.at[0]),
        pltpu.make_async_copy(sky_hbm.at[:, channels], sky, sems.at[1]),
    ]
    for block in range(blocks):
        copies.append(
            pltpu.make_async_copy(
                vis_hbm.at[:, channels, pl.ds(block * LANES, LANES)],
                out.at[pl.ds(8 * block, 8)],
                sems.at[2 + block],
            )
        )
    for copy in copies:
        copy.start()
    return copies


def mask_model(out, sky, mask):
    blocks = mask.shape[1] // LANES
    weights = mask[...].astype(jnp.float32).astype(jnp.bfloat16)
    for block in range(blocks):
        lanes = slice(block * LANES, (block + 1) * LANES)
        for plane in range(8):
            out[8 * (blocks + block) + plane] = sky[plane, :, lanes] * weights[:, lanes]


def first_kernel(step, vis_hbm, sky_hbm, mask_hbm, out, sky, mask, sems):
    copies = chunk_copies(step, vis_hbm, sky_hbm, mask_hbm, out, sky, mask, sems)
    for copy in copies[:2]:
        copy.wait()
    mask_model(out, sky, mask)
    for copy in copies[2:]:
        copy.wait()


def pack_kernel(steps, counts_ref, vis_hbm, sky_hbm, mask_hbm, pairs_hbm, *refs):
    outs, ends_out = refs[: len(steps)], refs[len(steps)]
    sky, mask, pairs, rows, pairs_sem, sems = refs[len(steps) + 1 :]
    blocks = pairs.shape[1] // LANES
    pairs_copy = pltpu.make_async_copy(pairs_hbm, pairs, pairs_sem)
    pairs_copy.start()
    copies = [
        chunk_copies(
            step, vis_hbm, sky_hbm, mask_hbm, outs[slot], sky.at[slot], mask.at[slot], sems.at[slot]
        )
        for slot, step in enumerate(steps)
    ]
    pairs_copy.wait()
    lane = lax.broadcasted_iota(jnp.int32, (1, LANES), 1)
    for end in range(2):
        for block in range(blocks):
            row = end * blocks + block
            station = pairs[end : end + 1, block * LANES : (block + 1) * LANES]
            live = lane + block * LANES < counts_ref[0]
            rows[row : row + 1, :] = jnp.where(live, station, STATION_COUNT)
    ends = (rows[...].astype(jnp.float32) - INDEX_SHIFT).astype(jnp.bfloat16)
    ends_out[0] = ends
    for slot in range(len(steps)):
        outs[slot][16 * blocks] = ends
        for copy in copies[slot][:2]:
            copy.wait()
        mask_model(outs[slot], sky.at[slot], mask.at[slot])
    for group in copies:
        for copy in group[2:]:
            copy.wait()


def pieces_of(values):
    high = values.astype(jnp.bfloat16)
    low = (values - high.astype(jnp.float32)).astype(jnp.bfloat16)
    return jnp.concatenate([high, low], axis=0)


def station_sums(first, second, table_ref):
    rows = first.shape[0]
    both = jnp.dot(
        pieces_of(jnp.concatenate([first, second], axis=1)),
        jnp.concatenate([table_ref[group] for group in range(table_ref.shape[0])], axis=1),
        preferred_element_type=jnp.float32,
    )
    return both[:rows] + both[rows:]


def end_table(ends_ref, table_ref):
    ends = ends_ref[ends_ref.shape[0] - 1].astype(jnp.float32).T
    lane = lax.broadcasted_iota(jnp.int32, (LANES, LANES), 1).astype(jnp.float32)
    one = jnp.ones((), jnp.bfloat16)
    zero = jnp.zeros((), jnp.bfloat16)
    stations = [
        (lane + (group * LANES - INDEX_SHIFT)).astype(jnp.bfloat16)
        for group in range(table_ref.shape[0])
    ]
    for row in range(table_ref.shape[1] // LANES):
        column = jnp.broadcast_to(ends[:, row : row + 1], (LANES, LANES)).astype(jnp.bfloat16)
        for group, station in enumerate(stations):
            table_ref[group, row * LANES : (row + 1) * LANES, :] = jnp.where(
                station == column, one, zero
            )


def unit_terms(chunk_ref, products_ref):
    blocks = products_ref.shape[2] // LANES
    plane_of = lambda base, plane: jnp.concatenate(
        [
            chunk_ref[8 * (base * blocks + block) + plane].astype(jnp.float32)
            for block in range(blocks)
        ],
        axis=1,
    )
    real, imag, power = {}, {}, {}
    for p in range(2):
        for q in range(2):
            plane = 2 * p + q
            vis_real = plane_of(0, plane)
            vis_imag = plane_of(0, 4 + plane)
            model_real = plane_of(1, plane)
            model_imag = plane_of(1, 4 + plane)
            real[p, q] = model_real * vis_real + model_imag * vis_imag
            imag[p, q] = model_real * vis_imag - model_imag * vis_real
            power[p, q] = model_real * model_real + model_imag * model_imag
            products_ref[plane] = real[p, q]
            products_ref[4 + plane] = imag[p, q]
            products_ref[8 + plane] = power[p, q]
    first = [real[p, 0] + real[p, 1] for p in range(2)]
    first += [imag[p, 0] + imag[p, 1] for p in range(2)]
    first += [power[p, 0] + power[p, 1] for p in range(2)]
    second = [real[0, q] + real[1, q] for q in range(2)]
    second += [-(imag[0, q] + imag[1, q]) for q in range(2)]
    second += [power[0, q] + power[1, q] for q in range(2)]
    return jnp.concatenate(first, 0), jnp.concatenate(second, 0)


def tile_kernel(chunk_ref, ends_ref, products_ref, table_ref, sums_ref):
    end_table(ends_ref, table_ref)
    sums_ref[...] = station_sums(*unit_terms(chunk_ref, products_ref), table_ref)


def end_gains(gains, ends_ref, share, blocks):
    ends = (ends_ref[ends_ref.shape[0] - 1].astype(jnp.float32) + INDEX_SHIFT).astype(jnp.int32)
    result = []
    for end in range(2):
        found = {row: [] for row in range(4)}
        for block in range(blocks):
            row = end * blocks + block
            index = jnp.broadcast_to(ends[row : row + 1, :], (share, LANES))
            lane = index % LANES
            group = index // LANES
            for part in range(4):
                rows = gains[part * share : (part + 1) * share]
                value = None
                for source in range(STATION_COUNT // LANES):
                    picked = jnp.take_along_axis(
                        rows[:, source * LANES : (source + 1) * LANES],
                        lane,
                        axis=1,
                        mode="promise_in_bounds",
                    )
                    value = picked if value is None else jnp.where(group == source, picked, value)
                found[part].append(value)
        result.append([jnp.concatenate(found[part], axis=1) for part in range(4)])
    return result


def gain_terms(gains, ends_ref, products_ref):
    share = products_ref.shape[1]
    blocks = products_ref.shape[2] // LANES
    at = end_gains(gains, ends_ref, share, blocks)
    gain = lambda part, feed, end: at[end][2 * part + feed]
    size = {
        (feed, end): gain(0, feed, end) * gain(0, feed, end)
        + gain(1, feed, end) * gain(1, feed, end)
        for feed in range(2)
        for end in range(2)
    }
    real = lambda p, q: products_ref[2 * p + q]
    imag = lambda p, q: products_ref[4 + 2 * p + q]
    power = lambda p, q: products_ref[8 + 2 * p + q]
    first = [
        sum(gain(0, q, 1) * real(p, q) - gain(1, q, 1) * imag(p, q) for q in range(2))
        for p in range(2)
    ]
    first += [
        sum(gain(0, q, 1) * imag(p, q) + gain(1, q, 1) * real(p, q) for q in range(2))
        for p in range(2)
    ]
    first += [sum(size[q, 1] * power(p, q) for q in range(2)) for p in range(2)]
    second = [
        sum(gain(0, p, 0) * real(p, q) + gain(1, p, 0) * imag(p, q) for p in range(2))
        for q in range(2)
    ]
    second += [
        sum(gain(1, p, 0) * real(p, q) - gain(0, p, 0) * imag(p, q) for p in range(2))
        for q in range(2)
    ]
    second += [sum(size[p, 0] * power(p, q) for p in range(2)) for q in range(2)]
    return jnp.concatenate(first, 0), jnp.concatenate(second, 0)


def solve_kernel(early, late, *refs):
    tiles = early + late
    chunks, refs = refs[:late], refs[late:]
    ends, refs = refs[:tiles], refs[tiles:]
    products, refs = refs[:early], refs[early:]
    tables, refs = refs[:early], refs[early:]
    sums, refs = refs[:early], refs[early:]
    outs, refs = refs[:tiles], refs[tiles:]
    late_products, refs = refs[:late], refs[late:]
    late_tables, refs = refs[:late], refs[late:]
    (solved_ref,) = refs
    share = products[0].shape[1]
    total = sum(part[...] for part in sums)
    for chunk_ref, ends_ref, products_ref, table_ref in zip(
        chunks, ends[early:], late_products, late_tables
    ):
        end_table(ends_ref, table_ref)
        total = total + station_sums(*unit_terms(chunk_ref, products_ref), table_ref)
    rows = 2 * share
    divisor = total[2 * rows :] + damping
    gains = jnp.concatenate([(total[:rows] + damping) / divisor, total[rows : 2 * rows] / divisor])
    total = 0.0
    for ends_ref, products_ref, table_ref in zip(
        ends, products + late_products, tables + late_tables
    ):
        total = total + station_sums(*gain_terms(gains, ends_ref, products_ref), table_ref)
    divisor = total[2 * rows :] + damping
    renewed = (total[: 2 * rows] + damping * gains) / jnp.concatenate([divisor, divisor])
    solved_ref[...] = 0.5 * (renewed + gains)
    owned = STATION_COUNT // tiles
    here = lax.axis_index("bl")
    for step in range(tiles):
        start = pl.multiple_of((here ^ step) * owned, owned)
        outs[step][...] = solved_ref[:, pl.ds(start, owned)]


def moment_kernel(basis_ref, *refs):
    pieces, moments_ref = refs[:-1], refs[-1]
    share = pieces[0].shape[0] // 4
    here = lax.axis_index("bl")
    columns = []
    for step in range(len(pieces)):
        start = pl.multiple_of((here ^ step) * share, share)
        columns.append(basis_ref[pl.ds(start, share), :])
    for degree in range(4):
        for part in range(4):
            terms = sum(
                piece[part * share : (part + 1) * share, :] * column[:, degree : degree + 1]
                for piece, column in zip(pieces, columns)
            )
            row = 4 * degree + part
            moments_ref[row : row + 1, :] = jnp.sum(terms, axis=0, keepdims=True)


def order_kernel(*refs):
    pieces, solved_ref = refs[:-1], refs[-1]
    share = pieces[0].shape[0] // 4
    here = lax.axis_index("bl")
    for step, piece in enumerate(pieces):
        start = pl.multiple_of((here ^ step) * share, share)
        for part in range(4):
            solved_ref[part, pl.ds(start, share), :] = piece[part * share : (part + 1) * share, :]


def fit_kernel(basis_ref, *refs):
    total = refs[0][...]
    for part in refs[1:-1]:
        total = total + part[...]
    fitted_ref = refs[-1]
    for part in range(4):
        fitted_ref[part] = sum(
            basis_ref[:, degree : degree + 1] * total[4 * degree + part : 4 * degree + part + 1, :]
            for degree in range(4)
        )


def vmem_call(kernel, outs, scratch=(), spaces=None, **options):
    def call(*args):
        return pl.pallas_call(
            kernel,
            out_shape=outs,
            in_specs=[
                pl.BlockSpec(memory_space=space) for space in spaces or [pltpu.VMEM] * len(args)
            ],
            out_specs=jax.tree.map(lambda _: pl.BlockSpec(memory_space=pltpu.VMEM), outs),
            scratch_shapes=list(scratch),
            compiler_params=pltpu.CompilerParams(vmem_limit_bytes=24 << 20),
            **options,
        )(*args)

    return call


def in_hbm(value):
    return pltpu.with_memory_space_constraint(value, pltpu.HBM)


def partners(count, step):
    return [(index, index ^ step) for index in range(count)]


def local_resplit(visibilities, sky_model, antenna_pairs, tile_counts, usable_mask):
    channel_local = visibilities.shape[1]
    slots = visibilities.shape[2]
    tiles = lax.axis_size("bl")
    groups = lax.axis_size("ch")
    share = channel_local // tiles
    owned = STATION_COUNT // tiles
    f32 = jnp.float32
    shape = jax.ShapeDtypeStruct

    steps = list(range(1, tiles))
    first = FIRST
    others = [step for step in steps if step != first] + [0]
    blocks = slots // LANES
    bf16 = jnp.bfloat16
    (lead,) = vmem_call(
        functools.partial(first_kernel, first),
        (shape((16 * blocks, share, LANES), bf16),),
        scratch=[
            pltpu.VMEM((8, share, slots), bf16),
            pltpu.VMEM((share, slots), jnp.int32),
            pltpu.SemaphoreType.DMA((2 + blocks,)),
        ],
        spaces=[pltpu.HBM] * 3,
    )(in_hbm(visibilities), in_hbm(sky_model), in_hbm(usable_mask))
    tile_counts, lead = lax.optimization_barrier((tile_counts, lead))
    *packed, own_ends = vmem_call(
        functools.partial(pack_kernel, others),
        (shape((16 * blocks + 1, share, LANES), bf16),) * len(others)
        + (shape((1, 2 * blocks, LANES), bf16),),
        scratch=[
            pltpu.VMEM((len(others), 8, share, slots), bf16),
            pltpu.VMEM((len(others), share, slots), jnp.int32),
            pltpu.VMEM((2, slots), jnp.int32),
            pltpu.VMEM((2 * blocks, LANES), jnp.int32),
            pltpu.SemaphoreType.DMA,
            pltpu.SemaphoreType.DMA((len(others), 2 + blocks)),
        ],
        spaces=[pltpu.SMEM] + [pltpu.HBM] * 4,
    )(
        tile_counts,
        in_hbm(visibilities),
        in_hbm(sky_model),
        in_hbm(usable_mask),
        in_hbm(antenna_pairs),
    )

    def exchange(piece, step):
        return lax.ppermute(piece, "bl", partners(tiles, step))

    chunks = {0: packed[-1], first: exchange(lead, first)}
    for piece, step in zip(packed[:-1], others):
        chunks[step] = exchange(piece, step)
    ends = dict(chunks)
    ends[first] = exchange(own_ends, first)

    products_shape = shape((12, share, slots), f32)
    table_dims = (STATION_COUNT // LANES, 2 * slots, LANES)
    table_shape = shape(table_dims, bf16)
    sums_shape = shape((6 * share, STATION_COUNT), f32)
    tile_outs = (products_shape, table_shape, sums_shape)
    late = [steps[-1]]
    done = {
        step: vmem_call(tile_kernel, tile_outs)(chunks[step], ends[step])
        for step in range(tiles)
        if step not in late
    }
    pieces = vmem_call(
        functools.partial(solve_kernel, len(done), len(late)),
        tuple(shape((4 * share, owned), f32) for _ in range(tiles)),
        scratch=[
            *[pltpu.VMEM((12, share, slots), f32) for _ in late],
            *[pltpu.VMEM(table_dims, bf16) for _ in late],
            pltpu.VMEM((4 * share, STATION_COUNT), f32),
        ],
    )(
        *[chunks[step] for step in late],
        *[ends[step] for step in list(done) + late],
        *[parts[0] for parts in done.values()],
        *[parts[1] for parts in done.values()],
        *[parts[2] for parts in done.values()],
    )
    received = {0: pieces[0]}
    for step in steps:
        received[step] = lax.ppermute(pieces[step], "bl", partners(tiles, step))
    received = [received[step] for step in range(tiles)]
    basis = lax.dynamic_slice_in_dim(
        jnp.asarray(poly_basis(channel_local * groups).T),
        lax.axis_index("ch") * channel_local,
        channel_local,
        0,
    )
    moments = vmem_call(moment_kernel, shape((16, owned), f32))(basis, *received)
    solved = vmem_call(order_kernel, shape((4, channel_local, owned), f32))(*received)
    moment_parts = [moments]
    for step in range(1, groups):
        moment_parts.append(lax.ppermute(moments, "ch", partners(groups, step)))
    fitted = vmem_call(fit_kernel, shape((4, channel_local, owned), f32))(basis, *moment_parts)
    out_shape = (2, 2, channel_local, owned)
    return solved.reshape(out_shape), fitted.reshape(out_shape)


FIRST = 2


def local(visibilities, sky_model, antenna_pairs, tile_counts, usable_mask):
    tiles = lax.axis_size("bl")
    groups = lax.axis_size("ch")
    power_of_two = lambda count: count & (count - 1) == 0
    resplit = (
        power_of_two(tiles)
        and power_of_two(groups)
        and 1 < tiles <= 4
        and groups <= 8
        and visibilities.shape[1] == 8 * tiles
        and STATION_COUNT % (128 * tiles) == 0
        and STATION_COUNT <= 2 * INDEX_SHIFT
        and visibilities.shape[2] == 4 * LANES
    )
    body = local_resplit if resplit else local_general
    return body(visibilities, sky_model, antenna_pairs, tile_counts, usable_mask)


def solution(mesh):
    return jax.shard_map(
        local,
        mesh=mesh,
        in_specs=(
            P(None, "ch", ("grp", "bl")),
            P(None, "ch", ("grp", "bl")),
            P(None, ("grp", "bl")),
            P(("grp", "bl")),
            P("ch", ("grp", "bl")),
        ),
        out_specs=(P(None, None, "ch", ("grp", "bl")), P(None, None, "ch", ("grp", "bl"))),
        check_vma=False,
    )
```

```python
import functools

import jax
import jax.numpy as jnp
import numpy as np
from jax import lax
from jax.experimental import pallas as pl
from jax.experimental.pallas import tpu as pltpu
from jax.sharding import PartitionSpec as P


STATION_COUNT = 512
SWEEPS = 2

damping = 4.0
highest = lax.Precision.HIGHEST


def poly_basis(channel_total):
    nodes = (2.0 * np.arange(channel_total, dtype=np.float64) - (channel_total - 1)) / (
        channel_total - 1
    )
    rows = []
    for degree in range(4):
        vector = nodes**degree
        for earlier in rows:
            vector = vector - np.sum(vector * earlier) * earlier
        rows.append(vector / np.sqrt(np.sum(vector * vector)))
    return np.stack(rows).astype(np.float32)


def split_parts(data):
    planes = data.astype(jnp.float32)
    shape_rest = planes.shape[1:]
    return (planes[:4].reshape((2, 2) + shape_rest), planes[4:].reshape((2, 2) + shape_rest))


def contributions(
    model_real_part, model_imaginary, vis_real, vis_imag, first_gain, second_gain, weights
):
    second_real = second_gain[0][None]
    second_imag = second_gain[1][None]
    left_real = model_real_part * second_real + model_imaginary * second_imag
    left_imag = model_imaginary * second_real - model_real_part * second_imag
    first_num_real = jnp.sum(left_real * vis_real + left_imag * vis_imag, axis=1) * weights
    first_num_imag = jnp.sum(left_real * vis_imag - left_imag * vis_real, axis=1) * weights
    first_den = jnp.sum(left_real * left_real + left_imag * left_imag, axis=1) * weights
    first_real = first_gain[0][:, None]
    first_imag = first_gain[1][:, None]
    right_real = model_real_part * first_real - model_imaginary * first_imag
    right_imag = model_real_part * first_imag + model_imaginary * first_real
    second_num_real = jnp.sum(right_real * vis_real + right_imag * vis_imag, axis=0) * weights
    second_num_imag = jnp.sum(right_imag * vis_real - right_real * vis_imag, axis=0) * weights
    second_den = jnp.sum(right_real * right_real + right_imag * right_imag, axis=0) * weights
    return (
        jnp.stack([first_num_real, first_num_imag, first_den]),
        jnp.stack([second_num_real, second_num_imag, second_den]),
    )


def refresh(station_sums, previous):
    divisor = station_sums[2] + damping
    return jnp.stack(
        [
            (station_sums[0] + damping * previous[0]) / divisor,
            (station_sums[1] + damping * previous[1]) / divisor,
        ]
    )


def station_totals(end_first, end_second, first_endpoints, second_ends):
    total_slots = end_first.shape[3]
    flat_first = end_first.reshape(-1, total_slots)
    flat_second = end_second.reshape(-1, total_slots)
    station_index = jnp.arange(STATION_COUNT, dtype=jnp.int32)
    table_first = (first_endpoints[:, None] == station_index[None, :]).astype(jnp.float32)
    table_second = (second_ends[:, None] == station_index[None, :]).astype(jnp.float32)
    summed = jnp.dot(
        flat_first, table_first, precision=highest, preferred_element_type=jnp.float32
    ) + jnp.dot(flat_second, table_second, precision=highest, preferred_element_type=jnp.float32)
    return summed.reshape(end_first.shape[:3] + (STATION_COUNT,))


def local_general(visibilities, sky_model, antenna_pairs, tile_counts, usable_mask):
    vis_real, vis_imag = split_parts(visibilities)
    model_real_part, model_imaginary = split_parts(sky_model)
    channel_local = visibilities.shape[1]
    tile_rows = visibilities.shape[2]
    owned_count = STATION_COUNT // lax.axis_size("bl")
    owner_start = lax.axis_index("bl") * owned_count
    live_slots = jnp.arange(tile_rows, dtype=jnp.int32) < tile_counts[0]
    weights = usable_mask.astype(jnp.float32) * live_slots.astype(jnp.float32)[None, :]
    channel_total = channel_local * lax.axis_size("ch")
    poly_rows = lax.dynamic_slice_in_dim(
        jnp.asarray(poly_basis(channel_total)),
        lax.axis_index("ch") * channel_local,
        channel_local,
        1,
    )
    gain_state = jnp.stack(
        [
            jnp.ones((2, channel_local, STATION_COUNT), jnp.float32),
            jnp.zeros((2, channel_local, STATION_COUNT), jnp.float32),
        ]
    )
    solved = gain_state
    for iteration in range(SWEEPS):
        first_gain = jnp.take(gain_state, antenna_pairs[0], axis=3)
        second_gain = jnp.take(gain_state, antenna_pairs[1], axis=3)
        end_first, end_second = contributions(
            model_real_part, model_imaginary, vis_real, vis_imag, first_gain, second_gain, weights
        )
        partial_sums = station_totals(end_first, end_second, antenna_pairs[0], antenna_pairs[1])
        station_sums = lax.psum_scatter(partial_sums, "bl", scatter_dimension=3, tiled=True)
        previous = lax.dynamic_slice_in_dim(gain_state, owner_start, owned_count, 3)
        renewed = refresh(station_sums, previous)
        if iteration == 1:
            renewed = 0.5 * (renewed + previous)
        solved = renewed
        if iteration < SWEEPS - 1:
            gain_state = lax.all_gather(renewed, "bl", axis=3, tiled=True)
    local_moments = jnp.einsum("kc,rfca->krfa", poly_rows, solved, precision=highest)
    moments = lax.psum(local_moments, "ch")
    fitted = jnp.einsum("kc,krfa->rfca", poly_rows, moments, precision=highest)
    return (solved, fitted)


LANES = 128
INDEX_SHIFT = 256.0


def chunk_copies(step, vis_hbm, sky_hbm, mask_hbm, out, sky, mask, sems):
    share, slots = mask.shape
    blocks = slots // LANES
    channels = pl.ds(pl.multiple_of((lax.axis_index("bl") ^ step) * share, share), share)
    copies = [
        pltpu.make_async_copy(mask_hbm.at[channels], mask, sems.at[0]),
        pltpu.make_async_copy(sky_hbm.at[:, channels], sky, sems.at[1]),
    ]
    for block in range(blocks):
        copies.append(
            pltpu.make_async_copy(
                vis_hbm.at[:, channels, pl.ds(block * LANES, LANES)],
                out.at[pl.ds(8 * block, 8)],
                sems.at[2 + block],
            )
        )
    for copy in copies:
        copy.start()
    return copies


def mask_model(out, sky, mask):
    blocks = mask.shape[1] // LANES
    weights = mask[...].astype(jnp.float32).astype(jnp.bfloat16)
    for block in range(blocks):
        lanes = slice(block * LANES, (block + 1) * LANES)
        for plane in range(8):
            out[8 * (blocks + block) + plane] = sky[plane, :, lanes] * weights[:, lanes]


def first_kernel(step, vis_hbm, sky_hbm, mask_hbm, out, sky, mask, sems):
    copies = chunk_copies(step, vis_hbm, sky_hbm, mask_hbm, out, sky, mask, sems)
    for copy in copies[:2]:
        copy.wait()
    mask_model(out, sky, mask)
    for copy in copies[2:]:
        copy.wait()


def pack_kernel(steps, counts_ref, vis_hbm, sky_hbm, mask_hbm, pairs_hbm, *refs):
    outs, ends_out = refs[: len(steps)], refs[len(steps)]
    sky, mask, pairs, rows, pairs_sem, sems = refs[len(steps) + 1 :]
    blocks = pairs.shape[1] // LANES
    pairs_copy = pltpu.make_async_copy(pairs_hbm, pairs, pairs_sem)
    pairs_copy.start()
    copies = [
        chunk_copies(
            step, vis_hbm, sky_hbm, mask_hbm, outs[slot], sky.at[slot], mask.at[slot], sems.at[slot]
        )
        for slot, step in enumerate(steps)
    ]
    pairs_copy.wait()
    lane = lax.broadcasted_iota(jnp.int32, (1, LANES), 1)
    for end in range(2):
        for block in range(blocks):
            row = end * blocks + block
            station = pairs[end : end + 1, block * LANES : (block + 1) * LANES]
            live = lane + block * LANES < counts_ref[0]
            rows[row : row + 1, :] = jnp.where(live, station, STATION_COUNT)
    ends = (rows[...].astype(jnp.float32) - INDEX_SHIFT).astype(jnp.bfloat16)
    ends_out[0] = ends
    for slot in range(len(steps)):
        outs[slot][16 * blocks] = ends
        for copy in copies[slot][:2]:
            copy.wait()
        mask_model(outs[slot], sky.at[slot], mask.at[slot])
    for group in copies:
        for copy in group[2:]:
            copy.wait()


def pieces_of(values):
    high = values.astype(jnp.bfloat16)
    low = (values - high.astype(jnp.float32)).astype(jnp.bfloat16)
    return jnp.concatenate([high, low], axis=0)


def split_dot(values, table):
    rows = values.shape[0]
    both = jnp.dot(pieces_of(values), table, preferred_element_type=jnp.float32)
    return both[:rows] + both[rows:]


def station_sums(first, second, table):
    return split_dot(jnp.concatenate([first, second], axis=1), table)


def read_table(table_ref):
    return jnp.concatenate([table_ref[group] for group in range(table_ref.shape[0])], axis=1)


def shifted_stations(axis):
    station = lax.broadcasted_iota(jnp.int32, (LANES, LANES), axis).astype(jnp.float32)
    return [
        (station + (group * LANES - INDEX_SHIFT)).astype(jnp.bfloat16)
        for group in range(STATION_COUNT // LANES)
    ]


def end_table(ends):
    columns = ends.astype(jnp.float32).T
    one = jnp.ones((), jnp.bfloat16)
    zero = jnp.zeros((), jnp.bfloat16)
    blocks = [[] for _ in range(STATION_COUNT // LANES)]
    for row in range(ends.shape[0]):
        column = jnp.broadcast_to(columns[:, row : row + 1], (LANES, LANES)).astype(jnp.bfloat16)
        for block, station in zip(blocks, shifted_stations(1)):
            block.append(jnp.where(station == column, one, zero))
    return [jnp.concatenate(block, axis=0) for block in blocks]


def look_up_table(ends, table_ref):
    one = jnp.ones((), jnp.bfloat16)
    zero = jnp.zeros((), jnp.bfloat16)
    for row in range(ends.shape[0]):
        for group, station in enumerate(shifted_stations(0)):
            table_ref[row, group * LANES : (group + 1) * LANES, :] = jnp.where(
                station == ends[row : row + 1, :], one, zero
            )


def unit_terms(chunk_ref, products_ref):
    blocks = products_ref.shape[2] // LANES
    plane_of = lambda base, plane: jnp.concatenate(
        [
            chunk_ref[8 * (base * blocks + block) + plane].astype(jnp.float32)
            for block in range(blocks)
        ],
        axis=1,
    )
    real, imag, power = {}, {}, {}
    for p in range(2):
        for q in range(2):
            plane = 2 * p + q
            vis_real = plane_of(0, plane)
            vis_imag = plane_of(0, 4 + plane)
            model_real = plane_of(1, plane)
            model_imag = plane_of(1, 4 + plane)
            real[p, q] = model_real * vis_real + model_imag * vis_imag
            imag[p, q] = model_real * vis_imag - model_imag * vis_real
            power[p, q] = model_real * model_real + model_imag * model_imag
            products_ref[plane] = real[p, q]
            products_ref[4 + plane] = imag[p, q]
            products_ref[8 + plane] = power[p, q]
    first = [real[p, 0] + real[p, 1] for p in range(2)]
    first += [imag[p, 0] + imag[p, 1] for p in range(2)]
    first += [power[p, 0] + power[p, 1] for p in range(2)]
    second = [real[0, q] + real[1, q] for q in range(2)]
    second += [-(imag[0, q] + imag[1, q]) for q in range(2)]
    second += [power[0, q] + power[1, q] for q in range(2)]
    return jnp.concatenate(first, 0), jnp.concatenate(second, 0)


def tile_kernel(chunk_ref, ends_ref, products_ref, table_ref, sums_ref, *look_up_ref):
    ends = ends_ref[ends_ref.shape[0] - 1]
    for group, block in enumerate(end_table(ends)):
        table_ref[group] = block
    sums_ref[...] = station_sums(*unit_terms(chunk_ref, products_ref), read_table(table_ref))
    for ref in look_up_ref:
        look_up_table(ends, ref)


def dot_gains(gains, look_up_ref, share):
    found = split_dot(gains, read_table(look_up_ref))
    slots = found.shape[1] // 2
    return [
        [
            found[part * share : (part + 1) * share, end * slots : (end + 1) * slots]
            for part in range(4)
        ]
        for end in range(2)
    ]


def end_gains(gains, ends_ref, share, blocks):
    ends = (ends_ref[ends_ref.shape[0] - 1].astype(jnp.float32) + INDEX_SHIFT).astype(jnp.int32)
    result = []
    for end in range(2):
        found = {row: [] for row in range(4)}
        for block in range(blocks):
            row = end * blocks + block
            index = jnp.broadcast_to(ends[row : row + 1, :], (share, LANES))
            lane = index % LANES
            group = index // LANES
            for part in range(4):
                rows = gains[part * share : (part + 1) * share]
                value = None
                for source in range(STATION_COUNT // LANES):
                    picked = jnp.take_along_axis(
                        rows[:, source * LANES : (source + 1) * LANES],
                        lane,
                        axis=1,
                        mode="promise_in_bounds",
                    )
                    value = picked if value is None else jnp.where(group == source, picked, value)
                found[part].append(value)
        result.append([jnp.concatenate(found[part], axis=1) for part in range(4)])
    return result


def gain_terms(at, products_ref):
    gain = lambda part, feed, end: at[end][2 * part + feed]
    size = {
        (feed, end): gain(0, feed, end) * gain(0, feed, end)
        + gain(1, feed, end) * gain(1, feed, end)
        for feed in range(2)
        for end in range(2)
    }
    real = lambda p, q: products_ref[2 * p + q]
    imag = lambda p, q: products_ref[4 + 2 * p + q]
    power = lambda p, q: products_ref[8 + 2 * p + q]
    first = [
        sum(gain(0, q, 1) * real(p, q) - gain(1, q, 1) * imag(p, q) for q in range(2))
        for p in range(2)
    ]
    first += [
        sum(gain(0, q, 1) * imag(p, q) + gain(1, q, 1) * real(p, q) for q in range(2))
        for p in range(2)
    ]
    first += [sum(size[q, 1] * power(p, q) for q in range(2)) for p in range(2)]
    second = [
        sum(gain(0, p, 0) * real(p, q) + gain(1, p, 0) * imag(p, q) for p in range(2))
        for q in range(2)
    ]
    second += [
        sum(gain(1, p, 0) * real(p, q) - gain(0, p, 0) * imag(p, q) for p in range(2))
        for q in range(2)
    ]
    second += [sum(size[p, 0] * power(p, q) for p in range(2)) for q in range(2)]
    return jnp.concatenate(first, 0), jnp.concatenate(second, 0)


def solve_kernel(early, late, *refs):
    tiles = early + late
    chunks, refs = refs[:late], refs[late:]
    ends, refs = refs[:tiles], refs[tiles:]
    products, refs = refs[:early], refs[early:]
    tables, refs = refs[:early], refs[early:]
    sums, refs = refs[:early], refs[early:]
    look_up_ref, refs = refs[0], refs[1:]
    outs, refs = refs[:tiles], refs[tiles:]
    late_products, refs = refs[:late], refs[late:]
    (solved_ref,) = refs
    share = products[0].shape[1]
    total = sum(part[...] for part in sums)
    tables = [read_table(table_ref) for table_ref in tables]
    for chunk_ref, ends_ref, products_ref in zip(chunks, ends[early:], late_products):
        tables.append(jnp.concatenate(end_table(ends_ref[ends_ref.shape[0] - 1]), axis=1))
        total = total + station_sums(*unit_terms(chunk_ref, products_ref), tables[-1])
    rows = 2 * share
    divisor = total[2 * rows :] + damping
    gains = jnp.concatenate([(total[:rows] + damping) / divisor, total[rows : 2 * rows] / divisor])
    total = 0.0
    blocks = products[0].shape[2] // LANES
    for tile, products_ref in enumerate(products + late_products):
        if tile < 0:
            at = dot_gains(gains, look_up_ref, share)
        else:
            at = end_gains(gains, ends[tile], share, blocks)
        total = total + station_sums(*gain_terms(at, products_ref), tables[tile])
    divisor = total[2 * rows :] + damping
    renewed = (total[: 2 * rows] + damping * gains) / jnp.concatenate([divisor, divisor])
    solved_ref[...] = 0.5 * (renewed + gains)
    owned = STATION_COUNT // tiles
    here = lax.axis_index("bl")
    for step in range(tiles):
        start = pl.multiple_of((here ^ step) * owned, owned)
        outs[step][...] = solved_ref[:, pl.ds(start, owned)]


def moment_kernel(basis_ref, *refs):
    pieces, moments_ref = refs[:-1], refs[-1]
    share = pieces[0].shape[0] // 4
    here = lax.axis_index("bl")
    columns = []
    for step in range(len(pieces)):
        start = pl.multiple_of((here ^ step) * share, share)
        columns.append(basis_ref[pl.ds(start, share), :])
    for degree in range(4):
        for part in range(4):
            terms = sum(
                piece[part * share : (part + 1) * share, :] * column[:, degree : degree + 1]
                for piece, column in zip(pieces, columns)
            )
            row = 4 * degree + part
            moments_ref[row : row + 1, :] = jnp.sum(terms, axis=0, keepdims=True)


def order_kernel(*refs):
    pieces, solved_ref = refs[:-1], refs[-1]
    share = pieces[0].shape[0] // 4
    here = lax.axis_index("bl")
    for step, piece in enumerate(pieces):
        start = pl.multiple_of((here ^ step) * share, share)
        for part in range(4):
            solved_ref[part, pl.ds(start, share), :] = piece[part * share : (part + 1) * share, :]


def vmem_call(kernel, outs, scratch=(), spaces=None, **options):
    def call(*args):
        return pl.pallas_call(
            kernel,
            out_shape=outs,
            in_specs=[
                pl.BlockSpec(memory_space=space) for space in spaces or [pltpu.VMEM] * len(args)
            ],
            out_specs=jax.tree.map(lambda _: pl.BlockSpec(memory_space=pltpu.VMEM), outs),
            scratch_shapes=list(scratch),
            compiler_params=pltpu.CompilerParams(vmem_limit_bytes=24 << 20),
            **options,
        )(*args)

    return call


def in_hbm(value):
    return pltpu.with_memory_space_constraint(value, pltpu.HBM)


def partners(count, step):
    return [(index, index ^ step) for index in range(count)]


def local_resplit(visibilities, sky_model, antenna_pairs, tile_counts, usable_mask):
    channel_local = visibilities.shape[1]
    slots = visibilities.shape[2]
    tiles = lax.axis_size("bl")
    groups = lax.axis_size("ch")
    share = channel_local // tiles
    owned = STATION_COUNT // tiles
    f32 = jnp.float32
    shape = jax.ShapeDtypeStruct

    steps = list(range(1, tiles))
    first = FIRST
    others = [step for step in steps if step != first] + [0]
    blocks = slots // LANES
    bf16 = jnp.bfloat16
    (lead,) = vmem_call(
        functools.partial(first_kernel, first),
        (shape((16 * blocks, share, LANES), bf16),),
        scratch=[
            pltpu.VMEM((8, share, slots), bf16),
            pltpu.VMEM((share, slots), jnp.int32),
            pltpu.SemaphoreType.DMA((2 + blocks,)),
        ],
        spaces=[pltpu.HBM] * 3,
    )(in_hbm(visibilities), in_hbm(sky_model), in_hbm(usable_mask))
    tile_counts, lead = lax.optimization_barrier((tile_counts, lead))
    *packed, own_ends = vmem_call(
        functools.partial(pack_kernel, others),
        (shape((16 * blocks + 1, share, LANES), bf16),) * len(others)
        + (shape((1, 2 * blocks, LANES), bf16),),
        scratch=[
            pltpu.VMEM((len(others), 8, share, slots), bf16),
            pltpu.VMEM((len(others), share, slots), jnp.int32),
            pltpu.VMEM((2, slots), jnp.int32),
            pltpu.VMEM((2 * blocks, LANES), jnp.int32),
            pltpu.SemaphoreType.DMA,
            pltpu.SemaphoreType.DMA((len(others), 2 + blocks)),
        ],
        spaces=[pltpu.SMEM] + [pltpu.HBM] * 4,
    )(
        tile_counts,
        in_hbm(visibilities),
        in_hbm(sky_model),
        in_hbm(usable_mask),
        in_hbm(antenna_pairs),
    )

    def exchange(piece, step):
        return lax.ppermute(piece, "bl", partners(tiles, step))

    chunks = {0: packed[-1], first: exchange(lead, first)}
    for piece, step in zip(packed[:-1], others):
        chunks[step] = exchange(piece, step)
    ends = dict(chunks)
    ends[first] = exchange(own_ends, first)

    products_shape = shape((12, share, slots), f32)
    table_dims = (STATION_COUNT // LANES, 2 * slots, LANES)
    table_shape = shape(table_dims, bf16)
    sums_shape = shape((6 * share, STATION_COUNT), f32)
    look_up_shape = shape((2 * blocks, STATION_COUNT, LANES), bf16)
    tile_outs = (products_shape, table_shape, sums_shape)
    late = [steps[-1]]
    done = {
        step: vmem_call(tile_kernel, tile_outs + ((look_up_shape,) if step == 0 else ()))(
            chunks[step], ends[step]
        )
        for step in range(tiles)
        if step not in late
    }
    pieces = vmem_call(
        functools.partial(solve_kernel, len(done), len(late)),
        tuple(shape((4 * share, owned), f32) for _ in range(tiles)),
        scratch=[
            *[pltpu.VMEM((12, share, slots), f32) for _ in late],
            pltpu.VMEM((4 * share, STATION_COUNT), f32),
        ],
    )(
        *[chunks[step] for step in late],
        *[ends[step] for step in list(done) + late],
        *[parts[0] for parts in done.values()],
        *[parts[1] for parts in done.values()],
        *[parts[2] for parts in done.values()],
        done[0][3],
    )
    received = {0: pieces[0]}
    for step in steps:
        received[step] = lax.ppermute(pieces[step], "bl", partners(tiles, step))
    received = [received[step] for step in range(tiles)]
    basis = lax.dynamic_slice_in_dim(
        jnp.asarray(poly_basis(channel_local * groups).T),
        lax.axis_index("ch") * channel_local,
        channel_local,
        0,
    )
    moments = vmem_call(moment_kernel, shape((16, owned), f32))(basis, *received)
    solved = vmem_call(order_kernel, shape((4, channel_local, owned), f32))(*received)
    moment_parts = [moments]
    for step in range(1, groups):
        moment_parts.append(lax.ppermute(moments, "ch", partners(groups, step)))
    total = sum(moment_parts).reshape(4, 4, owned)
    fitted = sum(basis[None, :, k, None] * total[k][:, None, :] for k in range(4))
    out_shape = (2, 2, channel_local, owned)
    return solved.reshape(out_shape), fitted.reshape(out_shape)


FIRST = 2


def local(visibilities, sky_model, antenna_pairs, tile_counts, usable_mask):
    tiles = lax.axis_size("bl")
    groups = lax.axis_size("ch")
    power_of_two = lambda count: count & (count - 1) == 0
    resplit = (
        power_of_two(tiles)
        and power_of_two(groups)
        and 1 < tiles <= 4
        and groups <= 8
        and visibilities.shape[1] == 8 * tiles
        and STATION_COUNT % (128 * tiles) == 0
        and STATION_COUNT <= 2 * INDEX_SHIFT
        and visibilities.shape[2] == 4 * LANES
    )
    body = local_resplit if resplit else local_general
    return body(visibilities, sky_model, antenna_pairs, tile_counts, usable_mask)


def solution(mesh):
    return jax.shard_map(
        local,
        mesh=mesh,
        in_specs=(
            P(None, "ch", ("grp", "bl")),
            P(None, "ch", ("grp", "bl")),
            P(None, ("grp", "bl")),
            P(("grp", "bl")),
            P("ch", ("grp", "bl")),
        ),
        out_specs=(P(None, None, "ch", ("grp", "bl")), P(None, None, "ch", ("grp", "bl"))),
        check_vma=False,
    )
```

```python
import functools

import jax
import jax.numpy as jnp
import numpy as np
from jax import lax
from jax.experimental import pallas as pl
from jax.experimental.pallas import tpu as pltpu
from jax.sharding import PartitionSpec as P


STATION_COUNT = 512
SWEEPS = 2

damping = 4.0
highest = lax.Precision.HIGHEST


def poly_basis(channel_total):
    nodes = (2.0 * np.arange(channel_total, dtype=np.float64) - (channel_total - 1)) / (
        channel_total - 1
    )
    rows = []
    for degree in range(4):
        vector = nodes**degree
        for earlier in rows:
            vector = vector - np.sum(vector * earlier) * earlier
        rows.append(vector / np.sqrt(np.sum(vector * vector)))
    return np.stack(rows).astype(np.float32)


def split_parts(data):
    planes = data.astype(jnp.float32)
    shape_rest = planes.shape[1:]
    return (planes[:4].reshape((2, 2) + shape_rest), planes[4:].reshape((2, 2) + shape_rest))


def contributions(
    model_real_part, model_imaginary, vis_real, vis_imag, first_gain, second_gain, weights
):
    second_real = second_gain[0][None]
    second_imag = second_gain[1][None]
    left_real = model_real_part * second_real + model_imaginary * second_imag
    left_imag = model_imaginary * second_real - model_real_part * second_imag
    first_num_real = jnp.sum(left_real * vis_real + left_imag * vis_imag, axis=1) * weights
    first_num_imag = jnp.sum(left_real * vis_imag - left_imag * vis_real, axis=1) * weights
    first_den = jnp.sum(left_real * left_real + left_imag * left_imag, axis=1) * weights
    first_real = first_gain[0][:, None]
    first_imag = first_gain[1][:, None]
    right_real = model_real_part * first_real - model_imaginary * first_imag
    right_imag = model_real_part * first_imag + model_imaginary * first_real
    second_num_real = jnp.sum(right_real * vis_real + right_imag * vis_imag, axis=0) * weights
    second_num_imag = jnp.sum(right_imag * vis_real - right_real * vis_imag, axis=0) * weights
    second_den = jnp.sum(right_real * right_real + right_imag * right_imag, axis=0) * weights
    return (
        jnp.stack([first_num_real, first_num_imag, first_den]),
        jnp.stack([second_num_real, second_num_imag, second_den]),
    )


def refresh(station_sums, previous):
    divisor = station_sums[2] + damping
    return jnp.stack(
        [
            (station_sums[0] + damping * previous[0]) / divisor,
            (station_sums[1] + damping * previous[1]) / divisor,
        ]
    )


def station_totals(end_first, end_second, first_endpoints, second_ends):
    total_slots = end_first.shape[3]
    flat_first = end_first.reshape(-1, total_slots)
    flat_second = end_second.reshape(-1, total_slots)
    station_index = jnp.arange(STATION_COUNT, dtype=jnp.int32)
    table_first = (first_endpoints[:, None] == station_index[None, :]).astype(jnp.float32)
    table_second = (second_ends[:, None] == station_index[None, :]).astype(jnp.float32)
    summed = jnp.dot(
        flat_first, table_first, precision=highest, preferred_element_type=jnp.float32
    ) + jnp.dot(flat_second, table_second, precision=highest, preferred_element_type=jnp.float32)
    return summed.reshape(end_first.shape[:3] + (STATION_COUNT,))


def local_general(visibilities, sky_model, antenna_pairs, tile_counts, usable_mask):
    vis_real, vis_imag = split_parts(visibilities)
    model_real_part, model_imaginary = split_parts(sky_model)
    channel_local = visibilities.shape[1]
    tile_rows = visibilities.shape[2]
    owned_count = STATION_COUNT // lax.axis_size("bl")
    owner_start = lax.axis_index("bl") * owned_count
    live_slots = jnp.arange(tile_rows, dtype=jnp.int32) < tile_counts[0]
    weights = usable_mask.astype(jnp.float32) * live_slots.astype(jnp.float32)[None, :]
    channel_total = channel_local * lax.axis_size("ch")
    poly_rows = lax.dynamic_slice_in_dim(
        jnp.asarray(poly_basis(channel_total)),
        lax.axis_index("ch") * channel_local,
        channel_local,
        1,
    )
    gain_state = jnp.stack(
        [
            jnp.ones((2, channel_local, STATION_COUNT), jnp.float32),
            jnp.zeros((2, channel_local, STATION_COUNT), jnp.float32),
        ]
    )
    solved = gain_state
    for iteration in range(SWEEPS):
        first_gain = jnp.take(gain_state, antenna_pairs[0], axis=3)
        second_gain = jnp.take(gain_state, antenna_pairs[1], axis=3)
        end_first, end_second = contributions(
            model_real_part, model_imaginary, vis_real, vis_imag, first_gain, second_gain, weights
        )
        partial_sums = station_totals(end_first, end_second, antenna_pairs[0], antenna_pairs[1])
        station_sums = lax.psum_scatter(partial_sums, "bl", scatter_dimension=3, tiled=True)
        previous = lax.dynamic_slice_in_dim(gain_state, owner_start, owned_count, 3)
        renewed = refresh(station_sums, previous)
        if iteration == 1:
            renewed = 0.5 * (renewed + previous)
        solved = renewed
        if iteration < SWEEPS - 1:
            gain_state = lax.all_gather(renewed, "bl", axis=3, tiled=True)
    local_moments = jnp.einsum("kc,rfca->krfa", poly_rows, solved, precision=highest)
    moments = lax.psum(local_moments, "ch")
    fitted = jnp.einsum("kc,krfa->rfca", poly_rows, moments, precision=highest)
    return (solved, fitted)


LANES = 128
INDEX_SHIFT = 256.0


def partner_step(slot, column, table):
    even, odd = table
    return even[slot] + (column % 2) * (odd[slot] - even[slot])


def chunk_copies(step, vis_hbm, sky_hbm, mask_hbm, out, sky, mask, sems):
    share, slots = mask.shape
    blocks = slots // LANES
    partner = lax.axis_index("bl") ^ partner_step(step, lax.axis_index("ch"), RAW_STEPS)
    channels = pl.ds(pl.multiple_of(partner * share, share), share)
    copies = [
        pltpu.make_async_copy(mask_hbm.at[channels], mask, sems.at[0]),
        pltpu.make_async_copy(sky_hbm.at[:, channels], sky, sems.at[1]),
    ]
    for block in range(blocks):
        copies.append(
            pltpu.make_async_copy(
                vis_hbm.at[:, channels, pl.ds(block * LANES, LANES)],
                out.at[pl.ds(8 * block, 8)],
                sems.at[2 + block],
            )
        )
    for copy in copies:
        copy.start()
    return copies


def mask_model(out, sky, mask):
    blocks = mask.shape[1] // LANES
    weights = mask[...].astype(jnp.float32).astype(jnp.bfloat16)
    for block in range(blocks):
        lanes = slice(block * LANES, (block + 1) * LANES)
        for plane in range(8):
            out[8 * (blocks + block) + plane] = sky[plane, :, lanes] * weights[:, lanes]


def first_kernel(step, vis_hbm, sky_hbm, mask_hbm, out, sky, mask, sems):
    copies = chunk_copies(step, vis_hbm, sky_hbm, mask_hbm, out, sky, mask, sems)
    for copy in copies[:2]:
        copy.wait()
    mask_model(out, sky, mask)
    for copy in copies[2:]:
        copy.wait()


def pack_kernel(steps, counts_ref, vis_hbm, sky_hbm, mask_hbm, pairs_hbm, *refs):
    outs, ends_out = refs[: len(steps)], refs[len(steps)]
    sky, mask, pairs, rows, pairs_sem, sems = refs[len(steps) + 1 :]
    blocks = pairs.shape[1] // LANES
    pairs_copy = pltpu.make_async_copy(pairs_hbm, pairs, pairs_sem)
    pairs_copy.start()
    copies = [
        chunk_copies(
            step, vis_hbm, sky_hbm, mask_hbm, outs[slot], sky.at[slot], mask.at[slot], sems.at[slot]
        )
        for slot, step in enumerate(steps)
    ]
    pairs_copy.wait()
    lane = lax.broadcasted_iota(jnp.int32, (1, LANES), 1)
    for end in range(2):
        for block in range(blocks):
            row = end * blocks + block
            station = pairs[end : end + 1, block * LANES : (block + 1) * LANES]
            live = lane + block * LANES < counts_ref[0]
            rows[row : row + 1, :] = jnp.where(live, station, STATION_COUNT)
    ends = (rows[...].astype(jnp.float32) - INDEX_SHIFT).astype(jnp.bfloat16)
    ends_out[0] = ends
    for slot in range(len(steps)):
        outs[slot][16 * blocks] = ends
        for copy in copies[slot][:2]:
            copy.wait()
        mask_model(outs[slot], sky.at[slot], mask.at[slot])
    for group in copies:
        for copy in group[2:]:
            copy.wait()


def pieces_of(values):
    high = values.astype(jnp.bfloat16)
    low = (values - high.astype(jnp.float32)).astype(jnp.bfloat16)
    return jnp.concatenate([high, low], axis=0)


def split_dot(values, table):
    rows = values.shape[0]
    both = jnp.dot(pieces_of(values), table, preferred_element_type=jnp.float32)
    return both[:rows] + both[rows:]


def station_sums(first, second, table):
    return split_dot(jnp.concatenate([first, second], axis=1), table)


def read_table(table_ref):
    return jnp.concatenate([table_ref[group] for group in range(table_ref.shape[0])], axis=1)


def shifted_stations(axis):
    station = lax.broadcasted_iota(jnp.int32, (LANES, LANES), axis).astype(jnp.float32)
    return [
        (station + (group * LANES - INDEX_SHIFT)).astype(jnp.bfloat16)
        for group in range(STATION_COUNT // LANES)
    ]


def end_table(ends):
    columns = ends.astype(jnp.float32).T
    one = jnp.ones((), jnp.bfloat16)
    zero = jnp.zeros((), jnp.bfloat16)
    blocks = [[] for _ in range(STATION_COUNT // LANES)]
    for row in range(ends.shape[0]):
        column = jnp.broadcast_to(columns[:, row : row + 1], (LANES, LANES)).astype(jnp.bfloat16)
        for block, station in zip(blocks, shifted_stations(1)):
            block.append(jnp.where(station == column, one, zero))
    return [jnp.concatenate(block, axis=0) for block in blocks]


def look_up_table(ends, table_ref):
    one = jnp.ones((), jnp.bfloat16)
    zero = jnp.zeros((), jnp.bfloat16)
    for row in range(ends.shape[0]):
        for group, station in enumerate(shifted_stations(0)):
            table_ref[row, group * LANES : (group + 1) * LANES, :] = jnp.where(
                station == ends[row : row + 1, :], one, zero
            )


def unit_terms(chunk_ref, products_ref):
    blocks = products_ref.shape[2] // LANES
    plane_of = lambda base, plane: jnp.concatenate(
        [
            chunk_ref[8 * (base * blocks + block) + plane].astype(jnp.float32)
            for block in range(blocks)
        ],
        axis=1,
    )
    real, imag, power = {}, {}, {}
    for p in range(2):
        for q in range(2):
            plane = 2 * p + q
            vis_real = plane_of(0, plane)
            vis_imag = plane_of(0, 4 + plane)
            model_real = plane_of(1, plane)
            model_imag = plane_of(1, 4 + plane)
            real[p, q] = model_real * vis_real + model_imag * vis_imag
            imag[p, q] = model_real * vis_imag - model_imag * vis_real
            power[p, q] = model_real * model_real + model_imag * model_imag
            products_ref[plane] = real[p, q]
            products_ref[4 + plane] = imag[p, q]
            products_ref[8 + plane] = power[p, q]
    first = [real[p, 0] + real[p, 1] for p in range(2)]
    first += [imag[p, 0] + imag[p, 1] for p in range(2)]
    first += [power[p, 0] + power[p, 1] for p in range(2)]
    second = [real[0, q] + real[1, q] for q in range(2)]
    second += [-(imag[0, q] + imag[1, q]) for q in range(2)]
    second += [power[0, q] + power[1, q] for q in range(2)]
    return jnp.concatenate(first, 0), jnp.concatenate(second, 0)


def tile_kernel(chunk_ref, ends_ref, products_ref, table_ref, sums_ref, *look_up_ref):
    ends = ends_ref[ends_ref.shape[0] - 1]
    for group, block in enumerate(end_table(ends)):
        table_ref[group] = block
    sums_ref[...] = station_sums(*unit_terms(chunk_ref, products_ref), read_table(table_ref))
    for ref in look_up_ref:
        look_up_table(ends, ref)


def dot_gains(gains, look_up_ref, share):
    found = split_dot(gains, read_table(look_up_ref))
    slots = found.shape[1] // 2
    return [
        [
            found[part * share : (part + 1) * share, end * slots : (end + 1) * slots]
            for part in range(4)
        ]
        for end in range(2)
    ]


def end_gains(gains, ends_ref, share, blocks):
    ends = (ends_ref[ends_ref.shape[0] - 1].astype(jnp.float32) + INDEX_SHIFT).astype(jnp.int32)
    result = []
    for end in range(2):
        found = {row: [] for row in range(4)}
        for block in range(blocks):
            row = end * blocks + block
            index = jnp.broadcast_to(ends[row : row + 1, :], (share, LANES))
            lane = index % LANES
            group = index // LANES
            for part in range(4):
                rows = gains[part * share : (part + 1) * share]
                value = None
                for source in range(STATION_COUNT // LANES):
                    picked = jnp.take_along_axis(
                        rows[:, source * LANES : (source + 1) * LANES],
                        lane,
                        axis=1,
                        mode="promise_in_bounds",
                    )
                    value = picked if value is None else jnp.where(group == source, picked, value)
                found[part].append(value)
        result.append([jnp.concatenate(found[part], axis=1) for part in range(4)])
    return result


def gain_terms(at, products_ref):
    gain = lambda part, feed, end: at[end][2 * part + feed]
    size = {
        (feed, end): gain(0, feed, end) * gain(0, feed, end)
        + gain(1, feed, end) * gain(1, feed, end)
        for feed in range(2)
        for end in range(2)
    }
    real = lambda p, q: products_ref[2 * p + q]
    imag = lambda p, q: products_ref[4 + 2 * p + q]
    power = lambda p, q: products_ref[8 + 2 * p + q]
    first = [
        sum(gain(0, q, 1) * real(p, q) - gain(1, q, 1) * imag(p, q) for q in range(2))
        for p in range(2)
    ]
    first += [
        sum(gain(0, q, 1) * imag(p, q) + gain(1, q, 1) * real(p, q) for q in range(2))
        for p in range(2)
    ]
    first += [sum(size[q, 1] * power(p, q) for q in range(2)) for p in range(2)]
    second = [
        sum(gain(0, p, 0) * real(p, q) + gain(1, p, 0) * imag(p, q) for p in range(2))
        for q in range(2)
    ]
    second += [
        sum(gain(1, p, 0) * real(p, q) - gain(0, p, 0) * imag(p, q) for p in range(2))
        for q in range(2)
    ]
    second += [sum(size[p, 0] * power(p, q) for p in range(2)) for q in range(2)]
    return jnp.concatenate(first, 0), jnp.concatenate(second, 0)


def solve_kernel(early, late, *refs):
    tiles = early + late
    chunks, refs = refs[:late], refs[late:]
    ends, refs = refs[:tiles], refs[tiles:]
    products, refs = refs[:early], refs[early:]
    tables, refs = refs[:early], refs[early:]
    sums, refs = refs[:early], refs[early:]
    look_up_ref, refs = refs[0], refs[1:]
    outs, refs = refs[:tiles], refs[tiles:]
    late_products, refs = refs[:late], refs[late:]
    (solved_ref,) = refs
    share = products[0].shape[1]
    total = sum(part[...] for part in sums)
    tables = [read_table(table_ref) for table_ref in tables]
    for chunk_ref, ends_ref, products_ref in zip(chunks, ends[early:], late_products):
        tables.append(jnp.concatenate(end_table(ends_ref[ends_ref.shape[0] - 1]), axis=1))
        total = total + station_sums(*unit_terms(chunk_ref, products_ref), tables[-1])
    rows = 2 * share
    divisor = total[2 * rows :] + damping
    gains = jnp.concatenate([(total[:rows] + damping) / divisor, total[rows : 2 * rows] / divisor])
    total = 0.0
    blocks = products[0].shape[2] // LANES
    for tile, products_ref in enumerate(products + late_products):
        if tile < 0:
            at = dot_gains(gains, look_up_ref, share)
        else:
            at = end_gains(gains, ends[tile], share, blocks)
        total = total + station_sums(*gain_terms(at, products_ref), tables[tile])
    divisor = total[2 * rows :] + damping
    renewed = (total[: 2 * rows] + damping * gains) / jnp.concatenate([divisor, divisor])
    solved_ref[...] = 0.5 * (renewed + gains)
    owned = STATION_COUNT // tiles
    here = lax.axis_index("bl")
    for step in range(tiles):
        start = pl.multiple_of(((here + tiles - step) % tiles) * owned, owned)
        outs[step][...] = solved_ref[:, pl.ds(start, owned)]


def moment_kernel(basis_ref, *refs):
    pieces, moments_ref = refs[:-1], refs[-1]
    share = pieces[0].shape[0] // 4
    here = lax.axis_index("bl")
    columns = []
    for step in range(len(pieces)):
        start = pl.multiple_of(((here + step) % len(pieces)) * share, share)
        columns.append(basis_ref[pl.ds(start, share), :])
    for degree in range(4):
        for part in range(4):
            terms = sum(
                piece[part * share : (part + 1) * share, :] * column[:, degree : degree + 1]
                for piece, column in zip(pieces, columns)
            )
            row = 4 * degree + part
            moments_ref[row : row + 1, :] = jnp.sum(terms, axis=0, keepdims=True)


def order_kernel(*refs):
    pieces, solved_ref = refs[:-1], refs[-1]
    share = pieces[0].shape[0] // 4
    here = lax.axis_index("bl")
    for step, piece in enumerate(pieces):
        start = pl.multiple_of(((here + step) % len(pieces)) * share, share)
        for part in range(4):
            solved_ref[part, pl.ds(start, share), :] = piece[part * share : (part + 1) * share, :]


def vmem_call(kernel, outs, scratch=(), spaces=None, **options):
    def call(*args):
        return pl.pallas_call(
            kernel,
            out_shape=outs,
            in_specs=[
                pl.BlockSpec(memory_space=space) for space in spaces or [pltpu.VMEM] * len(args)
            ],
            out_specs=jax.tree.map(lambda _: pl.BlockSpec(memory_space=pltpu.VMEM), outs),
            scratch_shapes=list(scratch),
            compiler_params=pltpu.CompilerParams(vmem_limit_bytes=24 << 20),
            **options,
        )(*args)

    return call


def in_hbm(value):
    return pltpu.with_memory_space_constraint(value, pltpu.HBM)


def mesh_partners(tiles, groups, step, table):
    return [
        (row * groups + column, (row ^ partner_step(step, column, table)) * groups + column)
        for row in range(tiles)
        for column in range(groups)
    ]


def partners(count, step):
    return [(index, index ^ step) for index in range(count)]


def local_resplit(visibilities, sky_model, antenna_pairs, tile_counts, usable_mask):
    channel_local = visibilities.shape[1]
    slots = visibilities.shape[2]
    tiles = lax.axis_size("bl")
    groups = lax.axis_size("ch")
    share = channel_local // tiles
    owned = STATION_COUNT // tiles
    f32 = jnp.float32
    shape = jax.ShapeDtypeStruct

    steps = list(range(1, tiles))
    first = FIRST
    others = [step for step in steps if step != first] + [0]
    blocks = slots // LANES
    bf16 = jnp.bfloat16
    (lead,) = vmem_call(
        functools.partial(first_kernel, first),
        (shape((16 * blocks, share, LANES), bf16),),
        scratch=[
            pltpu.VMEM((8, share, slots), bf16),
            pltpu.VMEM((share, slots), jnp.int32),
            pltpu.SemaphoreType.DMA((2 + blocks,)),
        ],
        spaces=[pltpu.HBM] * 3,
    )(in_hbm(visibilities), in_hbm(sky_model), in_hbm(usable_mask))
    tile_counts, lead = lax.optimization_barrier((tile_counts, lead))
    *packed, own_ends = vmem_call(
        functools.partial(pack_kernel, others),
        (shape((16 * blocks + 1, share, LANES), bf16),) * len(others)
        + (shape((1, 2 * blocks, LANES), bf16),),
        scratch=[
            pltpu.VMEM((len(others), 8, share, slots), bf16),
            pltpu.VMEM((len(others), share, slots), jnp.int32),
            pltpu.VMEM((2, slots), jnp.int32),
            pltpu.VMEM((2 * blocks, LANES), jnp.int32),
            pltpu.SemaphoreType.DMA,
            pltpu.SemaphoreType.DMA((len(others), 2 + blocks)),
        ],
        spaces=[pltpu.SMEM] + [pltpu.HBM] * 4,
    )(
        tile_counts,
        in_hbm(visibilities),
        in_hbm(sky_model),
        in_hbm(usable_mask),
        in_hbm(antenna_pairs),
    )

    def exchange(piece, step):
        return lax.ppermute(piece, ("bl", "ch"), mesh_partners(tiles, groups, step, RAW_STEPS))

    chunks = {0: packed[-1], first: exchange(lead, first)}
    for piece, step in zip(packed[:-1], others):
        chunks[step] = exchange(piece, step)
    ends = dict(chunks)
    ends[first] = exchange(own_ends, first)

    products_shape = shape((12, share, slots), f32)
    table_dims = (STATION_COUNT // LANES, 2 * slots, LANES)
    table_shape = shape(table_dims, bf16)
    sums_shape = shape((6 * share, STATION_COUNT), f32)
    look_up_shape = shape((2 * blocks, STATION_COUNT, LANES), bf16)
    tile_outs = (products_shape, table_shape, sums_shape)
    late = [steps[-1]]
    done = {
        step: vmem_call(tile_kernel, tile_outs + ((look_up_shape,) if step == 0 else ()))(
            chunks[step], ends[step]
        )
        for step in range(tiles)
        if step not in late
    }
    pieces = vmem_call(
        functools.partial(solve_kernel, len(done), len(late)),
        tuple(shape((4 * share, owned), f32) for _ in range(tiles)),
        scratch=[
            *[pltpu.VMEM((12, share, slots), f32) for _ in late],
            pltpu.VMEM((4 * share, STATION_COUNT), f32),
        ],
    )(
        *[chunks[step] for step in late],
        *[ends[step] for step in list(done) + late],
        *[parts[0] for parts in done.values()],
        *[parts[1] for parts in done.values()],
        *[parts[2] for parts in done.values()],
        done[0][3],
    )
    received = {0: pieces[0]}
    for step in steps:
        received[step] = lax.ppermute(
            pieces[step], "bl", [(row, (row - step) % tiles) for row in range(tiles)]
        )
    received = [received[step] for step in range(tiles)]
    basis = lax.dynamic_slice_in_dim(
        jnp.asarray(poly_basis(channel_local * groups).T),
        lax.axis_index("ch") * channel_local,
        channel_local,
        0,
    )
    moments = vmem_call(moment_kernel, shape((16, owned), f32))(basis, *received)
    solved = vmem_call(order_kernel, shape((4, channel_local, owned), f32))(*received)
    moment_parts = [moments]
    for step in range(1, groups):
        moment_parts.append(lax.ppermute(moments, "ch", partners(groups, step)))
    total = sum(moment_parts).reshape(4, 4, owned)
    fitted = sum(basis[None, :, k, None] * total[k][:, None, :] for k in range(4))
    out_shape = (2, 2, channel_local, owned)
    return solved.reshape(out_shape), fitted.reshape(out_shape)


FIRST = 2
RAW_STEPS = ((0, 1, 2, 3), (0, 1, 3, 2))


def local(visibilities, sky_model, antenna_pairs, tile_counts, usable_mask):
    tiles = lax.axis_size("bl")
    groups = lax.axis_size("ch")
    resplit = (
        tiles == 4
        and groups == 4
        and visibilities.shape[1] == 8 * tiles
        and STATION_COUNT % (128 * tiles) == 0
        and STATION_COUNT <= 2 * INDEX_SHIFT
        and visibilities.shape[2] == 4 * LANES
    )
    body = local_resplit if resplit else local_general
    return body(visibilities, sky_model, antenna_pairs, tile_counts, usable_mask)


def solution(mesh):
    return jax.shard_map(
        local,
        mesh=mesh,
        in_specs=(
            P(None, "ch", ("grp", "bl")),
            P(None, "ch", ("grp", "bl")),
            P(None, ("grp", "bl")),
            P(("grp", "bl")),
            P("ch", ("grp", "bl")),
        ),
        out_specs=(P(None, None, "ch", ("grp", "bl")), P(None, None, "ch", ("grp", "bl"))),
        check_vma=False,
    )
```

```python
import functools

import jax
import jax.numpy as jnp
import numpy as np
from jax import lax
from jax.experimental import pallas as pl
from jax.experimental.pallas import tpu as pltpu
from jax.sharding import PartitionSpec as P


STATION_COUNT = 512
SWEEPS = 2

damping = 4.0
highest = lax.Precision.HIGHEST


def poly_basis(channel_total):
    nodes = (2.0 * np.arange(channel_total, dtype=np.float64) - (channel_total - 1)) / (
        channel_total - 1
    )
    rows = []
    for degree in range(4):
        vector = nodes**degree
        for earlier in rows:
            vector = vector - np.sum(vector * earlier) * earlier
        rows.append(vector / np.sqrt(np.sum(vector * vector)))
    return np.stack(rows).astype(np.float32)


def split_parts(data):
    planes = data.astype(jnp.float32)
    shape_rest = planes.shape[1:]
    return (planes[:4].reshape((2, 2) + shape_rest), planes[4:].reshape((2, 2) + shape_rest))


def contributions(
    model_real_part, model_imaginary, vis_real, vis_imag, first_gain, second_gain, weights
):
    second_real = second_gain[0][None]
    second_imag = second_gain[1][None]
    left_real = model_real_part * second_real + model_imaginary * second_imag
    left_imag = model_imaginary * second_real - model_real_part * second_imag
    first_num_real = jnp.sum(left_real * vis_real + left_imag * vis_imag, axis=1) * weights
    first_num_imag = jnp.sum(left_real * vis_imag - left_imag * vis_real, axis=1) * weights
    first_den = jnp.sum(left_real * left_real + left_imag * left_imag, axis=1) * weights
    first_real = first_gain[0][:, None]
    first_imag = first_gain[1][:, None]
    right_real = model_real_part * first_real - model_imaginary * first_imag
    right_imag = model_real_part * first_imag + model_imaginary * first_real
    second_num_real = jnp.sum(right_real * vis_real + right_imag * vis_imag, axis=0) * weights
    second_num_imag = jnp.sum(right_imag * vis_real - right_real * vis_imag, axis=0) * weights
    second_den = jnp.sum(right_real * right_real + right_imag * right_imag, axis=0) * weights
    return (
        jnp.stack([first_num_real, first_num_imag, first_den]),
        jnp.stack([second_num_real, second_num_imag, second_den]),
    )


def refresh(station_sums, previous):
    divisor = station_sums[2] + damping
    return jnp.stack(
        [
            (station_sums[0] + damping * previous[0]) / divisor,
            (station_sums[1] + damping * previous[1]) / divisor,
        ]
    )


def station_totals(end_first, end_second, first_endpoints, second_ends):
    total_slots = end_first.shape[3]
    flat_first = end_first.reshape(-1, total_slots)
    flat_second = end_second.reshape(-1, total_slots)
    station_index = jnp.arange(STATION_COUNT, dtype=jnp.int32)
    table_first = (first_endpoints[:, None] == station_index[None, :]).astype(jnp.float32)
    table_second = (second_ends[:, None] == station_index[None, :]).astype(jnp.float32)
    summed = jnp.dot(
        flat_first, table_first, precision=highest, preferred_element_type=jnp.float32
    ) + jnp.dot(flat_second, table_second, precision=highest, preferred_element_type=jnp.float32)
    return summed.reshape(end_first.shape[:3] + (STATION_COUNT,))


def local_general(visibilities, sky_model, antenna_pairs, tile_counts, usable_mask):
    vis_real, vis_imag = split_parts(visibilities)
    model_real_part, model_imaginary = split_parts(sky_model)
    channel_local = visibilities.shape[1]
    tile_rows = visibilities.shape[2]
    owned_count = STATION_COUNT // lax.axis_size("bl")
    owner_start = lax.axis_index("bl") * owned_count
    live_slots = jnp.arange(tile_rows, dtype=jnp.int32) < tile_counts[0]
    weights = usable_mask.astype(jnp.float32) * live_slots.astype(jnp.float32)[None, :]
    channel_total = channel_local * lax.axis_size("ch")
    poly_rows = lax.dynamic_slice_in_dim(
        jnp.asarray(poly_basis(channel_total)),
        lax.axis_index("ch") * channel_local,
        channel_local,
        1,
    )
    gain_state = jnp.stack(
        [
            jnp.ones((2, channel_local, STATION_COUNT), jnp.float32),
            jnp.zeros((2, channel_local, STATION_COUNT), jnp.float32),
        ]
    )
    solved = gain_state
    for iteration in range(SWEEPS):
        first_gain = jnp.take(gain_state, antenna_pairs[0], axis=3)
        second_gain = jnp.take(gain_state, antenna_pairs[1], axis=3)
        end_first, end_second = contributions(
            model_real_part, model_imaginary, vis_real, vis_imag, first_gain, second_gain, weights
        )
        partial_sums = station_totals(end_first, end_second, antenna_pairs[0], antenna_pairs[1])
        station_sums = lax.psum_scatter(partial_sums, "bl", scatter_dimension=3, tiled=True)
        previous = lax.dynamic_slice_in_dim(gain_state, owner_start, owned_count, 3)
        renewed = refresh(station_sums, previous)
        if iteration == 1:
            renewed = 0.5 * (renewed + previous)
        solved = renewed
        if iteration < SWEEPS - 1:
            gain_state = lax.all_gather(renewed, "bl", axis=3, tiled=True)
    local_moments = jnp.einsum("kc,rfca->krfa", poly_rows, solved, precision=highest)
    moments = lax.psum(local_moments, "ch")
    fitted = jnp.einsum("kc,krfa->rfca", poly_rows, moments, precision=highest)
    return (solved, fitted)


LANES = 128
INDEX_SHIFT = 256.0


def partner_step(slot, column, table):
    even, odd = table
    return even[slot] + (column % 2) * (odd[slot] - even[slot])


def chunk_copies(step, vis_hbm, sky_hbm, mask_hbm, out, sky, mask, sems):
    share, slots = mask.shape
    blocks = slots // LANES
    partner = lax.axis_index("bl") ^ partner_step(step, lax.axis_index("ch"), RAW_STEPS)
    channels = pl.ds(pl.multiple_of(partner * share, share), share)
    copies = [
        pltpu.make_async_copy(mask_hbm.at[channels], mask, sems.at[0]),
        pltpu.make_async_copy(sky_hbm.at[:, channels], sky, sems.at[1]),
    ]
    for block in range(blocks):
        copies.append(
            pltpu.make_async_copy(
                vis_hbm.at[:, channels, pl.ds(block * LANES, LANES)],
                out.at[pl.ds(8 * block, 8)],
                sems.at[2 + block],
            )
        )
    for copy in copies:
        copy.start()
    return copies


def mask_model(out, sky, mask):
    blocks = mask.shape[1] // LANES
    weights = mask[...].astype(jnp.float32).astype(jnp.bfloat16)
    for block in range(blocks):
        lanes = slice(block * LANES, (block + 1) * LANES)
        for plane in range(8):
            out[8 * (blocks + block) + plane] = sky[plane, :, lanes] * weights[:, lanes]


def first_kernel(step, vis_hbm, sky_hbm, mask_hbm, out, sky, mask, sems):
    copies = chunk_copies(step, vis_hbm, sky_hbm, mask_hbm, out, sky, mask, sems)
    for copy in copies[:2]:
        copy.wait()
    mask_model(out, sky, mask)
    for copy in copies[2:]:
        copy.wait()


def pack_kernel(steps, counts_ref, vis_hbm, sky_hbm, mask_hbm, pairs_hbm, *refs):
    outs, ends_out = refs[: len(steps)], refs[len(steps)]
    sky, mask, pairs, rows, pairs_sem, sems = refs[len(steps) + 1 :]
    blocks = pairs.shape[1] // LANES
    pairs_copy = pltpu.make_async_copy(pairs_hbm, pairs, pairs_sem)
    pairs_copy.start()
    copies = [
        chunk_copies(
            step, vis_hbm, sky_hbm, mask_hbm, outs[slot], sky.at[slot], mask.at[slot], sems.at[slot]
        )
        for slot, step in enumerate(steps)
    ]
    pairs_copy.wait()
    lane = lax.broadcasted_iota(jnp.int32, (1, LANES), 1)
    for end in range(2):
        for block in range(blocks):
            row = end * blocks + block
            station = pairs[end : end + 1, block * LANES : (block + 1) * LANES]
            live = lane + block * LANES < counts_ref[0]
            rows[row : row + 1, :] = jnp.where(live, station, STATION_COUNT)
    ends = (rows[...].astype(jnp.float32) - INDEX_SHIFT).astype(jnp.bfloat16)
    ends_out[0] = ends
    for slot in range(len(steps)):
        outs[slot][16 * blocks] = ends
        for copy in copies[slot][:2]:
            copy.wait()
        mask_model(outs[slot], sky.at[slot], mask.at[slot])
    for group in copies:
        for copy in group[2:]:
            copy.wait()


def pieces_of(values):
    high = values.astype(jnp.bfloat16)
    low = (values - high.astype(jnp.float32)).astype(jnp.bfloat16)
    return jnp.concatenate([high, low], axis=0)


def split_dot(values, table):
    rows = values.shape[0]
    both = jnp.dot(pieces_of(values), table, preferred_element_type=jnp.float32)
    return both[:rows] + both[rows:]


def station_sums(first, second, table):
    return split_dot(jnp.concatenate([first, second], axis=1), table)


def read_table(table_ref):
    return jnp.concatenate([table_ref[group] for group in range(table_ref.shape[0])], axis=1)


def shifted_stations(axis):
    station = lax.broadcasted_iota(jnp.int32, (LANES, LANES), axis).astype(jnp.float32)
    return [
        (station + (group * LANES - INDEX_SHIFT)).astype(jnp.bfloat16)
        for group in range(STATION_COUNT // LANES)
    ]


def end_table(ends):
    columns = ends.astype(jnp.float32).T
    one = jnp.ones((), jnp.bfloat16)
    zero = jnp.zeros((), jnp.bfloat16)
    blocks = [[] for _ in range(STATION_COUNT // LANES)]
    for row in range(ends.shape[0]):
        column = jnp.broadcast_to(columns[:, row : row + 1], (LANES, LANES)).astype(jnp.bfloat16)
        for block, station in zip(blocks, shifted_stations(1)):
            block.append(jnp.where(station == column, one, zero))
    return [jnp.concatenate(block, axis=0) for block in blocks]


def look_up_table(ends, table_ref):
    one = jnp.ones((), jnp.bfloat16)
    zero = jnp.zeros((), jnp.bfloat16)
    for row in range(ends.shape[0]):
        for group, station in enumerate(shifted_stations(0)):
            table_ref[row, group * LANES : (group + 1) * LANES, :] = jnp.where(
                station == ends[row : row + 1, :], one, zero
            )


def unit_terms(chunk_ref, products_ref):
    blocks = products_ref.shape[2] // LANES
    plane_of = lambda base, plane: jnp.concatenate(
        [
            chunk_ref[8 * (base * blocks + block) + plane].astype(jnp.float32)
            for block in range(blocks)
        ],
        axis=1,
    )
    real, imag, power = {}, {}, {}
    for p in range(2):
        for q in range(2):
            plane = 2 * p + q
            vis_real = plane_of(0, plane)
            vis_imag = plane_of(0, 4 + plane)
            model_real = plane_of(1, plane)
            model_imag = plane_of(1, 4 + plane)
            real[p, q] = model_real * vis_real + model_imag * vis_imag
            imag[p, q] = model_real * vis_imag - model_imag * vis_real
            power[p, q] = model_real * model_real + model_imag * model_imag
            products_ref[plane] = real[p, q]
            products_ref[4 + plane] = imag[p, q]
            products_ref[8 + plane] = power[p, q]
    first = [real[p, 0] + real[p, 1] for p in range(2)]
    first += [imag[p, 0] + imag[p, 1] for p in range(2)]
    first += [power[p, 0] + power[p, 1] for p in range(2)]
    second = [real[0, q] + real[1, q] for q in range(2)]
    second += [-(imag[0, q] + imag[1, q]) for q in range(2)]
    second += [power[0, q] + power[1, q] for q in range(2)]
    return jnp.concatenate(first, 0), jnp.concatenate(second, 0)


def tile_kernel(chunk_ref, ends_ref, products_ref, table_ref, sums_ref, *look_up_ref):
    ends = ends_ref[ends_ref.shape[0] - 1]
    for group, block in enumerate(end_table(ends)):
        table_ref[group] = block
    sums_ref[...] = station_sums(*unit_terms(chunk_ref, products_ref), read_table(table_ref))
    for ref in look_up_ref:
        look_up_table(ends, ref)


def dot_gains(gains, look_up_ref, share):
    found = split_dot(gains, read_table(look_up_ref))
    slots = found.shape[1] // 2
    return [
        [
            found[part * share : (part + 1) * share, end * slots : (end + 1) * slots]
            for part in range(4)
        ]
        for end in range(2)
    ]


def end_gains(gains, ends_ref, share, blocks):
    ends = (ends_ref[ends_ref.shape[0] - 1].astype(jnp.float32) + INDEX_SHIFT).astype(jnp.int32)
    result = []
    for end in range(2):
        found = {row: [] for row in range(4)}
        for block in range(blocks):
            row = end * blocks + block
            index = jnp.broadcast_to(ends[row : row + 1, :], (share, LANES))
            lane = index % LANES
            group = index // LANES
            for part in range(4):
                rows = gains[part * share : (part + 1) * share]
                value = None
                for source in range(STATION_COUNT // LANES):
                    picked = jnp.take_along_axis(
                        rows[:, source * LANES : (source + 1) * LANES],
                        lane,
                        axis=1,
                        mode="promise_in_bounds",
                    )
                    value = picked if value is None else jnp.where(group == source, picked, value)
                found[part].append(value)
        result.append([jnp.concatenate(found[part], axis=1) for part in range(4)])
    return result


def gain_terms(at, products_ref):
    gain = lambda part, feed, end: at[end][2 * part + feed]
    size = {
        (feed, end): gain(0, feed, end) * gain(0, feed, end)
        + gain(1, feed, end) * gain(1, feed, end)
        for feed in range(2)
        for end in range(2)
    }
    real = lambda p, q: products_ref[2 * p + q]
    imag = lambda p, q: products_ref[4 + 2 * p + q]
    power = lambda p, q: products_ref[8 + 2 * p + q]
    first = [
        sum(gain(0, q, 1) * real(p, q) - gain(1, q, 1) * imag(p, q) for q in range(2))
        for p in range(2)
    ]
    first += [
        sum(gain(0, q, 1) * imag(p, q) + gain(1, q, 1) * real(p, q) for q in range(2))
        for p in range(2)
    ]
    first += [sum(size[q, 1] * power(p, q) for q in range(2)) for p in range(2)]
    second = [
        sum(gain(0, p, 0) * real(p, q) + gain(1, p, 0) * imag(p, q) for p in range(2))
        for q in range(2)
    ]
    second += [
        sum(gain(1, p, 0) * real(p, q) - gain(0, p, 0) * imag(p, q) for p in range(2))
        for q in range(2)
    ]
    second += [sum(size[p, 0] * power(p, q) for p in range(2)) for q in range(2)]
    return jnp.concatenate(first, 0), jnp.concatenate(second, 0)


def solve_kernel(early, late, *refs):
    tiles = early + late
    chunks, refs = refs[:late], refs[late:]
    ends, refs = refs[:tiles], refs[tiles:]
    products, refs = refs[:early], refs[early:]
    tables, refs = refs[:early], refs[early:]
    sums, refs = refs[:early], refs[early:]
    look_up_ref, refs = refs[0], refs[1:]
    outs, refs = refs[:tiles], refs[tiles:]
    late_products, refs = refs[:late], refs[late:]
    (solved_ref,) = refs
    share = products[0].shape[1]
    total = sum(part[...] for part in sums)
    tables = [read_table(table_ref) for table_ref in tables]
    for chunk_ref, ends_ref, products_ref in zip(chunks, ends[early:], late_products):
        tables.append(jnp.concatenate(end_table(ends_ref[ends_ref.shape[0] - 1]), axis=1))
        total = total + station_sums(*unit_terms(chunk_ref, products_ref), tables[-1])
    rows = 2 * share
    divisor = total[2 * rows :] + damping
    gains = jnp.concatenate([(total[:rows] + damping) / divisor, total[rows : 2 * rows] / divisor])
    total = 0.0
    blocks = products[0].shape[2] // LANES
    for tile, products_ref in enumerate(products + late_products):
        if tile < 0:
            at = dot_gains(gains, look_up_ref, share)
        else:
            at = end_gains(gains, ends[tile], share, blocks)
        total = total + station_sums(*gain_terms(at, products_ref), tables[tile])
    divisor = total[2 * rows :] + damping
    renewed = (total[: 2 * rows] + damping * gains) / jnp.concatenate([divisor, divisor])
    solved_ref[...] = 0.5 * (renewed + gains)
    owned = STATION_COUNT // tiles
    here = lax.axis_index("bl")
    for step in range(tiles):
        start = pl.multiple_of((here ^ partner_step(step, lax.axis_index("ch"), BACK_STEPS)) * owned, owned)
        outs[step][...] = solved_ref[:, pl.ds(start, owned)]


def moment_kernel(basis_ref, *refs):
    pieces, moments_ref = refs[:-1], refs[-1]
    share = pieces[0].shape[0] // 4
    here = lax.axis_index("bl")
    columns = []
    for step in range(len(pieces)):
        start = pl.multiple_of((here ^ partner_step(step, lax.axis_index("ch"), BACK_STEPS)) * share, share)
        columns.append(basis_ref[pl.ds(start, share), :])
    for degree in range(4):
        for part in range(4):
            terms = sum(
                piece[part * share : (part + 1) * share, :] * column[:, degree : degree + 1]
                for piece, column in zip(pieces, columns)
            )
            row = 4 * degree + part
            moments_ref[row : row + 1, :] = jnp.sum(terms, axis=0, keepdims=True)


def order_kernel(*refs):
    pieces, solved_ref = refs[:-1], refs[-1]
    share = pieces[0].shape[0] // 4
    here = lax.axis_index("bl")
    for step, piece in enumerate(pieces):
        start = pl.multiple_of((here ^ partner_step(step, lax.axis_index("ch"), BACK_STEPS)) * share, share)
        for part in range(4):
            solved_ref[part, pl.ds(start, share), :] = piece[part * share : (part + 1) * share, :]


def vmem_call(kernel, outs, scratch=(), spaces=None, **options):
    def call(*args):
        return pl.pallas_call(
            kernel,
            out_shape=outs,
            in_specs=[
                pl.BlockSpec(memory_space=space) for space in spaces or [pltpu.VMEM] * len(args)
            ],
            out_specs=jax.tree.map(lambda _: pl.BlockSpec(memory_space=pltpu.VMEM), outs),
            scratch_shapes=list(scratch),
            compiler_params=pltpu.CompilerParams(vmem_limit_bytes=24 << 20),
            **options,
        )(*args)

    return call


def in_hbm(value):
    return pltpu.with_memory_space_constraint(value, pltpu.HBM)


def mesh_partners(tiles, groups, step, table):
    return [
        (row * groups + column, (row ^ partner_step(step, column, table)) * groups + column)
        for row in range(tiles)
        for column in range(groups)
    ]


def partners(count, step):
    return [(index, index ^ step) for index in range(count)]


def local_resplit(visibilities, sky_model, antenna_pairs, tile_counts, usable_mask):
    channel_local = visibilities.shape[1]
    slots = visibilities.shape[2]
    tiles = lax.axis_size("bl")
    groups = lax.axis_size("ch")
    share = channel_local // tiles
    owned = STATION_COUNT // tiles
    f32 = jnp.float32
    shape = jax.ShapeDtypeStruct

    steps = list(range(1, tiles))
    first = FIRST
    others = [step for step in steps if step != first] + [0]
    blocks = slots // LANES
    bf16 = jnp.bfloat16
    (lead,) = vmem_call(
        functools.partial(first_kernel, first),
        (shape((16 * blocks, share, LANES), bf16),),
        scratch=[
            pltpu.VMEM((8, share, slots), bf16),
            pltpu.VMEM((share, slots), jnp.int32),
            pltpu.SemaphoreType.DMA((2 + blocks,)),
        ],
        spaces=[pltpu.HBM] * 3,
    )(in_hbm(visibilities), in_hbm(sky_model), in_hbm(usable_mask))
    tile_counts, lead = lax.optimization_barrier((tile_counts, lead))
    *packed, own_ends = vmem_call(
        functools.partial(pack_kernel, others),
        (shape((16 * blocks + 1, share, LANES), bf16),) * len(others)
        + (shape((1, 2 * blocks, LANES), bf16),),
        scratch=[
            pltpu.VMEM((len(others), 8, share, slots), bf16),
            pltpu.VMEM((len(others), share, slots), jnp.int32),
            pltpu.VMEM((2, slots), jnp.int32),
            pltpu.VMEM((2 * blocks, LANES), jnp.int32),
            pltpu.SemaphoreType.DMA,
            pltpu.SemaphoreType.DMA((len(others), 2 + blocks)),
        ],
        spaces=[pltpu.SMEM] + [pltpu.HBM] * 4,
    )(
        tile_counts,
        in_hbm(visibilities),
        in_hbm(sky_model),
        in_hbm(usable_mask),
        in_hbm(antenna_pairs),
    )

    def exchange(piece, step):
        return lax.ppermute(piece, ("bl", "ch"), mesh_partners(tiles, groups, step, RAW_STEPS))

    chunks = {0: packed[-1], first: exchange(lead, first)}
    for piece, step in zip(packed[:-1], others):
        chunks[step] = exchange(piece, step)
    ends = dict(chunks)
    ends[first] = exchange(own_ends, first)

    products_shape = shape((12, share, slots), f32)
    table_dims = (STATION_COUNT // LANES, 2 * slots, LANES)
    table_shape = shape(table_dims, bf16)
    sums_shape = shape((6 * share, STATION_COUNT), f32)
    look_up_shape = shape((2 * blocks, STATION_COUNT, LANES), bf16)
    tile_outs = (products_shape, table_shape, sums_shape)
    late = [steps[-1]]
    done = {
        step: vmem_call(tile_kernel, tile_outs + ((look_up_shape,) if step == 0 else ()))(
            chunks[step], ends[step]
        )
        for step in range(tiles)
        if step not in late
    }
    pieces = vmem_call(
        functools.partial(solve_kernel, len(done), len(late)),
        tuple(shape((4 * share, owned), f32) for _ in range(tiles)),
        scratch=[
            *[pltpu.VMEM((12, share, slots), f32) for _ in late],
            pltpu.VMEM((4 * share, STATION_COUNT), f32),
        ],
    )(
        *[chunks[step] for step in late],
        *[ends[step] for step in list(done) + late],
        *[parts[0] for parts in done.values()],
        *[parts[1] for parts in done.values()],
        *[parts[2] for parts in done.values()],
        done[0][3],
    )
    received = {0: pieces[0]}
    for step in steps:
        received[step] = lax.ppermute(
            pieces[step], ("bl", "ch"), mesh_partners(tiles, groups, step, BACK_STEPS)
        )
    received = [received[step] for step in range(tiles)]
    basis = lax.dynamic_slice_in_dim(
        jnp.asarray(poly_basis(channel_local * groups).T),
        lax.axis_index("ch") * channel_local,
        channel_local,
        0,
    )
    moments = vmem_call(moment_kernel, shape((16, owned), f32))(basis, *received)
    solved = vmem_call(order_kernel, shape((4, channel_local, owned), f32))(*received)
    moment_parts = [moments]
    for step in range(1, groups):
        moment_parts.append(lax.ppermute(moments, "ch", partners(groups, step)))
    total = sum(moment_parts).reshape(4, 4, owned)
    fitted = sum(basis[None, :, k, None] * total[k][:, None, :] for k in range(4))
    out_shape = (2, 2, channel_local, owned)
    return solved.reshape(out_shape), fitted.reshape(out_shape)


FIRST = 2
RAW_STEPS = ((0, 1, 2, 3), (0, 1, 3, 2))
BACK_STEPS = ((0, 1, 2, 3), (0, 2, 1, 3))


def local(visibilities, sky_model, antenna_pairs, tile_counts, usable_mask):
    tiles = lax.axis_size("bl")
    groups = lax.axis_size("ch")
    resplit = (
        tiles == 4
        and groups == 4
        and visibilities.shape[1] == 8 * tiles
        and STATION_COUNT % (128 * tiles) == 0
        and STATION_COUNT <= 2 * INDEX_SHIFT
        and visibilities.shape[2] == 4 * LANES
    )
    body = local_resplit if resplit else local_general
    return body(visibilities, sky_model, antenna_pairs, tile_counts, usable_mask)


def solution(mesh):
    return jax.shard_map(
        local,
        mesh=mesh,
        in_specs=(
            P(None, "ch", ("grp", "bl")),
            P(None, "ch", ("grp", "bl")),
            P(None, ("grp", "bl")),
            P(("grp", "bl")),
            P("ch", ("grp", "bl")),
        ),
        out_specs=(P(None, None, "ch", ("grp", "bl")), P(None, None, "ch", ("grp", "bl"))),
        check_vma=False,
    )
```
